32 devices in a mesh: epi: 2 (over y), space: 4 (over z), draw: 4 (over x, core).
Axes of the slice: x: 2, y: 2, z: 4, core: 2. Of those that a mesh axis runs over, the one named last changes fastest.
Arguments:
- log_perm: float32 [64, 64, 384], P(('epi', 'space')), parts along dimension 0, may hold values from -4 to 4
- noise: float32 [4, 64, 64, 384], P('draw', ('epi', 'space')), parts along dimension 1, may hold values from -3.5 to 3.5
- source: float32 [64, 64, 384], P(('epi', 'space')), parts along dimension 0, may hold values from -24 to 24
- start_pressure: float32 [64, 64, 384], P(('epi', 'space')), parts along dimension 0, may hold values from -18 to 18
- observe: float32 [64, 64, 384], P(('epi', 'space')), parts along dimension 0, may hold values from -12 to 12
Outputs:
- pressure: float32 [4, 64, 64, 384], P('draw', ('epi', 'space')), parts along dimension 1
- log_perm_grad: float32 [64, 64, 384], P(('epi', 'space'), 'draw'), parts along dimension 0
The draws below stay inside these ranges and needn't reach their ends.
There are 2 independent parts, one for each index of `epi`. The reference program is written for one: setup_inputs(seed, part) draws one part's arguments, and reference() takes and returns one part's arrays. A program takes and returns all parts, laid end to end along the dimension named above; each array names one. Nothing has to cross between parts.
All inputs are finite; a program needn't handle non-finite values.
Results may differ from the reference program's by a relative error of at most 0.00002.
Values sent between devices are 32-bit elements; how exact they have to be, the bound alone decides.
No kernel may reach another device: no remote copies, remote signals or barrier semaphores. Data moves between devices by JAX's collectives and lax.ppermute only.
A program may use at most 64 MiB of HBM per device.

```python
import jax
import jax.numpy as jnp
from jax import lax

NX = 64
NY = 384
SWEEPS = 3
NZ = 32
DRAWS = 4


def block_levels(stream_key, shape, pieces, low, largest):
    def one(dim, blocks):
        heights = jax.random.uniform(jax.random.fold_in(jax.random.fold_in(stream_key, 6), dim), (blocks,), jnp.float32, low / len(pieces), largest / len(pieces))
        return jnp.repeat(jnp.exp(heights), shape[dim] // blocks).reshape((-1,) + (1,) * (len(shape) - dim - 1))

    loudness = one(*pieces[0])
    for cut in pieces[1:]:
        loudness = loudness * one(*cut)
    return loudness


def scatter_about(rng, shape, spread, bound, split=(), held_as=jnp.bfloat16):
    result = jax.random.normal(rng, shape, jnp.float32) * spread
    if len(split) > 0:
        result = block_levels(rng, shape, split, -0.22, 0.18) * result
    return jnp.clip(result, min=-bound, max=bound).astype(held_as)


def setup_inputs(seed: int = 0, part: int = 0) -> dict:
    arg_keys = jax.random.split(jax.random.key(seed), 6)
    own_keys = jax.random.split(jax.random.fold_in(arg_keys[5], part), 6)
    log_perm = scatter_about(own_keys[0], (NZ, NX, NY), 1.0, 4.0, ((0, 4),), jnp.float32)
    noise = scatter_about(own_keys[1], (DRAWS, NZ, NX, NY), 0.7, 3.5, ((0, 4), (1, 4)), jnp.float32)
    source = scatter_about(own_keys[2], (NZ, NX, NY), 4.0, 24.0, ((0, 4),), jnp.float32)
    start_pressure = scatter_about(own_keys[3], (NZ, NX, NY), 3.0, 18.0, ((0, 4),), jnp.float32)
    observe = scatter_about(own_keys[4], (NZ, NX, NY), 2.0, 12.0, ((0, 4),), jnp.float32)
    return dict(log_perm=log_perm, noise=noise, source=source, start_pressure=start_pressure, observe=observe)


def face_weights(padded_k):
    face_z = 0.5 * (padded_k[..., :-1, 1:-1, 1:-1] + padded_k[..., 1:, 1:-1, 1:-1])
    face_x = 0.5 * (padded_k[..., 1:-1, :-1, 1:-1] + padded_k[..., 1:-1, 1:, 1:-1])
    face_y = 0.5 * (padded_k[..., 1:-1, 1:-1, :-1] + padded_k[..., 1:-1, 1:-1, 1:])
    diag = 0.5 + face_z[..., :-1, :, :] + face_z[..., 1:, :, :] + face_x[..., :, :-1, :] + face_x[..., :, 1:, :] + face_y[..., :-1] + face_y[..., 1:]
    return (face_z, face_x, face_y), diag


def apply_faces(weights, padded_v):
    face_z, face_x, face_y = weights
    total = face_z[..., :-1, :, :] * padded_v[..., :-2, 1:-1, 1:-1] + face_z[..., 1:, :, :] * padded_v[..., 2:, 1:-1, 1:-1]
    total = total + face_x[..., :, :-1, :] * padded_v[..., 1:-1, :-2, 1:-1] + face_x[..., :, 1:, :] * padded_v[..., 1:-1, 2:, 1:-1]
    total = total + face_y[..., :-1] * padded_v[..., 1:-1, 1:-1, :-2] + face_y[..., 1:] * padded_v[..., 1:-1, 1:-1, 2:]
    return total


def face_terms(padded_u, padded_q, padded_e):
    grad_z = padded_u[..., :-1, 1:-1, 1:-1] * padded_q[..., 1:, 1:-1, 1:-1] + padded_u[..., 1:, 1:-1, 1:-1] * padded_q[..., :-1, 1:-1, 1:-1] + padded_e[..., :-1, 1:-1, 1:-1] + padded_e[..., 1:, 1:-1, 1:-1]
    grad_x = padded_u[..., 1:-1, :-1, 1:-1] * padded_q[..., 1:-1, 1:, 1:-1] + padded_u[..., 1:-1, 1:, 1:-1] * padded_q[..., 1:-1, :-1, 1:-1] + padded_e[..., 1:-1, :-1, 1:-1] + padded_e[..., 1:-1, 1:, 1:-1]
    grad_y = padded_u[..., 1:-1, 1:-1, :-1] * padded_q[..., 1:-1, 1:-1, 1:] + padded_u[..., 1:-1, 1:-1, 1:] * padded_q[..., 1:-1, 1:-1, :-1] + padded_e[..., 1:-1, 1:-1, :-1] + padded_e[..., 1:-1, 1:-1, 1:]
    return 0.5 * (grad_z[..., :-1, :, :] + grad_z[..., 1:, :, :] + grad_x[..., :, :-1, :] + grad_x[..., :, 1:, :] + grad_y[..., :-1] + grad_y[..., 1:])


def reference(log_perm, noise, source, start_pressure, observe):
    def one_draw(noise_one):
        conduct = jnp.exp(log_perm + noise_one)
        weights, diag = face_weights(jnp.pad(conduct, 1))
        rims = []
        current = start_pressure
        for step in range(SWEEPS):
            padded = jnp.pad(current, 1)
            rims.append(padded)
            current = (source + apply_faces(weights, padded)) / diag
        rims.append(jnp.pad(current, 1))
        adjoint = observe
        grad = jnp.zeros(observe.shape, jnp.float32)
        for step in reversed(range(SWEEPS)):
            mult = adjoint / diag
            later = rims[step + 1][1:-1, 1:-1, 1:-1]
            term = -mult * later
            padded_u = jnp.pad(mult, 1)
            grad = grad + face_terms(padded_u, rims[step], jnp.pad(term, 1))
            adjoint = apply_faces(weights, padded_u)
        return current, conduct * grad

    pressures, grads = lax.map(one_draw, noise)
    return pressures, jnp.sum(grads, axis=0)
```

```python
import functools

import jax
import jax.numpy as jnp
from jax import lax
from jax.experimental import pallas as pl
from jax.experimental.pallas import tpu as pltpu
from jax.sharding import PartitionSpec as P

SWEEPS = 3
HALO = SWEEPS + 1
LANES = 128
SUB = 8


def neighbours(ref, zz, r, rows):
    tiles = ref.shape[1]
    lane = lax.broadcasted_iota(jnp.int32, (SUB, LANES), 1)
    sub = lax.broadcasted_iota(jnp.int32, (SUB, LANES), 0)
    zero = jnp.zeros((SUB, LANES), jnp.float32)
    here = pl.ds(SUB * r, SUB)
    own = [ref[zz, c, here, :] for c in range(tiles)]
    fwd = [pltpu.roll(v, 1, 1) for v in own]
    bwd = [pltpu.roll(v, LANES - 1, 1) for v in own]
    out = []
    for c in range(tiles):
        left = jnp.where(lane == 0, fwd[c - 1] if c > 0 else zero, fwd[c])
        right = jnp.where(lane == LANES - 1, bwd[c + 1] if c + 1 < tiles else zero, bwd[c])
        if r > 0:
            north = ref[zz, c, pl.ds(SUB * r - 1, SUB), :]
        else:
            north = jnp.where(sub == 0, zero, pltpu.roll(own[c], 1, 0))
        if r + 1 < rows:
            south = ref[zz, c, pl.ds(SUB * r + 1, SUB), :]
        else:
            south = jnp.where(sub == SUB - 1, zero, pltpu.roll(own[c], SUB - 1, 0))
        out.append((left, right, north, south, ref[zz - 1, c, here, :], ref[zz + 1, c, here, :]))
    return own, out


def six(parts):
    a, b, c, d, e, f = parts
    return ((a + b) + (c + d)) + (e + f)


def kernel(
    k_in, klo_in, khi_in, p0_in, src_in, obs_in, alo_in, ahi_in, blo_in, bhi_in,
    press_out, keep_out, send_out,
    K, P0, P1, P2, P3, U1, U2, U3, X, Y, X2, Y2, E, G, NP0, RINV, SRC, OBS, sems,
):
    slab = p0_in.shape[0]
    nx = p0_in.shape[1]
    half = nx // 2
    rows, tiles = nx // SUB, p0_in.shape[2] // LANES
    top = HALO + slab
    depth = top + HALO
    draw, draws = lax.axis_index("draw"), lax.axis_size("draw")
    space, spaces = lax.axis_index("space"), lax.axis_size("space")
    par, group = draw % 2, draw // 2
    groups = draws // 2
    block = nx // draws

    copies = []

    def copy(src, dst):
        cp = pltpu.make_async_copy(src, dst, sems.at[len(copies)])
        cp.start()
        copies.append(cp)

    mine = pl.ds(pl.multiple_of(half * par, half), half)
    other = pl.ds(pl.multiple_of(half * (1 - par), half), half)
    for c in range(tiles):
        cols = pl.ds(c * LANES, LANES)
        copy(k_in.at[:, :, cols], K.at[pl.ds(HALO, slab), c])
        copy(klo_in.at[:, :, cols], K.at[pl.ds(0, HALO), c])
        copy(khi_in.at[:, :, cols], K.at[pl.ds(top, HALO), c])
        copy(p0_in.at[:, :, cols], P0.at[pl.ds(HALO, slab), c])
        for lo, hi, at in ((alo_in, ahi_in, mine), (blo_in, bhi_in, other)):
            copy(lo.at[pl.ds(0, HALO), :, cols], P0.at[pl.ds(0, HALO), c, at])
            copy(hi.at[pl.ds(0, HALO), :, cols], P0.at[pl.ds(top, HALO), c, at])
    copy(src_in, SRC.at[pl.ds(HALO, slab)])
    copy(obs_in, OBS.at[pl.ds(HALO, slab)])
    for lo, hi, at in ((alo_in, ahi_in, mine), (blo_in, bhi_in, other)):
        copy(lo.at[pl.ds(HALO, SWEEPS)], SRC.at[pl.ds(1, SWEEPS), at])
        copy(lo.at[pl.ds(HALO + SWEEPS, SWEEPS)], OBS.at[pl.ds(1, SWEEPS), at])
        copy(hi.at[pl.ds(HALO, SWEEPS)], SRC.at[pl.ds(top, SWEEPS), at])
        copy(hi.at[pl.ds(HALO + SWEEPS, SWEEPS)], OBS.at[pl.ds(top, SWEEPS), at])
    for cp in copies:
        cp.wait()

    low_in = jnp.where(space > 0, 1.0, 0.0).astype(jnp.float32)
    high_in = jnp.where(space + 1 < spaces, 1.0, 0.0).astype(jnp.float32)

    def at(r):
        return pl.ds(SUB * r, SUB)

    def cl(c):
        return pl.ds(c * LANES, LANES)

    def stage1(zz, _):
        inside = jnp.where(zz < HALO, low_in, jnp.where(zz >= top, high_in, jnp.float32(1.0)))
        for r in range(rows):
            k, kn = neighbours(K, zz, r, rows)
            p, pn = neighbours(P0, zz, r, rows)
            for c in range(tiles):
                rinv = inside / (0.5 + 0.5 * (6.0 * k[c] + six(kn[c])))
                flow = six([(k[c] + a) * b for a, b in zip(kn[c], pn[c])])
                p1 = (SRC[zz, at(r), cl(c)] + 0.5 * flow) * rinv
                u3 = OBS[zz, at(r), cl(c)] * rinv
                RINV[zz, c, at(r), :] = rinv
                NP0[zz, c, at(r), :] = six(pn[c])
                P1[zz, c, at(r), :] = p1
                U3[zz, c, at(r), :] = u3
                X[zz, c, at(r), :] = k[c] * p1
                Y[zz, c, at(r), :] = k[c] * u3
        return 0

    lax.fori_loop(1, depth - 1, stage1, 0)

    def stage2(zz, _):
        for r in range(rows):
            _, a = neighbours(P1, zz, r, rows)
            _, b = neighbours(X, zz, r, rows)
            _, v = neighbours(U3, zz, r, rows)
            _, w = neighbours(Y, zz, r, rows)
            for c in range(tiles):
                k, rinv = K[zz, c, at(r), :], RINV[zz, c, at(r), :]
                np1, nu3 = six(a[c]), six(v[c])
                p2 = (SRC[zz, at(r), cl(c)] + 0.5 * (k * np1 + six(b[c]))) * rinv
                u2 = (0.5 * (k * nu3 + six(w[c]))) * rinv
                P2[zz, c, at(r), :] = p2
                U2[zz, c, at(r), :] = u2
                X2[zz, c, at(r), :] = k * p2
                Y2[zz, c, at(r), :] = k * u2
                G[zz, c, at(r), :] = u2 * np1 + p2 * nu3
        return 0

    lax.fori_loop(2, depth - 2, stage2, 0)

    def stage3(zz, _):
        for r in range(rows):
            p2, a = neighbours(P2, zz, r, rows)
            _, b = neighbours(X2, zz, r, rows)
            u2, v = neighbours(U2, zz, r, rows)
            _, w = neighbours(Y2, zz, r, rows)
            for c in range(tiles):
                k, rinv = K[zz, c, at(r), :], RINV[zz, c, at(r), :]
                p1, u3 = P1[zz, c, at(r), :], U3[zz, c, at(r), :]
                np2, nu2 = six(a[c]), six(v[c])
                p3 = (SRC[zz, at(r), cl(c)] + 0.5 * (k * np2 + six(b[c]))) * rinv
                u1 = (0.5 * (k * nu2 + six(w[c]))) * rinv
                e = -(u1 * p1 + u2[c] * p2[c] + u3 * p3)
                g = G[zz, c, at(r), :] + u3 * np2 + p1 * nu2 + u1 * NP0[zz, c, at(r), :]
                P3[zz, at(r), cl(c)] = p3
                U1[zz, c, at(r), :] = u1
                E[zz, c, at(r), :] = e
                G[zz, c, at(r), :] = g + 6.0 * e
        return 0

    lax.fori_loop(3, depth - 3, stage3, 0)
    out = pltpu.make_async_copy(P3.at[pl.ds(HALO, slab)], press_out, sems.at[0])
    out.start()

    def gradient(zz, r):
        _, v = neighbours(U1, zz, r, rows)
        _, w = neighbours(E, zz, r, rows)
        return [
            0.5 * K[zz, c, at(r), :] * (G[zz, c, at(r), :] + P0[zz, c, at(r), :] * six(v[c]) + six(w[c]))
            for c in range(tiles)
        ]

    def stage4(z, _):
        zz = z + HALO
        for h in range(groups):
            slot = (h - group + groups) % groups
            for q in range(block // SUB):
                even = gradient(zz, (2 * h * block) // SUB + q)
                odd = gradient(zz, ((2 * h + 1) * block) // SUB + q)
                for c in range(tiles):
                    keep_out[slot, z, pl.ds(SUB * q, SUB), cl(c)] = jnp.where(par == 0, even[c], odd[c])
                    send_out[slot, z, pl.ds(SUB * q, SUB), cl(c)] = jnp.where(par == 0, odd[c], even[c])
        return 0

    lax.fori_loop(0, slab, stage4, 0)
    out.wait()


def solve(k, klo, khi, p0, src, obs, alo, ahi, blo, bhi, draws):
    slab, nx, ny = p0.shape
    tiles = ny // LANES
    depth = slab + 2 * HALO
    field = pltpu.VMEM((depth, tiles, nx, LANES), jnp.float32)
    plain = pltpu.VMEM((depth, nx, ny), jnp.float32)
    part = jax.ShapeDtypeStruct((draws // 2, slab, nx // draws, ny), jnp.float32)
    anywhere = pl.BlockSpec(memory_space=pl.ANY)
    whole = pl.BlockSpec(memory_space=pltpu.VMEM)
    return pl.pallas_call(
        kernel,
        out_shape=(jax.ShapeDtypeStruct((slab, nx, ny), jnp.float32), part, part),
        in_specs=[anywhere] * 10,
        out_specs=(anywhere, whole, whole),
        scratch_shapes=[
            field, field, field, field, plain, field, field, field, field, field, field, field, field, field, field,
            field, plain, plain, pltpu.SemaphoreType.DMA((8 * tiles + 10,)),
        ],
        compiler_params=pltpu.CompilerParams(vmem_limit_bytes=56 * 2**20),
        cost_estimate=pl.CostEstimate(flops=200 * depth * nx * ny, bytes_accessed=40 * slab * nx * ny, transcendentals=0),
    )(k, klo, khi, p0, src, obs, alo, ahi, blo, bhi)


def local(log_perm, noise, source, start_pressure, observe):
    draws, spaces = lax.axis_size("draw"), lax.axis_size("space")
    draw = lax.axis_index("draw")
    nx = log_perm.shape[1]
    half = nx // 2
    up = [(i, i + 1) for i in range(spaces - 1)]
    down = [(j, i) for i, j in up]
    pair = [(i, i ^ 1) for i in range(draws)]

    def edge(start):
        pick = (lambda a, w: a[a.shape[0] - w :]) if start is None else (lambda a, w: a[:w])
        joined = [pick(start_pressure, HALO), pick(source, SWEEPS), pick(observe, SWEEPS)]
        cut = [lax.dynamic_slice_in_dim(a, (draw % 2) * half, half, axis=1) for a in joined]
        return jnp.concatenate(cut, axis=0)

    alo = lax.ppermute(edge(None), "space", up)
    ahi = lax.ppermute(edge(0), "space", down)
    k = jnp.exp(log_perm + noise[0])
    klo = lax.ppermute(k[k.shape[0] - HALO :], "space", up)
    khi = lax.ppermute(k[:HALO], "space", down)
    blo = lax.ppermute(alo, "draw", pair)
    bhi = lax.ppermute(ahi, "draw", pair)
    press, keep, send = solve(k, klo, khi, start_pressure, source, observe, alo, ahi, blo, bhi, draws)
    both = keep + lax.ppermute(send, "draw", pair)
    total = both[0]
    for s in range(1, draws // 2):
        total = total + lax.ppermute(both[s], "draw", [(j, (j + 2 * s) % draws) for j in range(draws)])
    return press[None], total


def solution(mesh):
    return jax.shard_map(
        local,
        mesh=mesh,
        in_specs=(
            P(("epi", "space"), None, None),
            P("draw", ("epi", "space"), None, None),
            P(("epi", "space"), None, None),
            P(("epi", "space"), None, None),
            P(("epi", "space"), None, None),
        ),
        out_specs=(P("draw", ("epi", "space"), None, None), P(("epi", "space"), "draw", None)),
        check_vma=False,
    )
```

```python
import jax
import jax.numpy as jnp
from jax import lax
from jax.experimental import pallas as pl
from jax.experimental.pallas import tpu as pltpu
from jax.sharding import PartitionSpec as P

SWEEPS = 3
HALO = SWEEPS + 1
EDGE = HALO + 2 * SWEEPS
LANES = 128
SUB = 8
ANYWHERE = pl.BlockSpec(memory_space=pl.ANY)
OFFCHIP = pl.BlockSpec(memory_space=pltpu.HBM)
ONCHIP = pl.BlockSpec(memory_space=pltpu.VMEM)


def around(ref, zz, r, rows):
    tiles = ref.shape[1]
    lane = lax.broadcasted_iota(jnp.int32, (SUB, LANES), 1)
    sub = lax.broadcasted_iota(jnp.int32, (SUB, LANES), 0)
    zero = jnp.zeros((SUB, LANES), jnp.float32)
    here = pl.ds(SUB * r, SUB)
    own = [ref[zz, c, here, :] for c in range(tiles)]
    fwd = [pltpu.roll(v, 1, 1) for v in own]
    bwd = [pltpu.roll(v, LANES - 1, 1) for v in own]
    out = []
    for c in range(tiles):
        left = jnp.where(lane == 0, fwd[c - 1] if c > 0 else zero, fwd[c])
        right = jnp.where(lane == LANES - 1, bwd[c + 1] if c + 1 < tiles else zero, bwd[c])
        out.append((left, right) + cross(ref, zz, c, r, rows, own[c], sub, zero))
    return own, out


def cross(ref, zz, c, r, rows, own, sub, zero):
    if r > 0:
        north = ref[zz, c, pl.ds(SUB * r - 1, SUB), :]
    else:
        north = jnp.where(sub == 0, zero, pltpu.roll(own, 1, 0))
    if r + 1 < rows:
        south = ref[zz, c, pl.ds(SUB * r + 1, SUB), :]
    else:
        south = jnp.where(sub == SUB - 1, zero, pltpu.roll(own, SUB - 1, 0))
    here = pl.ds(SUB * r, SUB)
    return north, south, ref[zz - 1, c, here, :], ref[zz + 1, c, here, :]


def faces(K, WL, WR, zz, c, r, rows):
    sub = lax.broadcasted_iota(jnp.int32, (SUB, LANES), 0)
    zero = jnp.zeros((SUB, LANES), jnp.float32)
    here = pl.ds(SUB * r, SUB)
    k = K[zz, c, here, :]
    rest = [k + v for v in cross(K, zz, c, r, rows, k, sub, zero)]
    return (WL[zz, c, here, :], WR[zz, c, here, :], *rest)


def six(parts):
    a, b, c, d, e, f = parts
    return ((a + b) + (c + d)) + (e + f)


def weighted(weights, parts):
    return six([w * v for w, v in zip(weights, parts)])


def sweeps(refs, ranges, inside, press):
    K, P0, SRC, OBS, P1, P2, U1, U2, U3, HR, SR, NP0, WL, WR, G, E = refs
    tiles, rows = K.shape[1], K.shape[2] // SUB

    def at(r):
        return pl.ds(SUB * r, SUB)

    def first(zz):
        valid = inside(zz)
        for r in range(rows):
            k, kn = around(K, zz, r, rows)
            _, pn = around(P0, zz, r, rows)
            for c in range(tiles):
                w = [k[c] + v for v in kn[c]]
                rinv = valid / (0.5 + 0.5 * six(w))
                hr = 0.5 * rinv
                sr = SRC[zz, c, at(r), :] * rinv
                HR[zz, c, at(r), :] = hr
                SR[zz, c, at(r), :] = sr
                WL[zz, c, at(r), :] = w[0]
                WR[zz, c, at(r), :] = w[1]
                NP0[zz, c, at(r), :] = six(pn[c])
                P1[zz, c, at(r), :] = sr + weighted(w, pn[c]) * hr
                U3[zz, c, at(r), :] = OBS[zz, c, at(r), :] * rinv

    def second(zz):
        for r in range(rows):
            _, a = around(P1, zz, r, rows)
            _, v = around(U3, zz, r, rows)
            for c in range(tiles):
                w = faces(K, WL, WR, zz, c, r, rows)
                hr = HR[zz, c, at(r), :]
                p2 = SR[zz, c, at(r), :] + weighted(w, a[c]) * hr
                u2 = weighted(w, v[c]) * hr
                P2[zz, c, at(r), :] = p2
                U2[zz, c, at(r), :] = u2
                G[zz, c, at(r), :] = u2 * six(a[c]) + p2 * six(v[c])

    def third(zz, own):
        for r in range(rows):
            p2, a = around(P2, zz, r, rows)
            u2, v = around(U2, zz, r, rows)
            for c in range(tiles):
                w = faces(K, WL, WR, zz, c, r, rows)
                hr = HR[zz, c, at(r), :]
                p1, u3 = P1[zz, c, at(r), :], U3[zz, c, at(r), :]
                p3 = SR[zz, c, at(r), :] + weighted(w, a[c]) * hr
                u1 = weighted(w, v[c]) * hr
                e = -(u1 * p1 + u2[c] * p2[c] + u3 * p3)
                U1[zz, c, at(r), :] = u1
                E[zz, c, at(r), :] = e
                if own:
                    g = u3 * six(a[c]) + p1 * six(v[c]) + u1 * NP0[zz, c, at(r), :]
                    press(zz)[at(r), pl.ds(c * LANES, LANES)] = p3
                    G[zz, c, at(r), :] = (G[zz, c, at(r), :] + 6.0 * e) + g

    for body, spans in zip((first, second, third), ranges):
        for span in spans:
            lo, hi, *own = span
            lax.fori_loop(lo, hi, lambda zz, _, body=body, own=own: body(zz, *own) or 0, 0)


def edges_kernel(p0, src, obs, up, down, sems):
    nx, ny = p0.shape[1:]
    slab, half = p0.shape[0], nx // 2
    rows = pl.ds(pl.multiple_of(half * (lax.axis_index("draw") % 2), half), half)
    copies = []
    for c in range(ny // LANES):
        cols = pl.ds(c * LANES, LANES)
        at = 0
        for ref, width in ((p0, HALO), (src, SWEEPS), (obs, SWEEPS)):
            for start, out in ((slab - width, up), (0, down)):
                copies.append(
                    pltpu.make_async_copy(
                        ref.at[pl.ds(start, width), rows, cols], out.at[pl.ds(at, width), c], sems.at[len(copies)]
                    )
                )
            at += width
    for cp in copies:
        cp.start()
    for cp in copies:
        cp.wait()


def conduct_kernel(log_perm, noise, K, top, bottom):
    slab, nx, ny = log_perm.shape

    def plane(z, _):
        for r in range(nx // SUB):
            for c in range(ny // LANES):
                here, cols = pl.ds(SUB * r, SUB), pl.ds(c * LANES, LANES)
                K[z + HALO, c, here, :] = jnp.exp(log_perm[z, here, cols] + noise[z, here, cols])
        return 0

    lax.fori_loop(0, slab, plane, 0)

    def edge(z, _):
        top[z] = K[slab + z]
        bottom[z] = K[HALO + z]
        return 0

    lax.fori_loop(0, HALO, edge, 0)


def inner_kernel(K, p0, src, obs, P0, SRC, OBS, P1, P2, U1, U2, U3, HR, SR, NP0, WL, WR, G, E, mid, sems):
    slab = p0.shape[0]
    top = HALO + slab
    copies = []
    for c in range(K.shape[1]):
        for ref, out in ((p0, P0), (src, SRC), (obs, OBS)):
            copies.append(
                pltpu.make_async_copy(
                    ref.at[:, :, pl.ds(c * LANES, LANES)], out.at[pl.ds(HALO, slab), c], sems.at[len(copies)]
                )
            )
    for cp in copies:
        cp.start()
    for cp in copies:
        cp.wait()
    refs = (K, P0, SRC, OBS, P1, P2, U1, U2, U3, HR, SR, NP0, WL, WR, G, E)
    ranges = [[(HALO + n, top - n)] for n in (1, 2)] + [[(HALO + 3, top - 3, True)]]
    sweeps(refs, ranges, lambda zz: jnp.float32(1.0), lambda zz: mid.at[zz - HALO - SWEEPS])


def outer_kernel(*args):
    klo, khi, alo, ahi, blo, bhi, mid = args[:7]
    refs, (press_out, keep_out, send_out, press, sems) = args[-21:-5], args[-5:]
    K, P0, SRC, OBS, P1, P2, U1, U2, U3, HR, SR, NP0, WL, WR, G, E = refs
    slab, nx = press.shape[:2]
    half, top, depth = nx // 2, HALO + slab, slab + 2 * HALO
    tiles, rows = K.shape[1], nx // SUB
    draw, draws = lax.axis_index("draw"), lax.axis_size("draw")
    space, spaces = lax.axis_index("space"), lax.axis_size("space")
    par, group, groups = draw % 2, draw // 2, draws // 2
    block = nx // draws

    pairs = [(klo, K.at[pl.ds(0, HALO)]), (khi, K.at[pl.ds(top, HALO)])]
    mine = pl.ds(pl.multiple_of(half * par, half), half)
    other = pl.ds(pl.multiple_of(half * (1 - par), half), half)
    for lo, hi, at in ((alo, ahi, mine), (blo, bhi, other)):
        first = 0
        for field, width in ((P0, HALO), (SRC, SWEEPS), (OBS, SWEEPS)):
            span = pl.ds(first, width)
            pairs.append((lo.at[span], field.at[pl.ds(HALO - width, width), :, at]))
            pairs.append((hi.at[span], field.at[pl.ds(top, width), :, at]))
            first += width
    copies = [pltpu.make_async_copy(a, b, sems.at[i]) for i, (a, b) in enumerate(pairs)]
    for cp in copies:
        cp.start()
    for cp in copies:
        cp.wait()

    low = jnp.where(space > 0, 1.0, 0.0).astype(jnp.float32)
    high = jnp.where(space + 1 < spaces, 1.0, 0.0).astype(jnp.float32)

    def inside(zz):
        return jnp.where(zz < HALO, low, jnp.where(zz >= top, high, jnp.float32(1.0)))

    ranges = [
        [(1, HALO + 1), (top - 1, depth - 1)],
        [(2, HALO + 2), (top - 2, depth - 2)],
        [(3, HALO, False), (HALO, HALO + 3, True), (top - 3, top, True), (top, depth - 3, False)],
    ]
    sweeps(refs, ranges, inside, lambda zz: press.at[zz - HALO])
    done = [
        pltpu.make_async_copy(press.at[span], press_out.at[span], sems.at[i])
        for i, span in enumerate((pl.ds(0, SWEEPS), pl.ds(slab - SWEEPS, SWEEPS)))
    ]
    middle = pl.ds(SWEEPS, slab - 2 * SWEEPS)
    done.append(pltpu.make_async_copy(mid, press_out.at[middle], sems.at[len(done)]))
    for cp in done:
        cp.start()

    def at(r):
        return pl.ds(SUB * r, SUB)

    def gradient(zz, r):
        _, v = around(U1, zz, r, rows)
        _, w = around(E, zz, r, rows)
        return [
            0.5 * K[zz, c, at(r), :] * (G[zz, c, at(r), :] + P0[zz, c, at(r), :] * six(v[c]) + six(w[c]))
            for c in range(tiles)
        ]

    def last(z, _):
        zz = z + HALO
        for h in range(groups):
            slot = (h - group + groups) % groups
            for q in range(block // SUB):
                even = gradient(zz, (2 * h * block) // SUB + q)
                odd = gradient(zz, ((2 * h + 1) * block) // SUB + q)
                for c in range(tiles):
                    cols = pl.ds(c * LANES, LANES)
                    keep_out[slot, z, pl.ds(SUB * q, SUB), cols] = jnp.where(par == 0, even[c], odd[c])
                    send_out[slot, z, pl.ds(SUB * q, SUB), cols] = jnp.where(par == 0, odd[c], even[c])
        return 0

    lax.fori_loop(0, slab, last, 0)
    for cp in done:
        cp.wait()


def local(log_perm, noise, source, start_pressure, observe):
    draws, spaces = lax.axis_size("draw"), lax.axis_size("space")
    slab, nx, ny = log_perm.shape
    tiles, depth, half = ny // LANES, slab + 2 * HALO, nx // 2
    up = [(i, i + 1) for i in range(spaces - 1)]
    down = [(j, i) for i, j in up]
    pair = [(i, i ^ 1) for i in range(draws)]
    f32 = jnp.float32
    field = pltpu.VMEM((depth, tiles, nx, LANES), f32)
    edge = jax.ShapeDtypeStruct((EDGE, tiles, half, LANES), f32)
    rim = jax.ShapeDtypeStruct((HALO, tiles, nx, LANES), f32)
    whole = jax.ShapeDtypeStruct((slab, nx, ny), f32)
    mid = jax.ShapeDtypeStruct((slab - 2 * SWEEPS, nx, ny), f32)
    part = jax.ShapeDtypeStruct((draws // 2, slab, nx // draws, ny), f32)
    params = pltpu.CompilerParams(vmem_limit_bytes=8 * 2**20)
    cells = slab * nx * ny

    aup, adown = pl.pallas_call(
        edges_kernel,
        out_shape=(edge, edge),
        in_specs=[OFFCHIP] * 3,
        out_specs=(ONCHIP, ONCHIP),
        scratch_shapes=[pltpu.SemaphoreType.DMA((6 * tiles,))],
        compiler_params=params,
        cost_estimate=pl.CostEstimate(flops=cells, bytes_accessed=20 * cells, transcendentals=0),
    )(start_pressure, source, observe)
    alo = lax.ppermute(aup, "space", up)
    ahi = lax.ppermute(adown, "space", down)
    K, top, bottom = pl.pallas_call(
        conduct_kernel,
        out_shape=(field, rim, rim),
        in_specs=[ONCHIP] * 2,
        out_specs=(ONCHIP,) * 3,
        compiler_params=params,
        cost_estimate=pl.CostEstimate(flops=cells, bytes_accessed=12 * cells, transcendentals=cells),
    )(log_perm, noise[0])
    klo = lax.ppermute(top, "space", up)
    khi = lax.ppermute(bottom, "space", down)
    state = pl.pallas_call(
        inner_kernel,
        out_shape=(field,) * 15 + (mid,),
        in_specs=[ONCHIP] + [ANYWHERE] * 3,
        out_specs=(ONCHIP,) * 16,
        scratch_shapes=[pltpu.SemaphoreType.DMA((3 * tiles,))],
        compiler_params=params,
        cost_estimate=pl.CostEstimate(flops=200 * cells, bytes_accessed=60 * cells, transcendentals=0),
    )(K, start_pressure, source, observe)
    alo, ahi, klo, khi, last = lax.optimization_barrier((alo, ahi, klo, khi, state[-2]))
    state = (*state[:-2], last, state[-1])
    blo = lax.ppermute(alo, "draw", pair)
    bhi = lax.ppermute(ahi, "draw", pair)
    fields = (K, *state[:-1])
    n = len(fields)
    *_, press, keep, send = pl.pallas_call(
        outer_kernel,
        out_shape=(field,) * n + (whole, part, part),
        in_specs=[ONCHIP] * (7 + n),
        out_specs=(ONCHIP,) * n + (OFFCHIP, ONCHIP, ONCHIP),
        scratch_shapes=[pltpu.VMEM((slab, nx, ny), f32), pltpu.SemaphoreType.DMA((14,))],
        input_output_aliases={7 + i: i for i in range(n)},
        compiler_params=params,
        cost_estimate=pl.CostEstimate(flops=200 * cells, bytes_accessed=60 * cells, transcendentals=0),
    )(klo, khi, alo, ahi, blo, bhi, state[-1], *fields)
    got = lax.ppermute(send, "draw", pair)
    moved = [
        lax.ppermute(keep[s] + got[s], "draw", [(j, (j + 2 * s) % draws) for j in range(draws)])
        for s in range(1, draws // 2)
    ]
    total = keep[0] + got[0]
    for part_sum in moved:
        total = total + part_sum
    return press[None], total


def solution(mesh):
    return jax.shard_map(
        local,
        mesh=mesh,
        in_specs=(
            P(("epi", "space"), None, None),
            P("draw", ("epi", "space"), None, None),
            P(("epi", "space"), None, None),
            P(("epi", "space"), None, None),
            P(("epi", "space"), None, None),
        ),
        out_specs=(P("draw", ("epi", "space"), None, None), P(("epi", "space"), "draw", None)),
        check_vma=False,
    )
```

```python
import functools

import jax
import jax.numpy as jnp
from jax import lax
from jax.experimental import pallas as pl
from jax.experimental.pallas import tpu as pltpu
from jax.sharding import PartitionSpec as P

SWEEPS = 3
HALO = SWEEPS + 1
EDGE = HALO + 2 * SWEEPS
FIELDS = 16
LANES = 128
SUB = 8
ANYWHERE = pl.BlockSpec(memory_space=pl.ANY)
OFFCHIP = pl.BlockSpec(memory_space=pltpu.HBM)
ONCHIP = pl.BlockSpec(memory_space=pltpu.VMEM)


def lane_shifts(own):
    lane = lax.broadcasted_iota(jnp.int32, (SUB, LANES), 1)
    zero = jnp.zeros((SUB, LANES), jnp.float32)
    fwd = [zero] + [pltpu.roll(v, 1, 1) for v in own]
    bwd = [pltpu.roll(v, LANES - 1, 1) for v in own] + [zero]
    return [
        (jnp.where(lane == 0, fwd[c], fwd[c + 1]), jnp.where(lane == LANES - 1, bwd[c + 1], bwd[c]))
        for c in range(len(own))
    ]


def around(ref, zz, r, rows):
    sub = lax.broadcasted_iota(jnp.int32, (SUB, LANES), 0)
    zero = jnp.zeros((SUB, LANES), jnp.float32)
    own = [ref[zz, c, pl.ds(SUB * r, SUB), :] for c in range(ref.shape[1])]
    sides = lane_shifts(own)
    return own, [sides[c] + cross(ref, zz, c, r, rows, own[c], sub, zero) for c in range(len(own))]


def around_padded(ref, zz, start):
    own = [ref[zz, c, pl.ds(start, SUB), :] for c in range(ref.shape[1])]
    out = []
    for c, pair in enumerate(lane_shifts(own)):
        rest = [ref[zz, c, pl.ds(start + d, SUB), :] for d in (-1, 1)]
        out.append(pair + tuple(rest) + tuple(ref[zz + d, c, pl.ds(start, SUB), :] for d in (-1, 1)))
    return out


def cross(ref, zz, c, r, rows, own, sub, zero):
    if r > 0:
        north = ref[zz, c, pl.ds(SUB * r - 1, SUB), :]
    else:
        north = jnp.where(sub == 0, zero, pltpu.roll(own, 1, 0))
    if r + 1 < rows:
        south = ref[zz, c, pl.ds(SUB * r + 1, SUB), :]
    else:
        south = jnp.where(sub == SUB - 1, zero, pltpu.roll(own, SUB - 1, 0))
    here = pl.ds(SUB * r, SUB)
    return north, south, ref[zz - 1, c, here, :], ref[zz + 1, c, here, :]


def faces(K, WL, WR, zz, c, r, rows):
    sub = lax.broadcasted_iota(jnp.int32, (SUB, LANES), 0)
    zero = jnp.zeros((SUB, LANES), jnp.float32)
    here = pl.ds(SUB * r, SUB)
    k = K[zz, c, here, :]
    rest = [k + v for v in cross(K, zz, c, r, rows, k, sub, zero)]
    return (WL[zz, c, here, :], WR[zz, c, here, :], *rest)


def six(parts):
    a, b, c, d, e, f = parts
    return ((a + b) + (c + d)) + (e + f)


def weighted(weights, parts):
    return six([w * v for w, v in zip(weights, parts)])


def sweeps(refs, ranges, inside, press):
    K, P0, SRC, OBS, P1, P2, U1, U2, U3, HR, SR, NP0, WL, WR, G, E = refs
    tiles, rows = K.shape[1], K.shape[2] // SUB

    def at(r):
        return pl.ds(SUB * r, SUB)

    def first(zz):
        valid = inside(zz)
        for r in range(rows):
            k, kn = around(K, zz, r, rows)
            _, pn = around(P0, zz, r, rows)
            for c in range(tiles):
                w = [k[c] + v for v in kn[c]]
                rinv = valid / (0.5 + 0.5 * six(w))
                hr = 0.5 * rinv
                sr = SRC[zz, c, at(r), :] * rinv
                HR[zz, c, at(r), :] = hr
                SR[zz, c, at(r), :] = sr
                WL[zz, c, at(r), :] = w[0]
                WR[zz, c, at(r), :] = w[1]
                NP0[zz, c, at(r), :] = six(pn[c])
                P1[zz, c, at(r), :] = sr + weighted(w, pn[c]) * hr
                U3[zz, c, at(r), :] = OBS[zz, c, at(r), :] * rinv

    def second(zz):
        for r in range(rows):
            _, a = around(P1, zz, r, rows)
            _, v = around(U3, zz, r, rows)
            for c in range(tiles):
                w = faces(K, WL, WR, zz, c, r, rows)
                hr = HR[zz, c, at(r), :]
                p2 = SR[zz, c, at(r), :] + weighted(w, a[c]) * hr
                u2 = weighted(w, v[c]) * hr
                P2[zz, c, at(r), :] = p2
                U2[zz, c, at(r), :] = u2
                G[zz, c, at(r), :] = u2 * six(a[c]) + p2 * six(v[c])

    def third(zz, own):
        for r in range(rows):
            p2, a = around(P2, zz, r, rows)
            u2, v = around(U2, zz, r, rows)
            for c in range(tiles):
                w = faces(K, WL, WR, zz, c, r, rows)
                hr = HR[zz, c, at(r), :]
                p1, u3 = P1[zz, c, at(r), :], U3[zz, c, at(r), :]
                p3 = SR[zz, c, at(r), :] + weighted(w, a[c]) * hr
                u1 = weighted(w, v[c]) * hr
                e = -(u1 * p1 + u2[c] * p2[c] + u3 * p3)
                U1[zz, c, at(r + 1), :] = u1
                E[zz, c, at(r + 1), :] = e
                if own:
                    g = u3 * six(a[c]) + p1 * six(v[c]) + u1 * NP0[zz, c, at(r), :]
                    press(zz)[at(r), pl.ds(c * LANES, LANES)] = p3
                    G[zz, c, at(r), :] = (G[zz, c, at(r), :] + 6.0 * e) + g

    for body, spans in zip((first, second, third), ranges):
        for span in spans:
            lo, hi, *own = span
            lax.fori_loop(lo, hi, lambda zz, _, body=body, own=own: body(zz, *own) or 0, 0)


def edges_kernel(p0, src, obs, up, down, sems):
    nx, ny = p0.shape[1:]
    slab, half = p0.shape[0], nx // 2
    rows = pl.ds(pl.multiple_of(half * (lax.axis_index("draw") % 2), half), half)
    copies = []
    for c in range(ny // LANES):
        cols = pl.ds(c * LANES, LANES)
        at = 0
        for ref, width in ((p0, HALO), (src, SWEEPS), (obs, SWEEPS)):
            for start, out in ((slab - width, up), (0, down)):
                copies.append(
                    pltpu.make_async_copy(
                        ref.at[pl.ds(start, width), rows, cols], out.at[pl.ds(at, width), c], sems.at[len(copies)]
                    )
                )
            at += width
    for cp in copies:
        cp.start()
    for cp in copies:
        cp.wait()


def conduct_kernel(log_perm, noise, K, top, bottom):
    slab, nx, ny = log_perm.shape

    def plane(z, _):
        for r in range(nx // SUB):
            for c in range(ny // LANES):
                here, cols = pl.ds(SUB * r, SUB), pl.ds(c * LANES, LANES)
                K[z + HALO, c, here, :] = jnp.exp(log_perm[z, here, cols] + noise[z, here, cols])
        return 0

    lax.fori_loop(0, slab, plane, 0)

    def edge(z, _):
        top[z] = K[slab + z]
        bottom[z] = K[HALO + z]
        return 0

    lax.fori_loop(0, HALO, edge, 0)


def inner_kernel(K, p0, src, obs, P0, SRC, OBS, P1, P2, U1, U2, U3, HR, SR, NP0, WL, WR, G, E, mid, sems):
    slab = p0.shape[0]
    top = HALO + slab
    copies = []
    for c in range(K.shape[1]):
        for ref, out in ((p0, P0), (src, SRC), (obs, OBS)):
            copies.append(
                pltpu.make_async_copy(
                    ref.at[:, :, pl.ds(c * LANES, LANES)], out.at[pl.ds(HALO, slab), c], sems.at[len(copies)]
                )
            )
    for cp in copies:
        cp.start()
    for cp in copies:
        cp.wait()
    rim = jnp.zeros((SUB, LANES), jnp.float32)

    def clear(zz, _):
        for ref in (U1, E):
            for c in range(ref.shape[1]):
                ref[zz, c, pl.ds(0, SUB), :] = rim
                ref[zz, c, pl.ds(ref.shape[2] - SUB, SUB), :] = rim
        return 0

    lax.fori_loop(HALO, top, clear, 0)
    refs = (K, P0, SRC, OBS, P1, P2, U1, U2, U3, HR, SR, NP0, WL, WR, G, E)
    ranges = [[(HALO + n, top - n)] for n in (1, 2)] + [[(HALO + 3, top - 3, True)]]
    sweeps(refs, ranges, lambda zz: jnp.float32(1.0), lambda zz: mid.at[zz - HALO - SWEEPS])


def side_kernel(low, *args):
    khalo, mine, theirs = args[:3]
    refs, sems = args[3 + FIELDS : 3 + 2 * FIELDS], args[-1]
    press, sends = args[3 + 2 * FIELDS], args[4 + 2 * FIELDS : -1]
    K, P0, SRC, OBS = refs[:4]
    nx = K.shape[2]
    depth = K.shape[0]
    half, top = nx // 2, depth - HALO
    par = lax.axis_index("draw") % 2

    pairs = [(khalo, K.at[pl.ds(0 if low else top, HALO)])]
    for half_rows, which in ((mine, par), (theirs, 1 - par)):
        rows = pl.ds(pl.multiple_of(half * which, half), half)
        first = 0
        for field, width in ((P0, HALO), (SRC, SWEEPS), (OBS, SWEEPS)):
            planes = pl.ds(HALO - width if low else top, width)
            pairs.append((half_rows.at[pl.ds(first, width)], field.at[planes, :, rows]))
            first += width
    copies = [pltpu.make_async_copy(a, b, sems.at[i]) for i, (a, b) in enumerate(pairs)]
    for cp in copies:
        cp.start()
    for cp in copies:
        cp.wait()

    space, spaces = lax.axis_index("space"), lax.axis_size("space")
    met = jnp.where(space > 0 if low else space + 1 < spaces, 1.0, 0.0).astype(jnp.float32)
    if low:
        ranges = [[(1, HALO + 1)], [(2, HALO + 2)], [(3, HALO, False), (HALO, HALO + 3, True)]]
        shift = HALO
    else:
        ranges = [[(top - 1, depth - 1)], [(top - 2, depth - 2)], [(top - 3, top, True), (top, depth - 3, False)]]
        shift = top - 3

    def inside(zz):
        return jnp.where(zz < HALO if low else zz >= top, met, jnp.float32(1.0))

    sweeps(refs, ranges, inside, lambda zz: press.at[zz - shift])
    if sends:
        gradients(K, P0, refs[6], refs[-2], refs[-1], [(sends[0], 1 - par, 1)])


def gradients(K, P0, U1, G, E, parts):
    tiles, nx, slab = K.shape[1], K.shape[2], K.shape[0] - 2 * HALO
    draw, draws = lax.axis_index("draw"), lax.axis_size("draw")
    block, groups = nx // draws, draws // 2

    def plane(z, _):
        zz = z + HALO
        for out, parity, first in parts:
            for s in range(out.shape[0]):
                base = (2 * ((draw // 2 + first + s) % groups) + parity) * block
                for q in range(block // SUB):
                    start = pl.multiple_of(base + SUB * q, SUB)
                    v = around_padded(U1, zz, pl.multiple_of(start + SUB, SUB))
                    w = around_padded(E, zz, pl.multiple_of(start + SUB, SUB))
                    at = pl.ds(start, SUB)
                    for c in range(tiles):
                        g = G[zz, c, at, :] + P0[zz, c, at, :] * six(v[c]) + six(w[c])
                        out[s, z, pl.ds(SUB * q, SUB), pl.ds(c * LANES, LANES)] = 0.5 * K[zz, c, at, :] * g
        return 0

    lax.fori_loop(0, slab, plane, 0)


def rest_kernel(low, mid, high, K, P0, U1, G, E, press, keep_near, keep_far, send_near, sems):
    slab, nx = press.shape[:2]
    par = lax.axis_index("draw") % 2
    copies, at = [], 0
    for ref in (low, mid, high):
        copies.append(pltpu.make_async_copy(ref, press.at[pl.ds(at, ref.shape[0])], sems.at[len(copies)]))
        at += ref.shape[0]
    for cp in copies:
        cp.start()
    gradients(K, P0, U1, G, E, [(keep_far, par, 1), (keep_near, par, 0), (send_near, 1 - par, 0)])
    for cp in copies:
        cp.wait()


def local(log_perm, noise, source, start_pressure, observe):
    draws, spaces = lax.axis_size("draw"), lax.axis_size("space")
    slab, nx, ny = log_perm.shape
    tiles, depth, half = ny // LANES, slab + 2 * HALO, nx // 2
    up = [(i, i + 1) for i in range(spaces - 1)]
    down = [(j, i) for i, j in up]
    pair = [(i, i ^ 1) for i in range(draws)]
    f32 = jnp.float32
    field = pltpu.VMEM((depth, tiles, nx, LANES), f32)
    padded = pltpu.VMEM((depth, tiles, nx + 2 * SUB, LANES), f32)
    kinds = [field] * 6 + [padded] + [field] * 8 + [padded]
    edge = jax.ShapeDtypeStruct((EDGE, tiles, half, LANES), f32)
    rim = jax.ShapeDtypeStruct((HALO, tiles, nx, LANES), f32)
    whole = jax.ShapeDtypeStruct((slab, nx, ny), f32)
    mid = jax.ShapeDtypeStruct((slab - 2 * SWEEPS, nx, ny), f32)
    groups = draws // 2
    near, far = [jax.ShapeDtypeStruct((n, slab, nx // draws, ny), f32) for n in (1, groups - 1)]
    params = pltpu.CompilerParams(vmem_limit_bytes=8 * 2**20)
    cells = slab * nx * ny

    aup, adown = pl.pallas_call(
        edges_kernel,
        out_shape=(edge, edge),
        in_specs=[OFFCHIP] * 3,
        out_specs=(ONCHIP, ONCHIP),
        scratch_shapes=[pltpu.SemaphoreType.DMA((6 * tiles,))],
        compiler_params=params,
        cost_estimate=pl.CostEstimate(flops=cells, bytes_accessed=20 * cells, transcendentals=0),
    )(*[pltpu.with_memory_space_constraint(a, pltpu.HBM) for a in (start_pressure, source, observe)])
    alo = lax.ppermute(aup, "space", up)
    ahi = lax.ppermute(adown, "space", down)
    K, top, bottom = pl.pallas_call(
        conduct_kernel,
        out_shape=(field, rim, rim),
        in_specs=[ONCHIP] * 2,
        out_specs=(ONCHIP,) * 3,
        compiler_params=params,
        cost_estimate=pl.CostEstimate(flops=cells, bytes_accessed=12 * cells, transcendentals=cells),
    )(log_perm, noise[0])
    klo = lax.ppermute(top, "space", up)
    khi = lax.ppermute(bottom, "space", down)
    state = pl.pallas_call(
        inner_kernel,
        out_shape=(*kinds[1:], mid),
        in_specs=[ONCHIP] + [ANYWHERE] * 3,
        out_specs=(ONCHIP,) * 16,
        scratch_shapes=[pltpu.SemaphoreType.DMA((3 * tiles,))],
        compiler_params=params,
        cost_estimate=pl.CostEstimate(flops=200 * cells, bytes_accessed=60 * cells, transcendentals=0),
    )(K, start_pressure, source, observe)
    alo, ahi, klo, khi, last = lax.optimization_barrier((alo, ahi, klo, khi, state[-2]))
    state = (*state[:-2], last, state[-1])
    blo = lax.ppermute(alo, "draw", pair)
    bhi = lax.ppermute(ahi, "draw", pair)
    fields, centre = (K, *state[:-1]), state[-1]

    def side(low, khalo, mine, theirs, fields):
        ends = (jax.ShapeDtypeStruct((SWEEPS, nx, ny), f32),) + ((far,) if low else ())
        out = pl.pallas_call(
            functools.partial(side_kernel, low),
            out_shape=(*kinds, *ends),
            in_specs=[ONCHIP] * (3 + FIELDS),
            out_specs=(ONCHIP,) * (FIELDS + len(ends)),
            scratch_shapes=[pltpu.SemaphoreType.DMA((7,))],
            input_output_aliases={3 + i: i for i in range(FIELDS)},
            compiler_params=params,
            cost_estimate=pl.CostEstimate(flops=100 * cells, bytes_accessed=30 * cells, transcendentals=0),
        )(khalo, mine, theirs, *fields)
        return out[:FIELDS], *out[FIELDS:]

    fields, high = side(False, khi, ahi, bhi, fields)
    fields, low, send_far = side(True, klo, alo, blo, fields)
    got_far = lax.ppermute(send_far, "draw", pair)
    press, keep_near, keep_far, send_near = pl.pallas_call(
        rest_kernel,
        out_shape=(whole, near, far, near),
        in_specs=[ONCHIP] * 8,
        out_specs=(OFFCHIP,) + (ONCHIP,) * 3,
        scratch_shapes=[pltpu.SemaphoreType.DMA((3,))],
        compiler_params=params,
        cost_estimate=pl.CostEstimate(flops=30 * cells, bytes_accessed=30 * cells, transcendentals=0),
    )(low, centre, high, fields[0], fields[1], fields[6], fields[14], fields[15])
    moved = [
        lax.ppermute(keep_far[s - 1] + got_far[s - 1], "draw", [(j, (j + 2 * s) % draws) for j in range(draws)])
        for s in range(1, groups)
    ]
    total = keep_near[0] + lax.ppermute(send_near, "draw", pair)[0]
    for part_sum in moved:
        total = total + part_sum
    return press[None], total


def solution(mesh):
    return jax.shard_map(
        local,
        mesh=mesh,
        in_specs=(
            P(("epi", "space"), None, None),
            P("draw", ("epi", "space"), None, None),
            P(("epi", "space"), None, None),
            P(("epi", "space"), None, None),
            P(("epi", "space"), None, None),
        ),
        out_specs=(P("draw", ("epi", "space"), None, None), P(("epi", "space"), "draw", None)),
        check_vma=False,
    )
```

```python
import functools

import jax
import jax.numpy as jnp
from jax import lax
from jax.experimental import pallas as pl
from jax.experimental.pallas import tpu as pltpu
from jax.sharding import PartitionSpec as P

SWEEPS = 3
HALO = SWEEPS + 1
EDGE = HALO + 2 * SWEEPS
FIELDS = 16
LANES = 128
SUB = 8
ANYWHERE = pl.BlockSpec(memory_space=pl.ANY)
OFFCHIP = pl.BlockSpec(memory_space=pltpu.HBM)
ONCHIP = pl.BlockSpec(memory_space=pltpu.VMEM)


def lane_shifts(own):
    lane = lax.broadcasted_iota(jnp.int32, (SUB, LANES), 1)
    zero = jnp.zeros((SUB, LANES), jnp.float32)
    fwd = [zero] + [pltpu.roll(v, 1, 1) for v in own]
    bwd = [pltpu.roll(v, LANES - 1, 1) for v in own] + [zero]
    return [
        (jnp.where(lane == 0, fwd[c], fwd[c + 1]), jnp.where(lane == LANES - 1, bwd[c + 1], bwd[c]))
        for c in range(len(own))
    ]


def around(ref, zz, r, rows):
    sub = lax.broadcasted_iota(jnp.int32, (SUB, LANES), 0)
    zero = jnp.zeros((SUB, LANES), jnp.float32)
    own = [ref[zz, c, pl.ds(SUB * r, SUB), :] for c in range(ref.shape[1])]
    sides = lane_shifts(own)
    return own, [sides[c] + cross(ref, zz, c, r, rows, own[c], sub, zero) for c in range(len(own))]


def around_padded(ref, zz, start):
    own = [ref[zz, c, pl.ds(start, SUB), :] for c in range(ref.shape[1])]
    out = []
    for c, pair in enumerate(lane_shifts(own)):
        rest = [ref[zz, c, pl.ds(start + d, SUB), :] for d in (-1, 1)]
        out.append(pair + tuple(rest) + tuple(ref[zz + d, c, pl.ds(start, SUB), :] for d in (-1, 1)))
    return out


def cross(ref, zz, c, r, rows, own, sub, zero):
    if r > 0:
        north = ref[zz, c, pl.ds(SUB * r - 1, SUB), :]
    else:
        north = jnp.where(sub == 0, zero, pltpu.roll(own, 1, 0))
    if r + 1 < rows:
        south = ref[zz, c, pl.ds(SUB * r + 1, SUB), :]
    else:
        south = jnp.where(sub == SUB - 1, zero, pltpu.roll(own, SUB - 1, 0))
    here = pl.ds(SUB * r, SUB)
    return north, south, ref[zz - 1, c, here, :], ref[zz + 1, c, here, :]


def faces(K, WL, WR, zz, c, r, rows):
    sub = lax.broadcasted_iota(jnp.int32, (SUB, LANES), 0)
    zero = jnp.zeros((SUB, LANES), jnp.float32)
    here = pl.ds(SUB * r, SUB)
    k = K[zz, c, here, :]
    rest = [k + v for v in cross(K, zz, c, r, rows, k, sub, zero)]
    return (WL[zz, c, here, :], WR[zz, c, here, :], *rest)


def six(parts):
    a, b, c, d, e, f = parts
    return ((a + b) + (c + d)) + (e + f)


def weighted(weights, parts):
    return six([w * v for w, v in zip(weights, parts)])


def sweeps(refs, ranges, inside, press):
    K, P0, SRC, OBS, P1, P2, U1, U2, U3, HR, SR, NP0, WL, WR, G, E = refs
    tiles, rows = K.shape[1], K.shape[2] // SUB

    def at(r):
        return pl.ds(SUB * r, SUB)

    def first(zz):
        valid = inside(zz)
        for r in range(rows):
            k, kn = around(K, zz, r, rows)
            _, pn = around(P0, zz, r, rows)
            for c in range(tiles):
                w = [k[c] + v for v in kn[c]]
                rinv = valid / (0.5 + 0.5 * six(w))
                hr = 0.5 * rinv
                sr = SRC[zz, c, at(r), :] * rinv
                HR[zz, c, at(r), :] = hr
                SR[zz, c, at(r), :] = sr
                WL[zz, c, at(r), :] = w[0]
                WR[zz, c, at(r), :] = w[1]
                NP0[zz, c, at(r), :] = six(pn[c])
                P1[zz, c, at(r), :] = sr + weighted(w, pn[c]) * hr
                U3[zz, c, at(r), :] = OBS[zz, c, at(r), :] * rinv

    def second(zz):
        for r in range(rows):
            _, a = around(P1, zz, r, rows)
            _, v = around(U3, zz, r, rows)
            for c in range(tiles):
                w = faces(K, WL, WR, zz, c, r, rows)
                hr = HR[zz, c, at(r), :]
                p2 = SR[zz, c, at(r), :] + weighted(w, a[c]) * hr
                u2 = weighted(w, v[c]) * hr
                P2[zz, c, at(r), :] = p2
                U2[zz, c, at(r), :] = u2
                G[zz, c, at(r), :] = u2 * six(a[c]) + p2 * six(v[c])

    def third(zz, own):
        for r in range(rows):
            p2, a = around(P2, zz, r, rows)
            u2, v = around(U2, zz, r, rows)
            for c in range(tiles):
                w = faces(K, WL, WR, zz, c, r, rows)
                hr = HR[zz, c, at(r), :]
                p1, u3 = P1[zz, c, at(r), :], U3[zz, c, at(r), :]
                p3 = SR[zz, c, at(r), :] + weighted(w, a[c]) * hr
                u1 = weighted(w, v[c]) * hr
                e = -(u1 * p1 + u2[c] * p2[c] + u3 * p3)
                U1[zz, c, at(r + 1), :] = u1
                E[zz, c, at(r + 1), :] = e
                if own:
                    g = u3 * six(a[c]) + p1 * six(v[c]) + u1 * NP0[zz, c, at(r), :]
                    press(zz)[at(r), pl.ds(c * LANES, LANES)] = p3
                    G[zz, c, at(r), :] = (G[zz, c, at(r), :] + 6.0 * e) + g

    for body, spans in zip((first, second, third), ranges):
        for span in spans:
            lo, hi, *own = span
            lax.fori_loop(lo, hi, lambda zz, _, body=body, own=own: body(zz, *own) or 0, 0)


def first_kernel(log_perm, noise, p0, src, obs, K, up, down, means, draws, sems):
    slab, nx, ny = log_perm.shape
    tiles, half = ny // LANES, nx // 2
    rows = pl.ds(pl.multiple_of(half * (lax.axis_index("draw") % 2), half), half)
    copies = []

    def copy(src_ref, dst_ref):
        copies.append(pltpu.make_async_copy(src_ref, dst_ref, sems.at[len(copies)]))

    copy(log_perm, means)
    copy(noise, draws)
    for c in range(tiles):
        cols = pl.ds(c * LANES, LANES)
        at = 0
        for ref, width in ((p0, HALO), (src, SWEEPS), (obs, SWEEPS)):
            for start, out in ((slab - width, up), (0, down)):
                copy(ref.at[pl.ds(start, width), rows, cols], out.at[pl.ds(at, width), c])
            at += width
    for cp in copies:
        cp.start()
    for cp in copies[:2]:
        cp.wait()

    def plane(z, _, out=None, first=0):
        for r in range(nx // SUB):
            for c in range(tiles):
                here, cols = pl.ds(SUB * r, SUB), pl.ds(c * LANES, LANES)
                k = jnp.exp(means[z, here, cols] + draws[z, here, cols])
                K[z + HALO, c, here, :] = k
                if out is not None:
                    part, at = divmod(SUB * r, half)
                    out[EDGE + part * HALO + z - first, c, pl.ds(at, SUB), :] = k
        return 0

    low, high = functools.partial(plane, out=down), functools.partial(plane, out=up, first=slab - HALO)
    lax.fori_loop(0, HALO, low, 0)
    lax.fori_loop(HALO, slab - HALO, plane, 0)
    lax.fori_loop(slab - HALO, slab, high, 0)
    for cp in copies[2:]:
        cp.wait()


def inner_kernel(K, p0, src, obs, P0, SRC, OBS, P1, P2, U1, U2, U3, HR, SR, NP0, WL, WR, G, E, mid, sems):
    slab = p0.shape[0]
    top = HALO + slab
    copies = []
    for c in range(K.shape[1]):
        for ref, out in ((p0, P0), (src, SRC), (obs, OBS)):
            copies.append(
                pltpu.make_async_copy(
                    ref.at[:, :, pl.ds(c * LANES, LANES)], out.at[pl.ds(HALO, slab), c], sems.at[len(copies)]
                )
            )
    for cp in copies:
        cp.start()
    for cp in copies:
        cp.wait()
    rim = jnp.zeros((SUB, LANES), jnp.float32)

    def clear(zz, _):
        for ref in (U1, E):
            for c in range(ref.shape[1]):
                ref[zz, c, pl.ds(0, SUB), :] = rim
                ref[zz, c, pl.ds(ref.shape[2] - SUB, SUB), :] = rim
        return 0

    lax.fori_loop(HALO, top, clear, 0)
    refs = (K, P0, SRC, OBS, P1, P2, U1, U2, U3, HR, SR, NP0, WL, WR, G, E)
    ranges = [[(HALO + n, top - n)] for n in (1, 2)] + [[(HALO + 3, top - 3, True)]]
    sweeps(refs, ranges, lambda zz: jnp.float32(1.0), lambda zz: mid.at[zz - HALO - SWEEPS])


def side_kernel(low, stages, *args):
    halos = args[: 2 if 0 in stages else 0]
    refs = args[len(halos) + FIELDS : len(halos) + 2 * FIELDS]
    ends = args[len(halos) + 2 * FIELDS :]
    K, P0, SRC, OBS = refs[:4]
    nx, depth = K.shape[2], K.shape[0]
    half, top = nx // 2, depth - HALO
    par = lax.axis_index("draw") % 2

    if halos:
        mine, theirs = halos
        sems = ends[-1]
        pairs = [
            (mine.at[pl.ds(EDGE + h * HALO, HALO)], K.at[pl.ds(0 if low else top, HALO), :, pl.ds(h * half, half)])
            for h in range(2)
        ]
        for half_rows, which in ((mine, par), (theirs, 1 - par)):
            rows = pl.ds(pl.multiple_of(half * which, half), half)
            first = 0
            for field, width in ((P0, HALO), (SRC, SWEEPS), (OBS, SWEEPS)):
                planes = pl.ds(HALO - width if low else top, width)
                pairs.append((half_rows.at[pl.ds(first, width)], field.at[planes, :, rows]))
                first += width
        copies = [pltpu.make_async_copy(a, b, sems.at[i]) for i, (a, b) in enumerate(pairs)]
        for cp in copies:
            cp.start()
        for cp in copies:
            cp.wait()

    space, spaces = lax.axis_index("space"), lax.axis_size("space")
    met = jnp.where(space > 0 if low else space + 1 < spaces, 1.0, 0.0).astype(jnp.float32)
    if low:
        ranges = [[(1, HALO + 1)], [(2, HALO + 2)], [(3, HALO, False), (HALO, HALO + 3, True)]]
        shift = HALO
    else:
        ranges = [[(top - 1, depth - 1)], [(top - 2, depth - 2)], [(top - 3, top, True), (top, depth - 3, False)]]
        shift = top - 3

    def inside(zz):
        return jnp.where(zz < HALO if low else zz >= top, met, jnp.float32(1.0))

    ranges = [spans if n in stages else [] for n, spans in enumerate(ranges)]
    sweeps(refs, ranges, inside, lambda zz: ends[0].at[zz - shift])
    if not low:
        gradients(K, P0, refs[6], refs[-2], refs[-1], [(ends[1], 1 - par, 1)])


def gradients(K, P0, U1, G, E, parts):
    tiles, nx, slab = K.shape[1], K.shape[2], K.shape[0] - 2 * HALO
    draw, draws = lax.axis_index("draw"), lax.axis_size("draw")
    block, groups = nx // draws, draws // 2

    def plane(z, _):
        zz = z + HALO
        for out, parity, first in parts:
            for s in range(out.shape[0]):
                base = (2 * ((draw // 2 + first + s) % groups) + parity) * block
                for q in range(block // SUB):
                    start = pl.multiple_of(base + SUB * q, SUB)
                    v = around_padded(U1, zz, pl.multiple_of(start + SUB, SUB))
                    w = around_padded(E, zz, pl.multiple_of(start + SUB, SUB))
                    at = pl.ds(start, SUB)
                    for c in range(tiles):
                        g = G[zz, c, at, :] + P0[zz, c, at, :] * six(v[c]) + six(w[c])
                        out[s, z, pl.ds(SUB * q, SUB), pl.ds(c * LANES, LANES)] = 0.5 * K[zz, c, at, :] * g
        return 0

    lax.fori_loop(0, slab, plane, 0)


def rest_kernel(low, mid, high, K, P0, U1, G, E, press, keep_near, keep_far, send_near, sems):
    slab, nx = press.shape[:2]
    par = lax.axis_index("draw") % 2
    copies, at = [], 0
    for ref in (low, mid, high):
        copies.append(pltpu.make_async_copy(ref, press.at[pl.ds(at, ref.shape[0])], sems.at[len(copies)]))
        at += ref.shape[0]
    for cp in copies:
        cp.start()
    gradients(K, P0, U1, G, E, [(keep_far, par, 1), (keep_near, par, 0), (send_near, 1 - par, 0)])
    for cp in copies:
        cp.wait()


def local(log_perm, noise, source, start_pressure, observe):
    draws, spaces = lax.axis_size("draw"), lax.axis_size("space")
    slab, nx, ny = log_perm.shape
    tiles, depth, half = ny // LANES, slab + 2 * HALO, nx // 2
    up = [(i, i + 1) for i in range(spaces - 1)]
    down = [(j, i) for i, j in up]
    pair = [(i, i ^ 1) for i in range(draws)]
    f32 = jnp.float32
    field = pltpu.VMEM((depth, tiles, nx, LANES), f32)
    padded = pltpu.VMEM((depth, tiles, nx + 2 * SUB, LANES), f32)
    kinds = [field] * 6 + [padded] + [field] * 8 + [padded]
    edge = jax.ShapeDtypeStruct((EDGE + 2 * HALO, tiles, half, LANES), f32)
    whole = jax.ShapeDtypeStruct((slab, nx, ny), f32)
    mid = jax.ShapeDtypeStruct((slab - 2 * SWEEPS, nx, ny), f32)
    groups = draws // 2
    near, far = [jax.ShapeDtypeStruct((n, slab, nx // draws, ny), f32) for n in (1, groups - 1)]
    params = pltpu.CompilerParams(vmem_limit_bytes=8 * 2**20)
    cells = slab * nx * ny

    inputs = (log_perm, noise[0], start_pressure, source, observe)
    K, to_up, to_down = pl.pallas_call(
        first_kernel,
        out_shape=(field, edge, edge),
        in_specs=[OFFCHIP] * 5,
        out_specs=(ONCHIP,) * 3,
        scratch_shapes=[pltpu.VMEM((slab, nx, ny), f32)] * 2 + [pltpu.SemaphoreType.DMA((2 + 6 * tiles,))],
        compiler_params=params,
        cost_estimate=pl.CostEstimate(flops=cells, bytes_accessed=20 * cells, transcendentals=cells),
    )(*[pltpu.with_memory_space_constraint(a, pltpu.HBM) for a in inputs])
    alo = lax.ppermute(to_up, "space", up)
    ahi = lax.ppermute(to_down, "space", down)
    state = pl.pallas_call(
        inner_kernel,
        out_shape=(*kinds[1:], mid),
        in_specs=[ONCHIP] + [ANYWHERE] * 3,
        out_specs=(ONCHIP,) * 16,
        scratch_shapes=[pltpu.SemaphoreType.DMA((3 * tiles,))],
        compiler_params=params,
        cost_estimate=pl.CostEstimate(flops=200 * cells, bytes_accessed=60 * cells, transcendentals=0),
    )(K, start_pressure, source, observe)
    fields, centre = (K, *state[:-1]), state[-1]

    def side(low, stages, halos, fields):
        ends = (jax.ShapeDtypeStruct((SWEEPS, nx, ny), f32),) if 2 in stages else ()
        ends = ends if low else (*ends, far)
        n = len(halos)
        out = pl.pallas_call(
            functools.partial(side_kernel, low, stages),
            out_shape=(*kinds, *ends),
            in_specs=[ONCHIP] * (n + FIELDS),
            out_specs=(ONCHIP,) * (FIELDS + len(ends)),
            scratch_shapes=[pltpu.SemaphoreType.DMA((8,))] if n else [],
            input_output_aliases={n + i: i for i in range(FIELDS)},
            compiler_params=params,
            cost_estimate=pl.CostEstimate(flops=60 * cells, bytes_accessed=20 * cells, transcendentals=0),
        )(*halos, *fields)
        return out[:FIELDS], *out[FIELDS:]

    def swapped(got, fields):
        got, last = lax.optimization_barrier((got, fields[-1]))
        return (got, lax.ppermute(got[:EDGE], "draw", pair)), (*fields[:-1], last)

    halos, fields = swapped(alo, fields)
    (fields,) = side(True, (0,), halos, fields)
    halos, fields = swapped(ahi, fields)
    fields, low = side(True, (1, 2), (), fields)
    fields, high, send_far = side(False, (0, 1, 2), halos, fields)
    got_far = lax.ppermute(send_far, "draw", pair)
    press, keep_near, keep_far, send_near = pl.pallas_call(
        rest_kernel,
        out_shape=(whole, near, far, near),
        in_specs=[ONCHIP] * 8,
        out_specs=(OFFCHIP,) + (ONCHIP,) * 3,
        scratch_shapes=[pltpu.SemaphoreType.DMA((3,))],
        compiler_params=params,
        cost_estimate=pl.CostEstimate(flops=30 * cells, bytes_accessed=30 * cells, transcendentals=0),
    )(low, centre, high, fields[0], fields[1], fields[6], fields[14], fields[15])
    moved = [
        lax.ppermute(keep_far[s - 1] + got_far[s - 1], "draw", [(j, (j + 2 * s) % draws) for j in range(draws)])
        for s in range(1, groups)
    ]
    total = keep_near[0] + lax.ppermute(send_near, "draw", pair)[0]
    for part_sum in moved:
        total = total + part_sum
    return press[None], total


def solution(mesh):
    return jax.shard_map(
        local,
        mesh=mesh,
        in_specs=(
            P(("epi", "space"), None, None),
            P("draw", ("epi", "space"), None, None),
            P(("epi", "space"), None, None),
            P(("epi", "space"), None, None),
            P(("epi", "space"), None, None),
        ),
        out_specs=(P("draw", ("epi", "space"), None, None), P(("epi", "space"), "draw", None)),
        check_vma=False,
    )
```

```python
import functools

import jax
import jax.numpy as jnp
from jax import lax
from jax.experimental import pallas as pl
from jax.experimental.pallas import tpu as pltpu
from jax.sharding import PartitionSpec as P

SWEEPS = 3
HALO = SWEEPS + 1
EDGE = HALO + 2 * SWEEPS
FIELDS = 16
LANES = 128
SUB = 8
ANYWHERE = pl.BlockSpec(memory_space=pl.ANY)
OFFCHIP = pl.BlockSpec(memory_space=pltpu.HBM)
ONCHIP = pl.BlockSpec(memory_space=pltpu.VMEM)


def lane_shifts(own):
    lane = lax.broadcasted_iota(jnp.int32, (SUB, LANES), 1)
    zero = jnp.zeros((SUB, LANES), jnp.float32)
    fwd = [zero] + [pltpu.roll(v, 1, 1) for v in own]
    bwd = [pltpu.roll(v, LANES - 1, 1) for v in own] + [zero]
    return [
        (jnp.where(lane == 0, fwd[c], fwd[c + 1]), jnp.where(lane == LANES - 1, bwd[c + 1], bwd[c]))
        for c in range(len(own))
    ]


def around(ref, zz, r, rows):
    sub = lax.broadcasted_iota(jnp.int32, (SUB, LANES), 0)
    zero = jnp.zeros((SUB, LANES), jnp.float32)
    own = [ref[zz, c, pl.ds(SUB * r, SUB), :] for c in range(ref.shape[1])]
    sides = lane_shifts(own)
    return own, [sides[c] + cross(ref, zz, c, r, rows, own[c], sub, zero) for c in range(len(own))]


def around_padded(ref, zz, start, count):
    sub = lax.broadcasted_iota(jnp.int32, (SUB, LANES), 0)
    groups = [pl.ds(pl.multiple_of(start + SUB * (q - 1), SUB), SUB) for q in range(count + 2)]
    tiles = ref.shape[1]
    own = [[ref[zz, c, g, :] for c in range(tiles)] for g in groups]
    down = [[pltpu.roll(v, 1, 0) for v in line] for line in own[:-1]]
    up = [[pltpu.roll(v, SUB - 1, 0) for v in line] for line in own[1:]]
    out = []
    for q in range(1, count + 1):
        sides = lane_shifts(own[q])
        line = []
        for c in range(tiles):
            north = jnp.where(sub == 0, down[q - 1][c], down[q][c])
            south = jnp.where(sub == SUB - 1, up[q][c], up[q - 1][c])
            line.append(sides[c] + (north, south, ref[zz - 1, c, groups[q], :], ref[zz + 1, c, groups[q], :]))
        out.append(line)
    return out


def cross(ref, zz, c, r, rows, own, sub, zero):
    if r > 0:
        north = ref[zz, c, pl.ds(SUB * r - 1, SUB), :]
    else:
        north = jnp.where(sub == 0, zero, pltpu.roll(own, 1, 0))
    if r + 1 < rows:
        south = ref[zz, c, pl.ds(SUB * r + 1, SUB), :]
    else:
        south = jnp.where(sub == SUB - 1, zero, pltpu.roll(own, SUB - 1, 0))
    here = pl.ds(SUB * r, SUB)
    return north, south, ref[zz - 1, c, here, :], ref[zz + 1, c, here, :]


def faces(K, WL, WR, zz, c, r, rows):
    sub = lax.broadcasted_iota(jnp.int32, (SUB, LANES), 0)
    zero = jnp.zeros((SUB, LANES), jnp.float32)
    here = pl.ds(SUB * r, SUB)
    k = K[zz, c, here, :]
    rest = [k + v for v in cross(K, zz, c, r, rows, k, sub, zero)]
    return (WL[zz, c, here, :], WR[zz, c, here, :], *rest)


def six(parts):
    a, b, c, d, e, f = parts
    return ((a + b) + (c + d)) + (e + f)


def weighted(weights, parts):
    return six([w * v for w, v in zip(weights, parts)])


def sweeps(refs, ranges, inside, press):
    K, P0, SRC, OBS, P1, P2, U1, U2, U3, HR, SR, NP0, WL, WR, G, E = refs
    tiles, rows = K.shape[1], K.shape[2] // SUB

    def at(r):
        return pl.ds(SUB * r, SUB)

    def coefficients(zz):
        valid = 0.5 * inside(zz)
        for r in range(rows):
            k, kn = around(K, zz, r, rows)
            for c in range(tiles):
                w = [k[c] + v for v in kn[c]]
                HR[zz, c, at(r), :] = valid / (0.5 + 0.5 * six(w))
                WL[zz, c, at(r), :] = w[0]
                WR[zz, c, at(r), :] = w[1]

    def first(zz):
        for r in range(rows):
            _, pn = around(P0, zz, r, rows)
            for c in range(tiles):
                w = faces(K, WL, WR, zz, c, r, rows)
                hr = HR[zz, c, at(r), :]
                rinv = hr + hr
                sr = SRC[zz, c, at(r), :] * rinv
                SR[zz, c, at(r), :] = sr
                NP0[zz, c, at(r), :] = six(pn[c])
                P1[zz, c, at(r), :] = sr + weighted(w, pn[c]) * hr
                U3[zz, c, at(r), :] = OBS[zz, c, at(r), :] * rinv

    def second(zz):
        for r in range(rows):
            _, a = around(P1, zz, r, rows)
            _, v = around(U3, zz, r, rows)
            for c in range(tiles):
                w = faces(K, WL, WR, zz, c, r, rows)
                hr = HR[zz, c, at(r), :]
                p2 = SR[zz, c, at(r), :] + weighted(w, a[c]) * hr
                u2 = weighted(w, v[c]) * hr
                P2[zz, c, at(r), :] = p2
                U2[zz, c, at(r), :] = u2
                G[zz, c, at(r), :] = u2 * six(a[c]) + p2 * six(v[c])

    def third(zz, own):
        for r in range(rows):
            p2, a = around(P2, zz, r, rows)
            u2, v = around(U2, zz, r, rows)
            for c in range(tiles):
                w = faces(K, WL, WR, zz, c, r, rows)
                hr = HR[zz, c, at(r), :]
                p1, u3 = P1[zz, c, at(r), :], U3[zz, c, at(r), :]
                p3 = SR[zz, c, at(r), :] + weighted(w, a[c]) * hr
                u1 = weighted(w, v[c]) * hr
                e = -(u1 * p1 + u2[c] * p2[c] + u3 * p3)
                U1[zz, c, at(r + 1), :] = u1
                E[zz, c, at(r + 1), :] = e
                if own:
                    g = u3 * six(a[c]) + p1 * six(v[c]) + u1 * NP0[zz, c, at(r), :]
                    press(zz)[at(r), pl.ds(c * LANES, LANES)] = p3
                    G[zz, c, at(r), :] = (G[zz, c, at(r), :] + 6.0 * e) + g

    for body, spans in zip((coefficients, first, second, third), ranges):
        for span in spans:
            lo, hi, *own = span
            lax.fori_loop(lo, hi, lambda zz, _, body=body, own=own: body(zz, *own) or 0, 0)


def first_kernel(log_perm, noise, p0, src, obs, K, up, down, means, draws, sems):
    slab, nx, ny = log_perm.shape
    tiles, half = ny // LANES, nx // 2
    rows = pl.ds(pl.multiple_of(half * (lax.axis_index("draw") % 2), half), half)
    copies = []

    def copy(src_ref, dst_ref):
        copies.append(pltpu.make_async_copy(src_ref, dst_ref, sems.at[len(copies)]))

    copy(log_perm, means)
    copy(noise, draws)
    for c in range(tiles):
        cols = pl.ds(c * LANES, LANES)
        at = 0
        for ref, width in ((p0, HALO), (src, SWEEPS), (obs, SWEEPS)):
            for start, out in ((slab - width, up), (0, down)):
                copy(ref.at[pl.ds(start, width), rows, cols], out.at[pl.ds(at, width), c])
            at += width
    for cp in copies:
        cp.start()
    for cp in copies[:2]:
        cp.wait()

    def plane(z, _, out=None, first=0):
        for r in range(nx // SUB):
            for c in range(tiles):
                here, cols = pl.ds(SUB * r, SUB), pl.ds(c * LANES, LANES)
                k = jnp.exp(means[z, here, cols] + draws[z, here, cols])
                K[z + HALO, c, here, :] = k
                if out is not None:
                    part, at = divmod(SUB * r, half)
                    out[EDGE + part * HALO + z - first, c, pl.ds(at, SUB), :] = k
        return 0

    low, high = functools.partial(plane, out=down), functools.partial(plane, out=up, first=slab - HALO)
    lax.fori_loop(0, HALO, low, 0)
    lax.fori_loop(HALO, slab - HALO, plane, 0)
    lax.fori_loop(slab - HALO, slab, high, 0)
    for cp in copies[2:]:
        cp.wait()


def inner_kernel(K, p0, src, obs, P0, SRC, OBS, P1, P2, U1, U2, U3, HR, SR, NP0, WL, WR, G, E, mid, sems):
    slab = p0.shape[0]
    top = HALO + slab
    copies = []
    for c in range(K.shape[1]):
        for ref, out in ((p0, P0), (src, SRC), (obs, OBS)):
            copies.append(
                pltpu.make_async_copy(
                    ref.at[:, :, pl.ds(c * LANES, LANES)], out.at[pl.ds(HALO, slab), c], sems.at[len(copies)]
                )
            )
    for cp in copies:
        cp.start()
    for cp in copies:
        cp.wait()
    rim = jnp.zeros((SUB, LANES), jnp.float32)

    def clear(zz, _):
        for ref in (U1, E):
            for c in range(ref.shape[1]):
                ref[zz, c, pl.ds(0, SUB), :] = rim
                ref[zz, c, pl.ds(ref.shape[2] - SUB, SUB), :] = rim
        return 0

    lax.fori_loop(HALO, top, clear, 0)
    refs = (K, P0, SRC, OBS, P1, P2, U1, U2, U3, HR, SR, NP0, WL, WR, G, E)
    ranges = [[(HALO + n, top - n)] for n in (1, 1, 2)] + [[(HALO + 3, top - 3, True)]]
    sweeps(refs, ranges, lambda zz: jnp.float32(1.0), lambda zz: mid.at[zz - HALO - SWEEPS])


def side_kernel(low, stages, parts, *args):
    halos = args[: len(args) - 2 * FIELDS - (3 in stages) - len(parts) - 1]
    refs = args[len(halos) + FIELDS : len(halos) + 2 * FIELDS]
    ends, sems = args[len(halos) + 2 * FIELDS : -1], args[-1]
    K, P0, SRC, OBS = refs[:4]
    nx, depth = K.shape[2], K.shape[0]
    half, top = nx // 2, depth - HALO
    par = lax.axis_index("draw") % 2

    pairs = []
    if 0 in stages:
        for h in range(2):
            rows = pl.ds(h * half, half)
            pairs.append((halos[0].at[pl.ds(EDGE + h * HALO, HALO)], K.at[pl.ds(0 if low else top, HALO), :, rows]))
    if 1 in stages:
        for half_rows, which in zip(halos[-2:], (par, 1 - par)):
            rows = pl.ds(pl.multiple_of(half * which, half), half)
            first = 0
            for field, width in ((P0, HALO), (SRC, SWEEPS), (OBS, SWEEPS)):
                planes = pl.ds(HALO - width if low else top, width)
                pairs.append((half_rows.at[pl.ds(first, width)], field.at[planes, :, rows]))
                first += width
    copies = [pltpu.make_async_copy(a, b, sems.at[i]) for i, (a, b) in enumerate(pairs)]
    for cp in copies:
        cp.start()
    for cp in copies:
        cp.wait()

    space, spaces = lax.axis_index("space"), lax.axis_size("space")
    met = jnp.where(space > 0 if low else space + 1 < spaces, 1.0, 0.0).astype(jnp.float32)
    if low:
        near, last, shift = (1, HALO + 1), [(3, HALO, False), (HALO, HALO + 3, True)], HALO
        ranges = [[near], [near], [(2, HALO + 2)], last]
    else:
        near, last, shift = (top - 1, depth - 1), [(top - 3, top, True), (top, depth - 3, False)], top - 3
        ranges = [[near], [near], [(top - 2, depth - 2)], last]

    def inside(zz):
        return jnp.where(zz < HALO if low else zz >= top, met, jnp.float32(1.0))

    ranges = [spans if n in stages else [] for n, spans in enumerate(ranges)]
    sweeps(refs, ranges, inside, lambda zz: ends[0].at[zz - shift])
    gradients(refs, [(out, *part) for out, part in zip(ends[len(ends) - len(parts) :], parts)])


def gradients(fields, parts):
    K, P0, U1, G, E = fields[0], fields[1], fields[6], fields[-2], fields[-1]
    tiles, nx = K.shape[1], K.shape[2]
    draw, draws = lax.axis_index("draw"), lax.axis_size("draw")
    block, groups = nx // draws, draws // 2
    count = block // SUB

    for out, own, first, z0 in parts:
        parity = draw % 2 if own else 1 - draw % 2

        def plane(z, _, out=out, first=first, z0=z0, parity=parity):
            zz = z + z0 + HALO
            for s in range(out.shape[0]):
                base = (2 * ((draw // 2 + first + s) % groups) + parity) * block
                start = pl.multiple_of(base, SUB)
                v = around_padded(U1, zz, start + SUB, count)
                w = around_padded(E, zz, start + SUB, count)
                for q in range(count):
                    at = pl.ds(pl.multiple_of(start + SUB * q, SUB), SUB)
                    for c in range(tiles):
                        g = G[zz, c, at, :] + P0[zz, c, at, :] * six(v[q][c]) + six(w[q][c])
                        out[s, z, pl.ds(SUB * q, SUB), pl.ds(c * LANES, LANES)] = 0.5 * K[zz, c, at, :] * g
            return 0

        lax.fori_loop(0, out.shape[1], plane, 0)


def far_kernel(z0, *args):
    gradients(args[:FIELDS], [(args[FIELDS], True, 1, z0)])


def rest_kernel(*args):
    pieces, fields = args[:3], args[3 : 3 + FIELDS]
    press, keep, sems = args[3 + FIELDS :]
    copies, at = [], 0
    for ref in pieces:
        copies.append(pltpu.make_async_copy(ref, press.at[pl.ds(at, ref.shape[0])], sems.at[len(copies)]))
        at += ref.shape[0]
    for cp in copies:
        cp.start()
    gradients(fields, [(keep, True, 0, 0)])
    for cp in copies:
        cp.wait()


def local(log_perm, noise, source, start_pressure, observe):
    draws, spaces = lax.axis_size("draw"), lax.axis_size("space")
    slab, nx, ny = log_perm.shape
    tiles, depth, half = ny // LANES, slab + 2 * HALO, nx // 2
    up = [(i, i + 1) for i in range(spaces - 1)]
    down = [(j, i) for i, j in up]
    pair = [(i, i ^ 1) for i in range(draws)]
    f32 = jnp.float32
    field = pltpu.VMEM((depth, tiles, nx, LANES), f32)
    padded = pltpu.VMEM((depth, tiles, nx + 2 * SUB, LANES), f32)
    kinds = [field] * 6 + [padded] + [field] * 8 + [padded]
    edge = jax.ShapeDtypeStruct((EDGE + 2 * HALO, tiles, half, LANES), f32)
    whole = jax.ShapeDtypeStruct((slab, nx, ny), f32)
    mid = jax.ShapeDtypeStruct((slab - 2 * SWEEPS, nx, ny), f32)
    groups = draws // 2
    cut = slab // 2
    near = jax.ShapeDtypeStruct((1, slab, nx // draws, ny), f32)
    params = pltpu.CompilerParams(vmem_limit_bytes=8 * 2**20)
    cells = slab * nx * ny

    inputs = (log_perm, noise[0], start_pressure, source, observe)
    K, to_up, to_down = pl.pallas_call(
        first_kernel,
        out_shape=(field, edge, edge),
        in_specs=[OFFCHIP] * 5,
        out_specs=(ONCHIP,) * 3,
        scratch_shapes=[pltpu.VMEM((slab, nx, ny), f32)] * 2 + [pltpu.SemaphoreType.DMA((2 + 6 * tiles,))],
        compiler_params=params,
        cost_estimate=pl.CostEstimate(flops=cells, bytes_accessed=20 * cells, transcendentals=cells),
    )(*[pltpu.with_memory_space_constraint(a, pltpu.HBM) for a in inputs])
    alo = lax.ppermute(to_up, "space", up)
    ahi = lax.ppermute(to_down, "space", down)
    state = pl.pallas_call(
        inner_kernel,
        out_shape=(*kinds[1:], mid),
        in_specs=[ONCHIP] + [ANYWHERE] * 3,
        out_specs=(ONCHIP,) * 16,
        scratch_shapes=[pltpu.SemaphoreType.DMA((3 * tiles,))],
        compiler_params=params,
        cost_estimate=pl.CostEstimate(flops=200 * cells, bytes_accessed=60 * cells, transcendentals=0),
    )(K, start_pressure, source, observe)
    fields, centre = (K, *state[:-1]), state[-1]

    def blocks(count, planes):
        return jax.ShapeDtypeStruct((count, planes, nx // draws, ny), f32)

    def side(low, stages, halos, fields, parts=()):
        ends = (jax.ShapeDtypeStruct((SWEEPS, nx, ny), f32),) if 3 in stages else ()
        ends += tuple(blocks(groups - 1 if first else 1, planes) for _, first, _, planes in parts)
        n = len(halos)
        out = pl.pallas_call(
            functools.partial(side_kernel, low, stages, [part[:-1] for part in parts]),
            out_shape=(*kinds, *ends),
            in_specs=[ONCHIP] * (n + FIELDS),
            out_specs=(ONCHIP,) * (FIELDS + len(ends)),
            scratch_shapes=[pltpu.SemaphoreType.DMA((8,))],
            input_output_aliases={n + i: i for i in range(FIELDS)},
            compiler_params=params,
            cost_estimate=pl.CostEstimate(flops=30 * len(stages) * cells, bytes_accessed=10 * cells, transcendentals=0),
        )(*halos, *fields)
        return out[:FIELDS], *out[FIELDS:]

    def swapped(got, fields):
        got, last = lax.optimization_barrier((got, fields[-1]))
        return got, lax.ppermute(got[:EDGE], "draw", pair), (*fields[:-1], last)

    def onward(keep, got):
        return [
            lax.ppermute(keep[s - 1] + got[s - 1], "draw", [(j, (j + 2 * s) % draws) for j in range(draws)])
            for s in range(1, groups)
        ]

    def swap(send):
        return lax.ppermute(send, "draw", pair)

    def keep_far(z0, planes, fields):
        return pl.pallas_call(
            functools.partial(far_kernel, z0),
            out_shape=blocks(groups - 1, planes),
            in_specs=[ONCHIP] * FIELDS,
            out_specs=ONCHIP,
            compiler_params=params,
            cost_estimate=pl.CostEstimate(flops=10 * cells, bytes_accessed=10 * cells, transcendentals=0),
        )(*fields)

    mine, theirs, fields = swapped(alo, fields)
    (fields,) = side(True, (0,), (mine,), fields)
    (fields,) = side(True, (1,), (mine, theirs), fields)
    mine, theirs, fields = swapped(ahi, fields)
    parts = [(False, 1, 0, cut), (False, 0, 0, cut), (True, 1, 0, cut)]
    fields, low, send_far, send_near, keep = side(True, (2, 3), (), fields, parts)
    got_far, near_low = swap(send_far), swap(send_near)
    (fields,) = side(False, (0, 1), (mine, mine, theirs), fields)
    got_far, last = lax.optimization_barrier((got_far, fields[-1]))
    moved_low = onward(keep, got_far)
    parts = [(False, 1, cut, cut // 2), (False, 1, cut + cut // 2, slab - cut - cut // 2), (False, 0, cut, slab - cut)]
    fields, high, *send_far, send_near = side(False, (2, 3), (), (*fields[:-1], last), parts)
    got_far, near_high = [swap(a) for a in send_far], swap(send_near)
    moved_low, last = lax.optimization_barrier((moved_low, fields[-1]))
    fields = (*fields[:-1], last)
    keep = keep_far(cut, slab - cut, fields)
    sums = [keep[s - 1] + jnp.concatenate([a[s - 1] for a in got_far], axis=0) for s in range(1, groups)]
    sums, last = lax.optimization_barrier((sums, fields[-1]))
    fields = (*fields[:-1], last)
    moved_high = [
        lax.ppermute(a, "draw", [(j, (j + 2 * s) % draws) for j in range(draws)]) for s, a in enumerate(sums, 1)
    ]
    press, keep = pl.pallas_call(
        rest_kernel,
        out_shape=(whole, near),
        in_specs=[ONCHIP] * (3 + FIELDS),
        out_specs=(OFFCHIP, ONCHIP),
        scratch_shapes=[pltpu.SemaphoreType.DMA((3,))],
        compiler_params=params,
        cost_estimate=pl.CostEstimate(flops=30 * cells, bytes_accessed=30 * cells, transcendentals=0),
    )(low, centre, high, *fields)
    total = keep[0] + jnp.concatenate([near_low[0], near_high[0]], axis=0)
    for a, b in zip(moved_low, moved_high):
        total = total + jnp.concatenate([a, b], axis=0)
    return press[None], total


def solution(mesh):
    return jax.shard_map(
        local,
        mesh=mesh,
        in_specs=(
            P(("epi", "space"), None, None),
            P("draw", ("epi", "space"), None, None),
            P(("epi", "space"), None, None),
            P(("epi", "space"), None, None),
            P(("epi", "space"), None, None),
        ),
        out_specs=(P("draw", ("epi", "space"), None, None), P(("epi", "space"), "draw", None)),
        check_vma=False,
    )
```

```python
import functools

import jax
import jax.numpy as jnp
from jax import lax
from jax.experimental import pallas as pl
from jax.experimental.pallas import tpu as pltpu
from jax.sharding import PartitionSpec as P

SWEEPS = 3
HALO = SWEEPS + 1
EDGE = HALO + 2 * SWEEPS
FIELDS = 16
LANES = 128
SUB = 8
ANYWHERE = pl.BlockSpec(memory_space=pl.ANY)
OFFCHIP = pl.BlockSpec(memory_space=pltpu.HBM)
ONCHIP = pl.BlockSpec(memory_space=pltpu.VMEM)


def lane_shifts(own):
    lane = lax.broadcasted_iota(jnp.int32, (SUB, LANES), 1)
    zero = jnp.zeros((SUB, LANES), jnp.float32)
    fwd = [zero] + [pltpu.roll(v, 1, 1) for v in own]
    bwd = [pltpu.roll(v, LANES - 1, 1) for v in own] + [zero]
    return [
        (jnp.where(lane == 0, fwd[c], fwd[c + 1]), jnp.where(lane == LANES - 1, bwd[c + 1], bwd[c]))
        for c in range(len(own))
    ]


def around(ref, zz, r, rows):
    sub = lax.broadcasted_iota(jnp.int32, (SUB, LANES), 0)
    zero = jnp.zeros((SUB, LANES), jnp.float32)
    own = [ref[zz, c, pl.ds(SUB * r, SUB), :] for c in range(ref.shape[1])]
    sides = lane_shifts(own)
    return own, [sides[c] + cross(ref, zz, c, r, rows, own[c], sub, zero) for c in range(len(own))]


def around_padded(ref, zz, start, count):
    sub = lax.broadcasted_iota(jnp.int32, (SUB, LANES), 0)
    groups = [pl.ds(pl.multiple_of(start + SUB * (q - 1), SUB), SUB) for q in range(count + 2)]
    tiles = ref.shape[1]
    own = [[ref[zz, c, g, :] for c in range(tiles)] for g in groups]
    down = [[pltpu.roll(v, 1, 0) for v in line] for line in own[:-1]]
    up = [[pltpu.roll(v, SUB - 1, 0) for v in line] for line in own[1:]]
    out = []
    for q in range(1, count + 1):
        sides = lane_shifts(own[q])
        line = []
        for c in range(tiles):
            north = jnp.where(sub == 0, down[q - 1][c], down[q][c])
            south = jnp.where(sub == SUB - 1, up[q][c], up[q - 1][c])
            line.append(sides[c] + (north, south, ref[zz - 1, c, groups[q], :], ref[zz + 1, c, groups[q], :]))
        out.append(line)
    return out


def cross(ref, zz, c, r, rows, own, sub, zero):
    if r > 0:
        north = ref[zz, c, pl.ds(SUB * r - 1, SUB), :]
    else:
        north = jnp.where(sub == 0, zero, pltpu.roll(own, 1, 0))
    if r + 1 < rows:
        south = ref[zz, c, pl.ds(SUB * r + 1, SUB), :]
    else:
        south = jnp.where(sub == SUB - 1, zero, pltpu.roll(own, SUB - 1, 0))
    here = pl.ds(SUB * r, SUB)
    return north, south, ref[zz - 1, c, here, :], ref[zz + 1, c, here, :]


def faces(K, WL, WR, zz, c, r, rows):
    sub = lax.broadcasted_iota(jnp.int32, (SUB, LANES), 0)
    zero = jnp.zeros((SUB, LANES), jnp.float32)
    here = pl.ds(SUB * r, SUB)
    k = K[zz, c, here, :]
    rest = [k + v for v in cross(K, zz, c, r, rows, k, sub, zero)]
    return (WL[zz, c, here, :], WR[zz, c, here, :], *rest)


def six(parts):
    a, b, c, d, e, f = parts
    return ((a + b) + (c + d)) + (e + f)


def weighted(weights, parts):
    return six([w * v for w, v in zip(weights, parts)])


def sweeps(refs, ranges, inside, press):
    K, P0, SRC, OBS, P1, P2, U1, U2, U3, HR, SR, NP0, WL, WR, G, E = refs
    tiles, rows = K.shape[1], K.shape[2] // SUB

    def at(r):
        return pl.ds(SUB * r, SUB)

    def coefficients(zz):
        valid = 0.5 * inside(zz)
        for r in range(rows):
            k, kn = around(K, zz, r, rows)
            for c in range(tiles):
                w = [k[c] + v for v in kn[c]]
                HR[zz, c, at(r), :] = valid / (0.5 + 0.5 * six(w))
                WL[zz, c, at(r), :] = w[0]
                WR[zz, c, at(r), :] = w[1]

    def first(zz):
        for r in range(rows):
            _, pn = around(P0, zz, r, rows)
            for c in range(tiles):
                w = faces(K, WL, WR, zz, c, r, rows)
                hr = HR[zz, c, at(r), :]
                rinv = hr + hr
                sr = SRC[zz, c, at(r), :] * rinv
                SR[zz, c, at(r), :] = sr
                NP0[zz, c, at(r), :] = six(pn[c])
                P1[zz, c, at(r), :] = sr + weighted(w, pn[c]) * hr
                U3[zz, c, at(r), :] = OBS[zz, c, at(r), :] * rinv

    def combined(zz):
        valid = inside(zz)
        for r in range(rows):
            k, kn = around(K, zz, r, rows)
            _, pn = around(P0, zz, r, rows)
            for c in range(tiles):
                w = [k[c] + v for v in kn[c]]
                rinv = valid / (0.5 + 0.5 * six(w))
                hr = 0.5 * rinv
                sr = SRC[zz, c, at(r), :] * rinv
                HR[zz, c, at(r), :] = hr
                SR[zz, c, at(r), :] = sr
                WL[zz, c, at(r), :] = w[0]
                WR[zz, c, at(r), :] = w[1]
                NP0[zz, c, at(r), :] = six(pn[c])
                P1[zz, c, at(r), :] = sr + weighted(w, pn[c]) * hr
                U3[zz, c, at(r), :] = OBS[zz, c, at(r), :] * rinv

    def second(zz):
        for r in range(rows):
            _, a = around(P1, zz, r, rows)
            _, v = around(U3, zz, r, rows)
            for c in range(tiles):
                w = faces(K, WL, WR, zz, c, r, rows)
                hr = HR[zz, c, at(r), :]
                p2 = SR[zz, c, at(r), :] + weighted(w, a[c]) * hr
                u2 = weighted(w, v[c]) * hr
                P2[zz, c, at(r), :] = p2
                U2[zz, c, at(r), :] = u2
                G[zz, c, at(r), :] = u2 * six(a[c]) + p2 * six(v[c])

    def third(zz, own):
        for r in range(rows):
            p2, a = around(P2, zz, r, rows)
            u2, v = around(U2, zz, r, rows)
            for c in range(tiles):
                w = faces(K, WL, WR, zz, c, r, rows)
                hr = HR[zz, c, at(r), :]
                p1, u3 = P1[zz, c, at(r), :], U3[zz, c, at(r), :]
                p3 = SR[zz, c, at(r), :] + weighted(w, a[c]) * hr
                u1 = weighted(w, v[c]) * hr
                e = -(u1 * p1 + u2[c] * p2[c] + u3 * p3)
                U1[zz, c, at(r + 1), :] = u1
                E[zz, c, at(r + 1), :] = e
                if own:
                    g = u3 * six(a[c]) + p1 * six(v[c]) + u1 * NP0[zz, c, at(r), :]
                    press(zz)[at(r), pl.ds(c * LANES, LANES)] = p3
                    G[zz, c, at(r), :] = (G[zz, c, at(r), :] + 6.0 * e) + g

    stages = [coefficients, first, second, third]
    if ranges[0] and ranges[0] == ranges[1]:
        stages, ranges = [combined, second, third], ranges[1:]
    for body, spans in zip(stages, ranges):
        for span in spans:
            lo, hi, *own = span
            lax.fori_loop(lo, hi, lambda zz, _, body=body, own=own: body(zz, *own) or 0, 0)


def first_kernel(log_perm, noise, p0, src, obs, K, up, down, means, draws, sems):
    slab, nx, ny = log_perm.shape
    tiles, half = ny // LANES, nx // 2
    rows = pl.ds(pl.multiple_of(half * (lax.axis_index("draw") % 2), half), half)
    copies = []

    def copy(src_ref, dst_ref):
        copies.append(pltpu.make_async_copy(src_ref, dst_ref, sems.at[len(copies)]))

    copy(log_perm, means)
    copy(noise, draws)
    for c in range(tiles):
        cols = pl.ds(c * LANES, LANES)
        at = 0
        for ref, width in ((p0, HALO), (src, SWEEPS), (obs, SWEEPS)):
            for start, out in ((slab - width, up), (0, down)):
                copy(ref.at[pl.ds(start, width), rows, cols], out.at[pl.ds(at, width), c])
            at += width
    for cp in copies:
        cp.start()
    for cp in copies[:2]:
        cp.wait()

    def plane(z, _, out=None, first=0):
        for r in range(nx // SUB):
            for c in range(tiles):
                here, cols = pl.ds(SUB * r, SUB), pl.ds(c * LANES, LANES)
                k = jnp.exp(means[z, here, cols] + draws[z, here, cols])
                K[z + HALO, c, here, :] = k
                if out is not None:
                    part, at = divmod(SUB * r, half)
                    out[EDGE + part * HALO + z - first, c, pl.ds(at, SUB), :] = k
        return 0

    low, high = functools.partial(plane, out=down), functools.partial(plane, out=up, first=slab - HALO)
    lax.fori_loop(0, HALO, low, 0)
    lax.fori_loop(HALO, slab - HALO, plane, 0)
    lax.fori_loop(slab - HALO, slab, high, 0)
    for cp in copies[2:]:
        cp.wait()


def inner_kernel(K, p0, src, obs, P0, SRC, OBS, P1, P2, U1, U2, U3, HR, SR, NP0, WL, WR, G, E, mid, sems):
    slab = p0.shape[0]
    top = HALO + slab
    copies = []
    for c in range(K.shape[1]):
        for ref, out in ((p0, P0), (src, SRC), (obs, OBS)):
            copies.append(
                pltpu.make_async_copy(
                    ref.at[:, :, pl.ds(c * LANES, LANES)], out.at[pl.ds(HALO, slab), c], sems.at[len(copies)]
                )
            )
    for cp in copies:
        cp.start()
    for cp in copies:
        cp.wait()
    rim = jnp.zeros((SUB, LANES), jnp.float32)

    def clear(zz, _):
        for ref in (U1, E):
            for c in range(ref.shape[1]):
                ref[zz, c, pl.ds(0, SUB), :] = rim
                ref[zz, c, pl.ds(ref.shape[2] - SUB, SUB), :] = rim
        return 0

    lax.fori_loop(HALO, top, clear, 0)
    refs = (K, P0, SRC, OBS, P1, P2, U1, U2, U3, HR, SR, NP0, WL, WR, G, E)
    ranges = [[(HALO + n, top - n)] for n in (1, 1, 2)] + [[(HALO + 3, top - 3, True)]]
    sweeps(refs, ranges, lambda zz: jnp.float32(1.0), lambda zz: mid.at[zz - HALO - SWEEPS])


def side_kernel(low, stages, parts, *args):
    halos = args[: len(args) - 2 * FIELDS - (3 in stages) - len(parts) - 1]
    refs = args[len(halos) + FIELDS : len(halos) + 2 * FIELDS]
    ends, sems = args[len(halos) + 2 * FIELDS : -1], args[-1]
    K, P0, SRC, OBS = refs[:4]
    nx, depth = K.shape[2], K.shape[0]
    half, top = nx // 2, depth - HALO
    par = lax.axis_index("draw") % 2

    pairs = []
    if 0 in stages:
        for h in range(2):
            rows = pl.ds(h * half, half)
            pairs.append((halos[0].at[pl.ds(EDGE + h * HALO, HALO)], K.at[pl.ds(0 if low else top, HALO), :, rows]))
    if 1 in stages:
        for half_rows, which in zip(halos[-2:], (par, 1 - par)):
            rows = pl.ds(pl.multiple_of(half * which, half), half)
            first = 0
            for field, width in ((P0, HALO), (SRC, SWEEPS), (OBS, SWEEPS)):
                planes = pl.ds(HALO - width if low else top, width)
                pairs.append((half_rows.at[pl.ds(first, width)], field.at[planes, :, rows]))
                first += width
    copies = [pltpu.make_async_copy(a, b, sems.at[i]) for i, (a, b) in enumerate(pairs)]
    for cp in copies:
        cp.start()
    for cp in copies:
        cp.wait()

    space, spaces = lax.axis_index("space"), lax.axis_size("space")
    met = jnp.where(space > 0 if low else space + 1 < spaces, 1.0, 0.0).astype(jnp.float32)
    if low:
        near, last, shift = (1, HALO + 1), [(3, HALO, False), (HALO, HALO + 3, True)], HALO
        ranges = [[near], [near], [(2, HALO + 2)], last]
    else:
        near, last, shift = (top - 1, depth - 1), [(top - 3, top, True), (top, depth - 3, False)], top - 3
        ranges = [[near], [near], [(top - 2, depth - 2)], last]

    def inside(zz):
        return jnp.where(zz < HALO if low else zz >= top, met, jnp.float32(1.0))

    ranges = [spans if n in stages else [] for n, spans in enumerate(ranges)]
    sweeps(refs, ranges, inside, lambda zz: ends[0].at[zz - shift])
    gradients(refs, [(out, *part) for out, part in zip(ends[len(ends) - len(parts) :], parts)])


def gradients(fields, parts):
    K, P0, U1, G, E = fields[0], fields[1], fields[6], fields[-2], fields[-1]
    tiles, nx = K.shape[1], K.shape[2]
    draw, draws = lax.axis_index("draw"), lax.axis_size("draw")
    block, groups = nx // draws, draws // 2
    count = block // SUB

    for out, own, first, z0 in parts:
        parity = draw % 2 if own else 1 - draw % 2
        for s in range(out.shape[0]):
            base = (2 * ((draw // 2 + first + s) % groups) + parity) * block
            start = pl.multiple_of(base, SUB)
            for z in range(out.shape[1]):
                zz = z + z0 + HALO
                v = around_padded(U1, zz, start + SUB, count)
                w = around_padded(E, zz, start + SUB, count)
                for q in range(count):
                    at = pl.ds(pl.multiple_of(start + SUB * q, SUB), SUB)
                    for c in range(tiles):
                        g = G[zz, c, at, :] + P0[zz, c, at, :] * six(v[q][c]) + six(w[q][c])
                        out[s, z, pl.ds(SUB * q, SUB), pl.ds(c * LANES, LANES)] = 0.5 * K[zz, c, at, :] * g


def far_kernel(z0, *args):
    gradients(args[:FIELDS], [(args[FIELDS], True, 1, z0)])


def rest_kernel(*args):
    pieces, fields = args[:3], args[3 : 3 + FIELDS]
    press, keep, sems = args[3 + FIELDS :]
    copies, at = [], 0
    for ref in pieces:
        copies.append(pltpu.make_async_copy(ref, press.at[pl.ds(at, ref.shape[0])], sems.at[len(copies)]))
        at += ref.shape[0]
    for cp in copies:
        cp.start()
    gradients(fields, [(keep, True, 0, 0)])
    for cp in copies:
        cp.wait()


def local(log_perm, noise, source, start_pressure, observe):
    draws, spaces = lax.axis_size("draw"), lax.axis_size("space")
    slab, nx, ny = log_perm.shape
    tiles, depth, half = ny // LANES, slab + 2 * HALO, nx // 2
    up = [(i, i + 1) for i in range(spaces - 1)]
    down = [(j, i) for i, j in up]
    pair = [(i, i ^ 1) for i in range(draws)]
    f32 = jnp.float32
    field = pltpu.VMEM((depth, tiles, nx, LANES), f32)
    padded = pltpu.VMEM((depth, tiles, nx + 2 * SUB, LANES), f32)
    kinds = [field] * 6 + [padded] + [field] * 8 + [padded]
    edge = jax.ShapeDtypeStruct((EDGE + 2 * HALO, tiles, half, LANES), f32)
    whole = jax.ShapeDtypeStruct((slab, nx, ny), f32)
    mid = jax.ShapeDtypeStruct((slab - 2 * SWEEPS, nx, ny), f32)
    groups = draws // 2
    cut = slab // 2
    near = jax.ShapeDtypeStruct((1, slab, nx // draws, ny), f32)
    params = pltpu.CompilerParams(vmem_limit_bytes=8 * 2**20)
    cells = slab * nx * ny

    inputs = (log_perm, noise[0], start_pressure, source, observe)
    K, to_up, to_down = pl.pallas_call(
        first_kernel,
        out_shape=(field, edge, edge),
        in_specs=[OFFCHIP] * 5,
        out_specs=(ONCHIP,) * 3,
        scratch_shapes=[pltpu.VMEM((slab, nx, ny), f32)] * 2 + [pltpu.SemaphoreType.DMA((2 + 6 * tiles,))],
        compiler_params=params,
        cost_estimate=pl.CostEstimate(flops=cells, bytes_accessed=20 * cells, transcendentals=cells),
    )(*[pltpu.with_memory_space_constraint(a, pltpu.HBM) for a in inputs])
    alo = lax.ppermute(to_up, "space", up)
    ahi = lax.ppermute(to_down, "space", down)
    state = pl.pallas_call(
        inner_kernel,
        out_shape=(*kinds[1:], mid),
        in_specs=[ONCHIP] + [ANYWHERE] * 3,
        out_specs=(ONCHIP,) * 16,
        scratch_shapes=[pltpu.SemaphoreType.DMA((3 * tiles,))],
        compiler_params=params,
        cost_estimate=pl.CostEstimate(flops=200 * cells, bytes_accessed=60 * cells, transcendentals=0),
    )(K, start_pressure, source, observe)
    fields, centre = (K, *state[:-1]), state[-1]

    def blocks(count, planes):
        return jax.ShapeDtypeStruct((count, planes, nx // draws, ny), f32)

    def side(low, stages, halos, fields, parts=()):
        ends = (jax.ShapeDtypeStruct((SWEEPS, nx, ny), f32),) if 3 in stages else ()
        ends += tuple(blocks(groups - 1 if first else 1, planes) for _, first, _, planes in parts)
        n = len(halos)
        out = pl.pallas_call(
            functools.partial(side_kernel, low, stages, [part[:-1] for part in parts]),
            out_shape=(*kinds, *ends),
            in_specs=[ONCHIP] * (n + FIELDS),
            out_specs=(ONCHIP,) * (FIELDS + len(ends)),
            scratch_shapes=[pltpu.SemaphoreType.DMA((8,))],
            input_output_aliases={n + i: i for i in range(FIELDS)},
            compiler_params=params,
            cost_estimate=pl.CostEstimate(flops=30 * len(stages) * cells, bytes_accessed=10 * cells, transcendentals=0),
        )(*halos, *fields)
        return out[:FIELDS], *out[FIELDS:]

    def swapped(got, fields):
        got, last = lax.optimization_barrier((got, fields[-1]))
        return got, lax.ppermute(got[:EDGE], "draw", pair), (*fields[:-1], last)

    def onward(keep, got):
        return [
            lax.ppermute(keep[s - 1] + got[s - 1], "draw", [(j, (j + 2 * s) % draws) for j in range(draws)])
            for s in range(1, groups)
        ]

    def swap(send):
        return lax.ppermute(send, "draw", pair)

    def keep_far(z0, planes, fields):
        return pl.pallas_call(
            functools.partial(far_kernel, z0),
            out_shape=blocks(groups - 1, planes),
            in_specs=[ONCHIP] * FIELDS,
            out_specs=ONCHIP,
            compiler_params=params,
            cost_estimate=pl.CostEstimate(flops=10 * cells, bytes_accessed=10 * cells, transcendentals=0),
        )(*fields)

    mine, theirs, fields = swapped(alo, fields)
    (fields,) = side(True, (0,), (mine,), fields)
    (fields,) = side(True, (1,), (mine, theirs), fields)
    (fields,) = side(True, (2,), (), fields)
    mine, theirs, fields = swapped(ahi, fields)
    parts = [(False, 1, 0, cut), (False, 0, 0, cut), (True, 1, 0, cut)]
    fields, low, send_far, send_near, keep = side(True, (3,), (), fields, parts)
    got_far, near_low = swap(send_far), swap(send_near)
    (fields,) = side(False, (0, 1), (mine, mine, theirs), fields)
    got_far, near_low, last = lax.optimization_barrier((got_far, near_low, fields[-1]))
    moved_low = onward(keep, got_far)
    parts = [(False, 1, cut, slab - cut), (False, 0, cut, slab - cut)]
    fields, high, send_far, send_near = side(False, (2, 3), (), (*fields[:-1], last), parts)
    got_far, near_high = swap(send_far), swap(send_near)
    moved_low, last = lax.optimization_barrier((moved_low, fields[-1]))
    fields = (*fields[:-1], last)
    keep = keep_far(cut, slab - cut, fields)
    sums = [keep[s - 1] + got_far[s - 1] for s in range(1, groups)]
    sums, last = lax.optimization_barrier((sums, fields[-1]))
    fields = (*fields[:-1], last)
    moved_high = [
        lax.ppermute(a, "draw", [(j, (j + 2 * s) % draws) for j in range(draws)]) for s, a in enumerate(sums, 1)
    ]
    press, keep = pl.pallas_call(
        rest_kernel,
        out_shape=(whole, near),
        in_specs=[ONCHIP] * (3 + FIELDS),
        out_specs=(OFFCHIP, ONCHIP),
        scratch_shapes=[pltpu.SemaphoreType.DMA((3,))],
        compiler_params=params,
        cost_estimate=pl.CostEstimate(flops=30 * cells, bytes_accessed=30 * cells, transcendentals=0),
    )(low, centre, high, *fields)
    total = keep[0] + jnp.concatenate([near_low[0], near_high[0]], axis=0)
    for a, b in zip(moved_low, moved_high):
        total = total + jnp.concatenate([a, b], axis=0)
    return press[None], total


def solution(mesh):
    return jax.shard_map(
        local,
        mesh=mesh,
        in_specs=(
            P(("epi", "space"), None, None),
            P("draw", ("epi", "space"), None, None),
            P(("epi", "space"), None, None),
            P(("epi", "space"), None, None),
            P(("epi", "space"), None, None),
        ),
        out_specs=(P("draw", ("epi", "space"), None, None), P(("epi", "space"), "draw", None)),
        check_vma=False,
    )
```

```python
import functools

import jax
import jax.numpy as jnp
from jax import lax
from jax.experimental import pallas as pl
from jax.experimental.pallas import tpu as pltpu
from jax.sharding import PartitionSpec as P

SWEEPS = 3
HALO = SWEEPS + 1
EDGE = HALO + 2 * SWEEPS
FIELDS = 16
LANES = 128
SUB = 8
ANYWHERE = pl.BlockSpec(memory_space=pl.ANY)
OFFCHIP = pl.BlockSpec(memory_space=pltpu.HBM)
ONCHIP = pl.BlockSpec(memory_space=pltpu.VMEM)


def lane_shifts(own):
    lane = lax.broadcasted_iota(jnp.int32, (SUB, LANES), 1)
    zero = jnp.zeros((SUB, LANES), jnp.float32)
    fwd = [zero] + [pltpu.roll(v, 1, 1) for v in own]
    bwd = [pltpu.roll(v, LANES - 1, 1) for v in own] + [zero]
    return [
        (jnp.where(lane == 0, fwd[c], fwd[c + 1]), jnp.where(lane == LANES - 1, bwd[c + 1], bwd[c]))
        for c in range(len(own))
    ]


def around(ref, zz, r, rows):
    sub = lax.broadcasted_iota(jnp.int32, (SUB, LANES), 0)
    zero = jnp.zeros((SUB, LANES), jnp.float32)
    own = [ref[zz, c, pl.ds(SUB * r, SUB), :] for c in range(ref.shape[1])]
    sides = lane_shifts(own)
    return own, [sides[c] + cross(ref, zz, c, r, rows, own[c], sub, zero) for c in range(len(own))]


def around_padded(ref, zz, start, count):
    sub = lax.broadcasted_iota(jnp.int32, (SUB, LANES), 0)
    groups = [pl.ds(pl.multiple_of(start + SUB * (q - 1), SUB), SUB) for q in range(count + 2)]
    tiles = ref.shape[1]
    own = [[ref[zz, c, g, :] for c in range(tiles)] for g in groups]
    down = [[pltpu.roll(v, 1, 0) for v in line] for line in own[:-1]]
    up = [[pltpu.roll(v, SUB - 1, 0) for v in line] for line in own[1:]]
    out = []
    for q in range(1, count + 1):
        sides = lane_shifts(own[q])
        line = []
        for c in range(tiles):
            north = jnp.where(sub == 0, down[q - 1][c], down[q][c])
            south = jnp.where(sub == SUB - 1, up[q][c], up[q - 1][c])
            line.append(sides[c] + (north, south, ref[zz - 1, c, groups[q], :], ref[zz + 1, c, groups[q], :]))
        out.append(line)
    return out


def cross(ref, zz, c, r, rows, own, sub, zero):
    if r > 0:
        north = ref[zz, c, pl.ds(SUB * r - 1, SUB), :]
    else:
        north = jnp.where(sub == 0, zero, pltpu.roll(own, 1, 0))
    if r + 1 < rows:
        south = ref[zz, c, pl.ds(SUB * r + 1, SUB), :]
    else:
        south = jnp.where(sub == SUB - 1, zero, pltpu.roll(own, SUB - 1, 0))
    here = pl.ds(SUB * r, SUB)
    return north, south, ref[zz - 1, c, here, :], ref[zz + 1, c, here, :]


def faces(K, WL, WR, zz, c, r, rows):
    sub = lax.broadcasted_iota(jnp.int32, (SUB, LANES), 0)
    zero = jnp.zeros((SUB, LANES), jnp.float32)
    here = pl.ds(SUB * r, SUB)
    k = K[zz, c, here, :]
    rest = [k + v for v in cross(K, zz, c, r, rows, k, sub, zero)]
    return (WL[zz, c, here, :], WR[zz, c, here, :], *rest)


def six(parts):
    a, b, c, d, e, f = parts
    return ((a + b) + (c + d)) + (e + f)


def weighted(weights, parts):
    return six([w * v for w, v in zip(weights, parts)])


def sweeps(refs, ranges, inside, press):
    K, P0, SRC, OBS, P1, P2, U1, U2, U3, HR, SR, NP0, WL, WR, G, E = refs
    tiles, rows = K.shape[1], K.shape[2] // SUB

    def at(r):
        return pl.ds(SUB * r, SUB)

    def coefficients(zz):
        valid = 0.5 * inside(zz)
        for r in range(rows):
            k, kn = around(K, zz, r, rows)
            for c in range(tiles):
                w = [k[c] + v for v in kn[c]]
                HR[zz, c, at(r), :] = valid / (0.5 + 0.5 * six(w))
                WL[zz, c, at(r), :] = w[0]
                WR[zz, c, at(r), :] = w[1]

    def first(zz):
        for r in range(rows):
            _, pn = around(P0, zz, r, rows)
            for c in range(tiles):
                w = faces(K, WL, WR, zz, c, r, rows)
                hr = HR[zz, c, at(r), :]
                rinv = hr + hr
                sr = SRC[zz, c, at(r), :] * rinv
                SR[zz, c, at(r), :] = sr
                NP0[zz, c, at(r), :] = six(pn[c])
                P1[zz, c, at(r), :] = sr + weighted(w, pn[c]) * hr
                U3[zz, c, at(r), :] = OBS[zz, c, at(r), :] * rinv

    def combined(zz):
        valid = inside(zz)
        for r in range(rows):
            k, kn = around(K, zz, r, rows)
            _, pn = around(P0, zz, r, rows)
            for c in range(tiles):
                w = [k[c] + v for v in kn[c]]
                rinv = valid / (0.5 + 0.5 * six(w))
                hr = 0.5 * rinv
                sr = SRC[zz, c, at(r), :] * rinv
                HR[zz, c, at(r), :] = hr
                SR[zz, c, at(r), :] = sr
                WL[zz, c, at(r), :] = w[0]
                WR[zz, c, at(r), :] = w[1]
                NP0[zz, c, at(r), :] = six(pn[c])
                P1[zz, c, at(r), :] = sr + weighted(w, pn[c]) * hr
                U3[zz, c, at(r), :] = OBS[zz, c, at(r), :] * rinv

    def second(zz):
        for r in range(rows):
            _, a = around(P1, zz, r, rows)
            _, v = around(U3, zz, r, rows)
            for c in range(tiles):
                w = faces(K, WL, WR, zz, c, r, rows)
                hr = HR[zz, c, at(r), :]
                p2 = SR[zz, c, at(r), :] + weighted(w, a[c]) * hr
                u2 = weighted(w, v[c]) * hr
                P2[zz, c, at(r), :] = p2
                U2[zz, c, at(r), :] = u2
                G[zz, c, at(r), :] = u2 * six(a[c]) + p2 * six(v[c])

    def third(zz, own):
        for r in range(rows):
            p2, a = around(P2, zz, r, rows)
            u2, v = around(U2, zz, r, rows)
            for c in range(tiles):
                w = faces(K, WL, WR, zz, c, r, rows)
                hr = HR[zz, c, at(r), :]
                p1, u3 = P1[zz, c, at(r), :], U3[zz, c, at(r), :]
                p3 = SR[zz, c, at(r), :] + weighted(w, a[c]) * hr
                u1 = weighted(w, v[c]) * hr
                e = -(u1 * p1 + u2[c] * p2[c] + u3 * p3)
                U1[zz, c, at(r + 1), :] = u1
                E[zz, c, at(r + 1), :] = e
                if own:
                    g = u3 * six(a[c]) + p1 * six(v[c]) + u1 * NP0[zz, c, at(r), :]
                    press(zz)[at(r), pl.ds(c * LANES, LANES)] = p3
                    G[zz, c, at(r), :] = (G[zz, c, at(r), :] + 6.0 * e) + g

    stages = [coefficients, first, second, third]
    if ranges[0] and ranges[0] == ranges[1]:
        stages, ranges = [combined, second, third], ranges[1:]
    for body, spans in zip(stages, ranges):
        for span in spans:
            lo, hi, *own = span
            lax.fori_loop(lo, hi, lambda zz, _, body=body, own=own: body(zz, *own) or 0, 0)


def first_kernel(log_perm, noise, p0, src, obs, K, up, down, top, bottom, means, draws, sems):
    slab, nx, ny = log_perm.shape
    tiles, half = ny // LANES, nx // 2
    rows = pl.ds(pl.multiple_of(half * (lax.axis_index("draw") % 2), half), half)
    copies = []

    def copy(src_ref, dst_ref):
        copies.append(pltpu.make_async_copy(src_ref, dst_ref, sems.at[len(copies)]))

    copy(log_perm, means)
    copy(noise, draws)
    for c in range(tiles):
        cols = pl.ds(c * LANES, LANES)
        at = 0
        for ref, width in ((p0, HALO), (src, SWEEPS), (obs, SWEEPS)):
            for start, out in ((slab - width, up), (0, down)):
                copy(ref.at[pl.ds(start, width), rows, cols], out.at[pl.ds(at, width), c])
            at += width
    for cp in copies:
        cp.start()
    for cp in copies[:2]:
        cp.wait()

    def plane(z, _, out=None, first=0):
        for r in range(nx // SUB):
            for c in range(tiles):
                here, cols = pl.ds(SUB * r, SUB), pl.ds(c * LANES, LANES)
                k = jnp.exp(means[z, here, cols] + draws[z, here, cols])
                K[z + HALO, c, here, :] = k
                if out is not None:
                    out[z - first, c, here, :] = k
        return 0

    low, high = functools.partial(plane, out=bottom), functools.partial(plane, out=top, first=slab - HALO)
    lax.fori_loop(0, HALO, low, 0)
    lax.fori_loop(HALO, slab - HALO, plane, 0)
    lax.fori_loop(slab - HALO, slab, high, 0)
    for cp in copies[2:]:
        cp.wait()


def inner_kernel(K, p0, src, obs, P0, SRC, OBS, P1, P2, U1, U2, U3, HR, SR, NP0, WL, WR, G, E, mid, sems):
    slab = p0.shape[0]
    top = HALO + slab
    copies = []
    for c in range(K.shape[1]):
        for ref, out in ((p0, P0), (src, SRC), (obs, OBS)):
            copies.append(
                pltpu.make_async_copy(
                    ref.at[:, :, pl.ds(c * LANES, LANES)], out.at[pl.ds(HALO, slab), c], sems.at[len(copies)]
                )
            )
    for cp in copies:
        cp.start()
    for cp in copies:
        cp.wait()
    rim = jnp.zeros((SUB, LANES), jnp.float32)

    def clear(zz, _):
        for ref in (U1, E):
            for c in range(ref.shape[1]):
                ref[zz, c, pl.ds(0, SUB), :] = rim
                ref[zz, c, pl.ds(ref.shape[2] - SUB, SUB), :] = rim
        return 0

    lax.fori_loop(HALO, top, clear, 0)
    refs = (K, P0, SRC, OBS, P1, P2, U1, U2, U3, HR, SR, NP0, WL, WR, G, E)
    ranges = [[(HALO + n, top - n)] for n in (1, 1, 2)] + [[(HALO + 3, top - 3, True)]]
    sweeps(refs, ranges, lambda zz: jnp.float32(1.0), lambda zz: mid.at[zz - HALO - SWEEPS])


def side_kernel(low, stages, parts, *args):
    halos = args[: len(args) - 2 * FIELDS - (3 in stages) - len(parts) - 1]
    refs = args[len(halos) + FIELDS : len(halos) + 2 * FIELDS]
    ends, sems = args[len(halos) + 2 * FIELDS : -1], args[-1]
    K, P0, SRC, OBS = refs[:4]
    nx, depth = K.shape[2], K.shape[0]
    half, top = nx // 2, depth - HALO
    par = lax.axis_index("draw") % 2

    pairs = []
    if halos:
        k, mine, *theirs = halos
        pairs.append((k, K.at[pl.ds(0 if low else top, HALO)]))
        for half_rows, which in ((None, par), (theirs, 1 - par)):
            rows = pl.ds(pl.multiple_of(half * which, half), half)
            first = 0
            for field, width in ((P0, HALO), (SRC, SWEEPS), (OBS, SWEEPS)):
                planes = pl.ds(HALO - width if low else top, width)
                if half_rows is None:
                    ref = mine.at[pl.ds(first, width)]
                else:
                    ref = theirs[0] if first == 0 else theirs[1].at[pl.ds(first - HALO, width)]
                pairs.append((ref, field.at[planes, :, rows]))
                first += width
    copies = [pltpu.make_async_copy(a, b, sems.at[i]) for i, (a, b) in enumerate(pairs)]
    for cp in copies:
        cp.start()
    for cp in copies:
        cp.wait()

    space, spaces = lax.axis_index("space"), lax.axis_size("space")
    met = jnp.where(space > 0 if low else space + 1 < spaces, 1.0, 0.0).astype(jnp.float32)
    if low:
        near, last, shift = (1, HALO + 1), [(3, HALO, False), (HALO, HALO + 3, True)], HALO
        ranges = [[near], [near], [(2, HALO + 2)], last]
    else:
        near, last, shift = (top - 1, depth - 1), [(top - 3, top, True), (top, depth - 3, False)], top - 3
        ranges = [[near], [near], [(top - 2, depth - 2)], last]

    def inside(zz):
        return jnp.where(zz < HALO if low else zz >= top, met, jnp.float32(1.0))

    ranges = [spans if n in stages else [] for n, spans in enumerate(ranges)]
    sweeps(refs, ranges, inside, lambda zz: ends[0].at[zz - shift])
    gradients(refs, [(out, *part) for out, part in zip(ends[len(ends) - len(parts) :], parts)])


def gradients(fields, parts):
    K, P0, U1, G, E = fields[0], fields[1], fields[6], fields[-2], fields[-1]
    tiles, nx = K.shape[1], K.shape[2]
    draw, draws = lax.axis_index("draw"), lax.axis_size("draw")
    block, groups = nx // draws, draws // 2
    count = block // SUB

    for out, own, first, z0 in parts:
        parity = draw % 2 if own else 1 - draw % 2
        for s in range(out.shape[0]):
            base = (2 * ((draw // 2 + first + s) % groups) + parity) * block
            start = pl.multiple_of(base, SUB)
            for z in range(out.shape[1]):
                zz = z + z0 + HALO
                v = around_padded(U1, zz, start + SUB, count)
                w = around_padded(E, zz, start + SUB, count)
                for q in range(count):
                    at = pl.ds(pl.multiple_of(start + SUB * q, SUB), SUB)
                    for c in range(tiles):
                        g = G[zz, c, at, :] + P0[zz, c, at, :] * six(v[q][c]) + six(w[q][c])
                        out[s, z, pl.ds(SUB * q, SUB), pl.ds(c * LANES, LANES)] = 0.5 * K[zz, c, at, :] * g


def far_kernel(z0, *args):
    gradients(args[:FIELDS], [(args[FIELDS], True, 1, z0)])


def rest_kernel(*args):
    pieces, fields = args[:3], args[3 : 3 + FIELDS]
    press, keep, sems = args[3 + FIELDS :]
    copies, at = [], 0
    for ref in pieces:
        copies.append(pltpu.make_async_copy(ref, press.at[pl.ds(at, ref.shape[0])], sems.at[len(copies)]))
        at += ref.shape[0]
    for cp in copies:
        cp.start()
    gradients(fields, [(keep, True, 0, 0)])
    for cp in copies:
        cp.wait()


def local(log_perm, noise, source, start_pressure, observe):
    draws, spaces = lax.axis_size("draw"), lax.axis_size("space")
    slab, nx, ny = log_perm.shape
    tiles, depth, half = ny // LANES, slab + 2 * HALO, nx // 2
    up = [(i, i + 1) for i in range(spaces - 1)]
    down = [(j, i) for i, j in up]
    pair = [(i, i ^ 1) for i in range(draws)]
    f32 = jnp.float32
    field = pltpu.VMEM((depth, tiles, nx, LANES), f32)
    padded = pltpu.VMEM((depth, tiles, nx + 2 * SUB, LANES), f32)
    kinds = [field] * 6 + [padded] + [field] * 8 + [padded]
    edge = jax.ShapeDtypeStruct((EDGE, tiles, half, LANES), f32)
    rim = jax.ShapeDtypeStruct((HALO, tiles, nx, LANES), f32)
    whole = jax.ShapeDtypeStruct((slab, nx, ny), f32)
    mid = jax.ShapeDtypeStruct((slab - 2 * SWEEPS, nx, ny), f32)
    groups = draws // 2
    cut = slab // 2
    near = jax.ShapeDtypeStruct((1, slab, nx // draws, ny), f32)
    params = pltpu.CompilerParams(vmem_limit_bytes=8 * 2**20)
    cells = slab * nx * ny

    inputs = (log_perm, noise[0], start_pressure, source, observe)
    K, to_up, to_down, top, bottom = pl.pallas_call(
        first_kernel,
        out_shape=(field, edge, edge, rim, rim),
        in_specs=[OFFCHIP] * 5,
        out_specs=(ONCHIP,) * 5,
        scratch_shapes=[pltpu.VMEM((slab, nx, ny), f32)] * 2 + [pltpu.SemaphoreType.DMA((2 + 6 * tiles,))],
        compiler_params=params,
        cost_estimate=pl.CostEstimate(flops=cells, bytes_accessed=20 * cells, transcendentals=cells),
    )(*[pltpu.with_memory_space_constraint(a, pltpu.HBM) for a in inputs])
    alo = lax.ppermute(to_up, "space", up)
    ahi = lax.ppermute(to_down, "space", down)
    klo = lax.ppermute(top, "space", up)
    khi = lax.ppermute(bottom, "space", down)
    state = pl.pallas_call(
        inner_kernel,
        out_shape=(*kinds[1:], mid),
        in_specs=[ONCHIP] + [ANYWHERE] * 3,
        out_specs=(ONCHIP,) * 16,
        scratch_shapes=[pltpu.SemaphoreType.DMA((3 * tiles,))],
        compiler_params=params,
        cost_estimate=pl.CostEstimate(flops=200 * cells, bytes_accessed=60 * cells, transcendentals=0),
    )(K, start_pressure, source, observe)
    fields, centre = (K, *state[:-1]), state[-1]

    def blocks(count, planes):
        return jax.ShapeDtypeStruct((count, planes, nx // draws, ny), f32)

    def side(low, stages, halos, fields, parts=()):
        ends = (jax.ShapeDtypeStruct((SWEEPS, nx, ny), f32),) if 3 in stages else ()
        ends += tuple(blocks(groups - 1 if first else 1, planes) for _, first, _, planes in parts)
        n = len(halos)
        work = 1 if low else 30 * len(stages) * cells
        out = pl.pallas_call(
            functools.partial(side_kernel, low, stages, [part[:-1] for part in parts]),
            out_shape=(*kinds, *ends),
            in_specs=[ONCHIP] * (n + FIELDS),
            out_specs=(ONCHIP,) * (FIELDS + len(ends)),
            scratch_shapes=[pltpu.SemaphoreType.DMA((8,))],
            input_output_aliases={n + i: i for i in range(FIELDS)},
            compiler_params=params,
            cost_estimate=pl.CostEstimate(flops=work, bytes_accessed=work, transcendentals=0),
        )(*halos, *fields)
        return out[:FIELDS], *out[FIELDS:]

    alo, ahi, last = lax.optimization_barrier((alo, ahi, fields[-1]))
    fields = (*fields[:-1], last)
    lower, upper = [
        (k, mine, *[lax.ppermute(mine[a:b], "draw", pair) for a, b in ((0, HALO), (HALO, EDGE))])
        for k, mine in ((klo, alo), (khi, ahi))
    ]

    def onward(keep, got):
        return [
            lax.ppermute(keep[s - 1] + got[s - 1], "draw", [(j, (j + 2 * s) % draws) for j in range(draws)])
            for s in range(1, groups)
        ]

    def swap(send):
        return lax.ppermute(send, "draw", pair)

    def keep_far(z0, planes, fields):
        return pl.pallas_call(
            functools.partial(far_kernel, z0),
            out_shape=blocks(groups - 1, planes),
            in_specs=[ONCHIP] * FIELDS,
            out_specs=ONCHIP,
            compiler_params=params,
            cost_estimate=pl.CostEstimate(flops=10 * cells, bytes_accessed=10 * cells, transcendentals=0),
        )(*fields)

    (fields,) = side(True, (0, 1, 2), lower, fields)
    parts = [(False, 1, 0, cut), (False, 0, 0, cut), (True, 1, 0, cut)]
    fields, low, send_far, send_near, keep = side(True, (3,), (), fields, parts)
    got_far, near_low = swap(send_far), swap(send_near)
    (fields,) = side(False, (0, 1), upper, fields)
    got_far, near_low, last = lax.optimization_barrier((got_far, near_low, fields[-1]))
    moved_low = onward(keep, got_far)
    parts = [(False, 1, cut, slab - cut), (False, 0, cut, slab - cut)]
    fields, high, send_far, send_near = side(False, (2, 3), (), (*fields[:-1], last), parts)
    got_far, near_high = swap(send_far), swap(send_near)
    moved_low, last = lax.optimization_barrier((moved_low, fields[-1]))
    fields = (*fields[:-1], last)
    keep = keep_far(cut, slab - cut, fields)
    sums = [keep[s - 1] + got_far[s - 1] for s in range(1, groups)]
    sums, last = lax.optimization_barrier((sums, fields[-1]))
    fields = (*fields[:-1], last)
    moved_high = [
        lax.ppermute(a, "draw", [(j, (j + 2 * s) % draws) for j in range(draws)]) for s, a in enumerate(sums, 1)
    ]
    press, keep = pl.pallas_call(
        rest_kernel,
        out_shape=(whole, near),
        in_specs=[ONCHIP] * (3 + FIELDS),
        out_specs=(OFFCHIP, ONCHIP),
        scratch_shapes=[pltpu.SemaphoreType.DMA((3,))],
        compiler_params=params,
        cost_estimate=pl.CostEstimate(flops=30 * cells, bytes_accessed=30 * cells, transcendentals=0),
    )(low, centre, high, *fields)
    total = keep[0] + jnp.concatenate([near_low[0], near_high[0]], axis=0)
    for a, b in zip(moved_low, moved_high):
        total = total + jnp.concatenate([a, b], axis=0)
    return press[None], total


def solution(mesh):
    return jax.shard_map(
        local,
        mesh=mesh,
        in_specs=(
            P(("epi", "space"), None, None),
            P("draw", ("epi", "space"), None, None),
            P(("epi", "space"), None, None),
            P(("epi", "space"), None, None),
            P(("epi", "space"), None, None),
        ),
        out_specs=(P("draw", ("epi", "space"), None, None), P(("epi", "space"), "draw", None)),
        check_vma=False,
    )
```

```python
import functools

import jax
import jax.numpy as jnp
from jax import lax
from jax.experimental import pallas as pl
from jax.experimental.pallas import tpu as pltpu
from jax.sharding import PartitionSpec as P

SWEEPS = 3
HALO = SWEEPS + 1
SLOTS = HALO // 2
EDGE = SLOTS + 2 * SWEEPS
FIELDS = 16
LANES = 128
SUB = 8
ANYWHERE = pl.BlockSpec(memory_space=pl.ANY)
OFFCHIP = pl.BlockSpec(memory_space=pltpu.HBM)
ONCHIP = pl.BlockSpec(memory_space=pltpu.VMEM)


def lane_shifts(own):
    lane = lax.broadcasted_iota(jnp.int32, (SUB, LANES), 1)
    zero = jnp.zeros((SUB, LANES), jnp.float32)
    fwd = [zero] + [pltpu.roll(v, 1, 1) for v in own]
    bwd = [pltpu.roll(v, LANES - 1, 1) for v in own] + [zero]
    return [
        (jnp.where(lane == 0, fwd[c], fwd[c + 1]), jnp.where(lane == LANES - 1, bwd[c + 1], bwd[c]))
        for c in range(len(own))
    ]


def around(ref, zz, r, rows):
    sub = lax.broadcasted_iota(jnp.int32, (SUB, LANES), 0)
    zero = jnp.zeros((SUB, LANES), jnp.float32)
    own = [ref[zz, c, pl.ds(SUB * r, SUB), :] for c in range(ref.shape[1])]
    sides = lane_shifts(own)
    return own, [sides[c] + cross(ref, zz, c, r, rows, own[c], sub, zero) for c in range(len(own))]


def around_padded(ref, zz, start, count):
    sub = lax.broadcasted_iota(jnp.int32, (SUB, LANES), 0)
    groups = [pl.ds(pl.multiple_of(start + SUB * (q - 1), SUB), SUB) for q in range(count + 2)]
    tiles = ref.shape[1]
    own = [[ref[zz, c, g, :] for c in range(tiles)] for g in groups]
    down = [[pltpu.roll(v, 1, 0) for v in line] for line in own[:-1]]
    up = [[pltpu.roll(v, SUB - 1, 0) for v in line] for line in own[1:]]
    out = []
    for q in range(1, count + 1):
        sides = lane_shifts(own[q])
        line = []
        for c in range(tiles):
            north = jnp.where(sub == 0, down[q - 1][c], down[q][c])
            south = jnp.where(sub == SUB - 1, up[q][c], up[q - 1][c])
            line.append(sides[c] + (north, south, ref[zz - 1, c, groups[q], :], ref[zz + 1, c, groups[q], :]))
        out.append(line)
    return out


def cross(ref, zz, c, r, rows, own, sub, zero):
    if r > 0:
        north = ref[zz, c, pl.ds(SUB * r - 1, SUB), :]
    else:
        north = jnp.where(sub == 0, zero, pltpu.roll(own, 1, 0))
    if r + 1 < rows:
        south = ref[zz, c, pl.ds(SUB * r + 1, SUB), :]
    else:
        south = jnp.where(sub == SUB - 1, zero, pltpu.roll(own, SUB - 1, 0))
    here = pl.ds(SUB * r, SUB)
    return north, south, ref[zz - 1, c, here, :], ref[zz + 1, c, here, :]


def faces(K, WL, WR, zz, c, r, rows):
    sub = lax.broadcasted_iota(jnp.int32, (SUB, LANES), 0)
    zero = jnp.zeros((SUB, LANES), jnp.float32)
    here = pl.ds(SUB * r, SUB)
    k = K[zz, c, here, :]
    rest = [k + v for v in cross(K, zz, c, r, rows, k, sub, zero)]
    return (WL[zz, c, here, :], WR[zz, c, here, :], *rest)


def six(parts):
    a, b, c, d, e, f = parts
    return ((a + b) + (c + d)) + (e + f)


def weighted(weights, parts):
    return six([w * v for w, v in zip(weights, parts)])


def sweeps(refs, ranges, inside, press):
    K, P0, SRC, OBS, P1, P2, U1, U2, U3, HR, SR, NP0, WL, WR, G, E = refs
    tiles, rows = K.shape[1], K.shape[2] // SUB

    def at(r):
        return pl.ds(SUB * r, SUB)

    def coefficients(zz):
        valid = 0.5 * inside(zz)
        for r in range(rows):
            k, kn = around(K, zz, r, rows)
            for c in range(tiles):
                w = [k[c] + v for v in kn[c]]
                HR[zz, c, at(r), :] = valid / (0.5 + 0.5 * six(w))
                WL[zz, c, at(r), :] = w[0]
                WR[zz, c, at(r), :] = w[1]

    def first(zz):
        for r in range(rows):
            _, pn = around(P0, zz, r, rows)
            for c in range(tiles):
                w = faces(K, WL, WR, zz, c, r, rows)
                hr = HR[zz, c, at(r), :]
                rinv = hr + hr
                sr = SRC[zz, c, at(r), :] * rinv
                SR[zz, c, at(r), :] = sr
                NP0[zz, c, at(r), :] = six(pn[c])
                P1[zz, c, at(r), :] = sr + weighted(w, pn[c]) * hr
                U3[zz, c, at(r), :] = OBS[zz, c, at(r), :] * rinv

    def combined(zz):
        valid = inside(zz)
        for r in range(rows):
            k, kn = around(K, zz, r, rows)
            _, pn = around(P0, zz, r, rows)
            for c in range(tiles):
                w = [k[c] + v for v in kn[c]]
                rinv = valid / (0.5 + 0.5 * six(w))
                hr = 0.5 * rinv
                sr = SRC[zz, c, at(r), :] * rinv
                HR[zz, c, at(r), :] = hr
                SR[zz, c, at(r), :] = sr
                WL[zz, c, at(r), :] = w[0]
                WR[zz, c, at(r), :] = w[1]
                NP0[zz, c, at(r), :] = six(pn[c])
                P1[zz, c, at(r), :] = sr + weighted(w, pn[c]) * hr
                U3[zz, c, at(r), :] = OBS[zz, c, at(r), :] * rinv

    def second(zz):
        for r in range(rows):
            _, a = around(P1, zz, r, rows)
            _, v = around(U3, zz, r, rows)
            for c in range(tiles):
                w = faces(K, WL, WR, zz, c, r, rows)
                hr = HR[zz, c, at(r), :]
                p2 = SR[zz, c, at(r), :] + weighted(w, a[c]) * hr
                u2 = weighted(w, v[c]) * hr
                P2[zz, c, at(r), :] = p2
                U2[zz, c, at(r), :] = u2
                G[zz, c, at(r), :] = u2 * six(a[c]) + p2 * six(v[c])

    def third(zz, own):
        for r in range(rows):
            p2, a = around(P2, zz, r, rows)
            u2, v = around(U2, zz, r, rows)
            for c in range(tiles):
                w = faces(K, WL, WR, zz, c, r, rows)
                hr = HR[zz, c, at(r), :]
                p1, u3 = P1[zz, c, at(r), :], U3[zz, c, at(r), :]
                p3 = SR[zz, c, at(r), :] + weighted(w, a[c]) * hr
                u1 = weighted(w, v[c]) * hr
                e = -(u1 * p1 + u2[c] * p2[c] + u3 * p3)
                U1[zz, c, at(r + 1), :] = u1
                E[zz, c, at(r + 1), :] = e
                if own:
                    g = u3 * six(a[c]) + p1 * six(v[c]) + u1 * NP0[zz, c, at(r), :]
                    press(zz)[at(r), pl.ds(c * LANES, LANES)] = p3
                    G[zz, c, at(r), :] = (G[zz, c, at(r), :] + 6.0 * e) + g

    stages = [coefficients, first, second, third]
    if ranges[0] and ranges[0] == ranges[1]:
        stages, ranges = [combined, second, third], ranges[1:]
    for body, spans in zip(stages, ranges):
        for span in spans:
            lo, hi, *own = span
            lax.fori_loop(lo, hi, lambda zz, _, body=body, own=own: body(zz, *own) or 0, 0)


def first_kernel(log_perm, noise, p0, src, obs, K, up, down, top, bottom, means, draws, sems):
    slab, nx, ny = log_perm.shape
    tiles, half = ny // LANES, nx // 2
    draw, quarter = lax.axis_index("draw"), half // 2
    rows = pl.ds(pl.multiple_of(half * (draw % 2), half), half)
    few = pl.ds(pl.multiple_of(half * (draw % 2) + quarter * (draw // 2 % 2), quarter), quarter)
    copies = []

    def copy(src_ref, dst_ref):
        copies.append(pltpu.make_async_copy(src_ref, dst_ref, sems.at[len(copies)]))

    copy(log_perm, means)
    copy(noise, draws)
    for c in range(tiles):
        cols = pl.ds(c * LANES, LANES)
        for start, out in ((slab - HALO, up), (0, down)):
            for h in range(2):
                planes = pl.ds(start + h * SLOTS, SLOTS)
                copy(p0.at[planes, few, cols], out.at[pl.ds(0, SLOTS), c, pl.ds(h * quarter, quarter)])
        at = SLOTS
        for ref in (src, obs):
            for start, out in ((slab - SWEEPS, up), (0, down)):
                copy(ref.at[pl.ds(start, SWEEPS), rows, cols], out.at[pl.ds(at, SWEEPS), c])
            at += SWEEPS
    for cp in copies:
        cp.start()
    for cp in copies[:2]:
        cp.wait()

    def plane(z, _, out=None, first=0):
        for r in range(nx // SUB):
            for c in range(tiles):
                here, cols = pl.ds(SUB * r, SUB), pl.ds(c * LANES, LANES)
                k = jnp.exp(means[z, here, cols] + draws[z, here, cols])
                K[z + HALO, c, here, :] = k
                if out is not None:
                    out[z - first, c, here, :] = k
        return 0

    low, high = functools.partial(plane, out=bottom), functools.partial(plane, out=top, first=slab - HALO)
    lax.fori_loop(0, HALO, low, 0)
    lax.fori_loop(HALO, slab - HALO, plane, 0)
    lax.fori_loop(slab - HALO, slab, high, 0)
    for cp in copies[2:]:
        cp.wait()


def inner_kernel(K, p0, src, obs, P0, SRC, OBS, P1, P2, U1, U2, U3, HR, SR, NP0, WL, WR, G, E, mid, sems):
    slab = p0.shape[0]
    top = HALO + slab
    copies = []
    for c in range(K.shape[1]):
        for ref, out in ((p0, P0), (src, SRC), (obs, OBS)):
            copies.append(
                pltpu.make_async_copy(
                    ref.at[:, :, pl.ds(c * LANES, LANES)], out.at[pl.ds(HALO, slab), c], sems.at[len(copies)]
                )
            )
    for cp in copies:
        cp.start()
    for cp in copies:
        cp.wait()
    rim = jnp.zeros((SUB, LANES), jnp.float32)

    def clear(zz, _):
        for ref in (U1, E):
            for c in range(ref.shape[1]):
                ref[zz, c, pl.ds(0, SUB), :] = rim
                ref[zz, c, pl.ds(ref.shape[2] - SUB, SUB), :] = rim
        return 0

    lax.fori_loop(HALO, top, clear, 0)
    refs = (K, P0, SRC, OBS, P1, P2, U1, U2, U3, HR, SR, NP0, WL, WR, G, E)
    ranges = [[(HALO + n, top - n)] for n in (1, 1, 2)] + [[(HALO + 3, top - 3, True)]]
    sweeps(refs, ranges, lambda zz: jnp.float32(1.0), lambda zz: mid.at[zz - HALO - SWEEPS])


def side_kernel(low, stages, parts, *args):
    halos = args[: len(args) - 2 * FIELDS - (3 in stages) - len(parts) - 1]
    refs = args[len(halos) + FIELDS : len(halos) + 2 * FIELDS]
    ends, sems = args[len(halos) + 2 * FIELDS : -1], args[-1]
    K, P0, SRC, OBS = refs[:4]
    nx, depth = K.shape[2], K.shape[0]
    half, top = nx // 2, depth - HALO
    par = lax.axis_index("draw") % 2

    pairs = []
    if halos:
        k, mine, beside, theirs, theirs_beside, theirs_rest = halos
        pairs.append((k, K.at[pl.ds(0 if low else top, HALO)]))
        quarter, across = half // 2, lax.axis_index("draw") // 2 % 2
        pieces = ((mine, par, across), (beside, par, 1 - across), (theirs, 1 - par, across))
        for ref, which, part in (*pieces, (theirs_beside, 1 - par, 1 - across)):
            slots = pl.ds(0 if low or ref is mine else SLOTS, SLOTS)
            rows = pl.ds(pl.multiple_of(half * which + quarter * part, quarter), quarter)
            for h in range(2):
                planes = pl.ds((0 if low else top) + h * SLOTS, SLOTS)
                pairs.append((ref.at[slots, :, pl.ds(h * quarter, quarter)], P0.at[planes, :, rows]))
        for ref, which, first in ((mine, par, SLOTS), (theirs_rest, 1 - par, 0)):
            rows = pl.ds(pl.multiple_of(half * which, half), half)
            planes = pl.ds(HALO - SWEEPS if low else top, SWEEPS)
            for n, field in enumerate((SRC, OBS)):
                pairs.append((ref.at[pl.ds(first + n * SWEEPS, SWEEPS)], field.at[planes, :, rows]))
    copies = [pltpu.make_async_copy(a, b, sems.at[i]) for i, (a, b) in enumerate(pairs)]
    for cp in copies:
        cp.start()
    for cp in copies:
        cp.wait()

    space, spaces = lax.axis_index("space"), lax.axis_size("space")
    met = jnp.where(space > 0 if low else space + 1 < spaces, 1.0, 0.0).astype(jnp.float32)
    if low:
        near, last, shift = (1, HALO + 1), [(3, HALO, False), (HALO, HALO + 3, True)], HALO
        ranges = [[near], [near], [(2, HALO + 2)], last]
    else:
        near, last, shift = (top - 1, depth - 1), [(top - 3, top, True), (top, depth - 3, False)], top - 3
        ranges = [[near], [near], [(top - 2, depth - 2)], last]

    def inside(zz):
        return jnp.where(zz < HALO if low else zz >= top, met, jnp.float32(1.0))

    ranges = [spans if n in stages else [] for n, spans in enumerate(ranges)]
    sweeps(refs, ranges, inside, lambda zz: ends[0].at[zz - shift])
    gradients(refs, [(out, *part) for out, part in zip(ends[len(ends) - len(parts) :], parts)])


def gradients(fields, parts):
    K, P0, U1, G, E = fields[0], fields[1], fields[6], fields[-2], fields[-1]
    tiles, nx = K.shape[1], K.shape[2]
    draw, draws = lax.axis_index("draw"), lax.axis_size("draw")
    block, groups = nx // draws, draws // 2
    count = block // SUB

    for out, own, first, z0 in parts:
        parity = draw % 2 if own else 1 - draw % 2
        for s in range(out.shape[0]):
            base = (2 * ((draw // 2 + first + s) % groups) + parity) * block
            start = pl.multiple_of(base, SUB)
            for z in range(out.shape[1]):
                zz = z + z0 + HALO
                v = around_padded(U1, zz, start + SUB, count)
                w = around_padded(E, zz, start + SUB, count)
                for q in range(count):
                    at = pl.ds(pl.multiple_of(start + SUB * q, SUB), SUB)
                    for c in range(tiles):
                        g = G[zz, c, at, :] + P0[zz, c, at, :] * six(v[q][c]) + six(w[q][c])
                        out[s, z, pl.ds(SUB * q, SUB), pl.ds(c * LANES, LANES)] = 0.5 * K[zz, c, at, :] * g


def far_kernel(z0, *args):
    gradients(args[:FIELDS], [(args[FIELDS], True, 1, z0)])


def rest_kernel(*args):
    pieces, fields = args[:3], args[3 : 3 + FIELDS]
    press, keep, sems = args[3 + FIELDS :]
    copies, at = [], 0
    for ref in pieces:
        copies.append(pltpu.make_async_copy(ref, press.at[pl.ds(at, ref.shape[0])], sems.at[len(copies)]))
        at += ref.shape[0]
    for cp in copies:
        cp.start()
    gradients(fields, [(keep, True, 0, 0)])
    for cp in copies:
        cp.wait()


def local(log_perm, noise, source, start_pressure, observe):
    draws, spaces = lax.axis_size("draw"), lax.axis_size("space")
    slab, nx, ny = log_perm.shape
    tiles, depth, half = ny // LANES, slab + 2 * HALO, nx // 2
    up = [(i, i + 1) for i in range(spaces - 1)]
    down = [(j, i) for i, j in up]
    pair = [(i, i ^ 1) for i in range(draws)]
    f32 = jnp.float32
    field = pltpu.VMEM((depth, tiles, nx, LANES), f32)
    padded = pltpu.VMEM((depth, tiles, nx + 2 * SUB, LANES), f32)
    kinds = [field] * 6 + [padded] + [field] * 8 + [padded]
    edge = jax.ShapeDtypeStruct((EDGE, tiles, half, LANES), f32)
    rim = jax.ShapeDtypeStruct((HALO, tiles, nx, LANES), f32)
    whole = jax.ShapeDtypeStruct((slab, nx, ny), f32)
    mid = jax.ShapeDtypeStruct((slab - 2 * SWEEPS, nx, ny), f32)
    groups = draws // 2
    cut = slab // 2
    near = jax.ShapeDtypeStruct((1, slab, nx // draws, ny), f32)
    params = pltpu.CompilerParams(vmem_limit_bytes=8 * 2**20)
    cells = slab * nx * ny

    inputs = (log_perm, noise[0], start_pressure, source, observe)
    K, to_up, to_down, top, bottom = pl.pallas_call(
        first_kernel,
        out_shape=(field, edge, edge, rim, rim),
        in_specs=[OFFCHIP] * 5,
        out_specs=(ONCHIP,) * 5,
        scratch_shapes=[pltpu.VMEM((slab, nx, ny), f32)] * 2 + [pltpu.SemaphoreType.DMA((2 + 8 * tiles,))],
        compiler_params=params,
        cost_estimate=pl.CostEstimate(flops=cells, bytes_accessed=20 * cells, transcendentals=cells),
    )(*[pltpu.with_memory_space_constraint(a, pltpu.HBM) for a in inputs])
    alo = lax.ppermute(to_up, "space", up)
    ahi = lax.ppermute(to_down, "space", down)
    klo = lax.ppermute(top, "space", up)
    khi = lax.ppermute(bottom, "space", down)
    state = pl.pallas_call(
        inner_kernel,
        out_shape=(*kinds[1:], mid),
        in_specs=[ONCHIP] + [ANYWHERE] * 3,
        out_specs=(ONCHIP,) * 16,
        scratch_shapes=[pltpu.SemaphoreType.DMA((3 * tiles,))],
        compiler_params=params,
        cost_estimate=pl.CostEstimate(flops=200 * cells, bytes_accessed=60 * cells, transcendentals=0),
    )(K, start_pressure, source, observe)
    fields, centre = (K, *state[:-1]), state[-1]

    def blocks(count, planes):
        return jax.ShapeDtypeStruct((count, planes, nx // draws, ny), f32)

    def side(low, stages, halos, fields, parts=()):
        ends = (jax.ShapeDtypeStruct((SWEEPS, nx, ny), f32),) if 3 in stages else ()
        ends += tuple(blocks(groups - 1 if first else 1, planes) for _, first, _, planes in parts)
        n = len(halos)
        work = 1 if low else 30 * len(stages) * cells
        out = pl.pallas_call(
            functools.partial(side_kernel, low, stages, [part[:-1] for part in parts]),
            out_shape=(*kinds, *ends),
            in_specs=[ONCHIP] * (n + FIELDS),
            out_specs=(ONCHIP,) * (FIELDS + len(ends)),
            scratch_shapes=[pltpu.SemaphoreType.DMA((13,))],
            input_output_aliases={n + i: i for i in range(FIELDS)},
            compiler_params=params,
            cost_estimate=pl.CostEstimate(flops=work, bytes_accessed=work, transcendentals=0),
        )(*halos, *fields)
        return out[:FIELDS], *out[FIELDS:]

    alo, ahi, last = lax.optimization_barrier((alo, ahi, fields[-1]))
    fields = (*fields[:-1], last)
    own = jnp.concatenate([alo[:SLOTS], ahi[:SLOTS]], axis=0)
    beside = lax.ppermute(own, "draw", [(i, i ^ 2) for i in range(draws)])
    from_core = [lax.ppermute(a, "draw", pair) for a in (own, beside)]
    lower = (klo, alo, beside, *from_core, lax.ppermute(alo[SLOTS:], "draw", pair))
    upper = (khi, ahi, beside, *from_core, lax.ppermute(ahi[SLOTS:], "draw", pair))

    def onward(keep, got):
        return [
            lax.ppermute(keep[s - 1] + got[s - 1], "draw", [(j, (j + 2 * s) % draws) for j in range(draws)])
            for s in range(1, groups)
        ]

    def swap(send):
        return lax.ppermute(send, "draw", pair)

    def keep_far(z0, planes, fields):
        return pl.pallas_call(
            functools.partial(far_kernel, z0),
            out_shape=blocks(groups - 1, planes),
            in_specs=[ONCHIP] * FIELDS,
            out_specs=ONCHIP,
            compiler_params=params,
            cost_estimate=pl.CostEstimate(flops=10 * cells, bytes_accessed=10 * cells, transcendentals=0),
        )(*fields)

    (fields,) = side(True, (0, 1, 2), lower, fields)
    parts = [(False, 1, 0, cut), (False, 0, 0, cut), (True, 1, 0, cut)]
    fields, low, send_far, send_near, keep = side(True, (3,), (), fields, parts)
    got_far, near_low = swap(send_far), swap(send_near)
    (fields,) = side(False, (0, 1), upper, fields)
    got_far, near_low, last = lax.optimization_barrier((got_far, near_low, fields[-1]))
    moved_low = onward(keep, got_far)
    parts = [(False, 1, cut, slab - cut), (False, 0, cut, slab - cut)]
    fields, high, send_far, send_near = side(False, (2, 3), (), (*fields[:-1], last), parts)
    got_far, near_high = swap(send_far), swap(send_near)
    moved_low, last = lax.optimization_barrier((moved_low, fields[-1]))
    fields = (*fields[:-1], last)
    keep = keep_far(cut, slab - cut, fields)
    sums = [keep[s - 1] + got_far[s - 1] for s in range(1, groups)]
    sums, last = lax.optimization_barrier((sums, fields[-1]))
    fields = (*fields[:-1], last)
    moved_high = [
        lax.ppermute(a, "draw", [(j, (j + 2 * s) % draws) for j in range(draws)]) for s, a in enumerate(sums, 1)
    ]
    press, keep = pl.pallas_call(
        rest_kernel,
        out_shape=(whole, near),
        in_specs=[ONCHIP] * (3 + FIELDS),
        out_specs=(OFFCHIP, ONCHIP),
        scratch_shapes=[pltpu.SemaphoreType.DMA((3,))],
        compiler_params=params,
        cost_estimate=pl.CostEstimate(flops=30 * cells, bytes_accessed=30 * cells, transcendentals=0),
    )(low, centre, high, *fields)
    total = keep[0] + jnp.concatenate([near_low[0], near_high[0]], axis=0)
    for a, b in zip(moved_low, moved_high):
        total = total + jnp.concatenate([a, b], axis=0)
    return press[None], total


def solution(mesh):
    return jax.shard_map(
        local,
        mesh=mesh,
        in_specs=(
            P(("epi", "space"), None, None),
            P("draw", ("epi", "space"), None, None),
            P(("epi", "space"), None, None),
            P(("epi", "space"), None, None),
            P(("epi", "space"), None, None),
        ),
        out_specs=(P("draw", ("epi", "space"), None, None), P(("epi", "space"), "draw", None)),
        check_vma=False,
    )
```

```python
import functools

import jax
import jax.numpy as jnp
from jax import lax
from jax.experimental import pallas as pl
from jax.experimental.pallas import tpu as pltpu
from jax.sharding import PartitionSpec as P

SWEEPS = 3
HALO = SWEEPS + 1
EDGE = HALO + 2 * SWEEPS
FIELDS = 16
LANES = 128
SUB = 8
ANYWHERE = pl.BlockSpec(memory_space=pl.ANY)
OFFCHIP = pl.BlockSpec(memory_space=pltpu.HBM)
ONCHIP = pl.BlockSpec(memory_space=pltpu.VMEM)


def lane_shifts(own):
    lane = lax.broadcasted_iota(jnp.int32, (SUB, LANES), 1)
    zero = jnp.zeros((SUB, LANES), jnp.float32)
    fwd = [zero] + [pltpu.roll(v, 1, 1) for v in own]
    bwd = [pltpu.roll(v, LANES - 1, 1) for v in own] + [zero]
    return [
        (jnp.where(lane == 0, fwd[c], fwd[c + 1]), jnp.where(lane == LANES - 1, bwd[c + 1], bwd[c]))
        for c in range(len(own))
    ]


def around(ref, zz, r, rows):
    sub = lax.broadcasted_iota(jnp.int32, (SUB, LANES), 0)
    zero = jnp.zeros((SUB, LANES), jnp.float32)
    own = [ref[zz, c, pl.ds(SUB * r, SUB), :] for c in range(ref.shape[1])]
    sides = lane_shifts(own)
    return own, [sides[c] + cross(ref, zz, c, r, rows, own[c], sub, zero) for c in range(len(own))]


def around_padded(ref, zz, start, count):
    sub = lax.broadcasted_iota(jnp.int32, (SUB, LANES), 0)
    groups = [pl.ds(pl.multiple_of(start + SUB * (q - 1), SUB), SUB) for q in range(count + 2)]
    tiles = ref.shape[1]
    own = [[ref[zz, c, g, :] for c in range(tiles)] for g in groups]
    down = [[pltpu.roll(v, 1, 0) for v in line] for line in own[:-1]]
    up = [[pltpu.roll(v, SUB - 1, 0) for v in line] for line in own[1:]]
    out = []
    for q in range(1, count + 1):
        sides = lane_shifts(own[q])
        line = []
        for c in range(tiles):
            north = jnp.where(sub == 0, down[q - 1][c], down[q][c])
            south = jnp.where(sub == SUB - 1, up[q][c], up[q - 1][c])
            line.append(sides[c] + (north, south, ref[zz - 1, c, groups[q], :], ref[zz + 1, c, groups[q], :]))
        out.append(line)
    return out


def cross(ref, zz, c, r, rows, own, sub, zero):
    if r > 0:
        north = ref[zz, c, pl.ds(SUB * r - 1, SUB), :]
    else:
        north = jnp.where(sub == 0, zero, pltpu.roll(own, 1, 0))
    if r + 1 < rows:
        south = ref[zz, c, pl.ds(SUB * r + 1, SUB), :]
    else:
        south = jnp.where(sub == SUB - 1, zero, pltpu.roll(own, SUB - 1, 0))
    here = pl.ds(SUB * r, SUB)
    return north, south, ref[zz - 1, c, here, :], ref[zz + 1, c, here, :]


def faces(K, WL, WR, zz, c, r, rows):
    sub = lax.broadcasted_iota(jnp.int32, (SUB, LANES), 0)
    zero = jnp.zeros((SUB, LANES), jnp.float32)
    here = pl.ds(SUB * r, SUB)
    k = K[zz, c, here, :]
    rest = [k + v for v in cross(K, zz, c, r, rows, k, sub, zero)]
    return (WL[zz, c, here, :], WR[zz, c, here, :], *rest)


def six(parts):
    a, b, c, d, e, f = parts
    return ((a + b) + (c + d)) + (e + f)


def weighted(weights, parts):
    return six([w * v for w, v in zip(weights, parts)])


def sweeps(refs, ranges, inside, press):
    K, P0, SRC, OBS, P1, P2, U1, U2, U3, HR, SR, NP0, WL, WR, G, E = refs
    tiles, rows = K.shape[1], K.shape[2] // SUB

    def at(r):
        return pl.ds(SUB * r, SUB)

    def coefficients(zz):
        valid = 0.5 * inside(zz)
        for r in range(rows):
            k, kn = around(K, zz, r, rows)
            for c in range(tiles):
                w = [k[c] + v for v in kn[c]]
                HR[zz, c, at(r), :] = valid / (0.5 + 0.5 * six(w))
                WL[zz, c, at(r), :] = w[0]
                WR[zz, c, at(r), :] = w[1]

    def first(zz):
        for r in range(rows):
            _, pn = around(P0, zz, r, rows)
            for c in range(tiles):
                w = faces(K, WL, WR, zz, c, r, rows)
                hr = HR[zz, c, at(r), :]
                rinv = hr + hr
                sr = SRC[zz, c, at(r), :] * rinv
                SR[zz, c, at(r), :] = sr
                NP0[zz, c, at(r), :] = six(pn[c])
                P1[zz, c, at(r), :] = sr + weighted(w, pn[c]) * hr
                U3[zz, c, at(r), :] = OBS[zz, c, at(r), :] * rinv

    def combined(zz):
        valid = inside(zz)
        for r in range(rows):
            k, kn = around(K, zz, r, rows)
            _, pn = around(P0, zz, r, rows)
            for c in range(tiles):
                w = [k[c] + v for v in kn[c]]
                rinv = valid / (0.5 + 0.5 * six(w))
                hr = 0.5 * rinv
                sr = SRC[zz, c, at(r), :] * rinv
                HR[zz, c, at(r), :] = hr
                SR[zz, c, at(r), :] = sr
                WL[zz, c, at(r), :] = w[0]
                WR[zz, c, at(r), :] = w[1]
                NP0[zz, c, at(r), :] = six(pn[c])
                P1[zz, c, at(r), :] = sr + weighted(w, pn[c]) * hr
                U3[zz, c, at(r), :] = OBS[zz, c, at(r), :] * rinv

    def second(zz):
        for r in range(rows):
            _, a = around(P1, zz, r, rows)
            _, v = around(U3, zz, r, rows)
            for c in range(tiles):
                w = faces(K, WL, WR, zz, c, r, rows)
                hr = HR[zz, c, at(r), :]
                p2 = SR[zz, c, at(r), :] + weighted(w, a[c]) * hr
                u2 = weighted(w, v[c]) * hr
                P2[zz, c, at(r), :] = p2
                U2[zz, c, at(r), :] = u2
                G[zz, c, at(r), :] = u2 * six(a[c]) + p2 * six(v[c])

    def third(zz, own):
        for r in range(rows):
            p2, a = around(P2, zz, r, rows)
            u2, v = around(U2, zz, r, rows)
            for c in range(tiles):
                w = faces(K, WL, WR, zz, c, r, rows)
                hr = HR[zz, c, at(r), :]
                p1, u3 = P1[zz, c, at(r), :], U3[zz, c, at(r), :]
                p3 = SR[zz, c, at(r), :] + weighted(w, a[c]) * hr
                u1 = weighted(w, v[c]) * hr
                e = -(u1 * p1 + u2[c] * p2[c] + u3 * p3)
                U1[zz, c, at(r + 1), :] = u1
                E[zz, c, at(r + 1), :] = e
                if own:
                    g = u3 * six(a[c]) + p1 * six(v[c]) + u1 * NP0[zz, c, at(r), :]
                    press(zz)[at(r), pl.ds(c * LANES, LANES)] = p3
                    G[zz, c, at(r), :] = (G[zz, c, at(r), :] + 6.0 * e) + g

    stages = [coefficients, first, second, third]
    if ranges[0] and ranges[0] == ranges[1]:
        stages, ranges = [combined, second, third], ranges[1:]
    for body, spans in zip(stages, ranges):
        for span in spans:
            lo, hi, *own = span
            lax.fori_loop(lo, hi, lambda zz, _, body=body, own=own: body(zz, *own) or 0, 0)


def first_kernel(log_perm, noise, p0, src, obs, K, up, down, top, bottom, means, draws, sems):
    slab, nx, ny = log_perm.shape
    tiles, half = ny // LANES, nx // 2
    rows = pl.ds(pl.multiple_of(half * (lax.axis_index("draw") % 2), half), half)
    copies = []

    def copy(src_ref, dst_ref):
        copies.append(pltpu.make_async_copy(src_ref, dst_ref, sems.at[len(copies)]))

    copy(log_perm, means)
    copy(noise, draws)
    for c in range(tiles):
        cols = pl.ds(c * LANES, LANES)
        at = 0
        for ref, width in ((p0, HALO), (src, SWEEPS), (obs, SWEEPS)):
            for start, out in ((slab - width, up), (0, down)):
                copy(ref.at[pl.ds(start, width), rows, cols], out.at[pl.ds(at, width), c])
            at += width
    for cp in copies:
        cp.start()
    for cp in copies[:2]:
        cp.wait()

    def plane(z, _, out=None, first=0):
        for r in range(nx // SUB):
            for c in range(tiles):
                here, cols = pl.ds(SUB * r, SUB), pl.ds(c * LANES, LANES)
                k = jnp.exp(means[z, here, cols] + draws[z, here, cols])
                K[z + HALO, c, here, :] = k
                if out is not None:
                    out[z - first, c, here, :] = k
        return 0

    low, high = functools.partial(plane, out=bottom), functools.partial(plane, out=top, first=slab - HALO)
    lax.fori_loop(0, HALO, low, 0)
    lax.fori_loop(HALO, slab - HALO, plane, 0)
    lax.fori_loop(slab - HALO, slab, high, 0)
    for cp in copies[2:]:
        cp.wait()


def inner_kernel(K, p0, src, obs, P0, SRC, OBS, P1, P2, U1, U2, U3, HR, SR, NP0, WL, WR, G, E, mid, sems):
    slab = p0.shape[0]
    top = HALO + slab
    copies = []
    for c in range(K.shape[1]):
        for ref, out in ((p0, P0), (src, SRC), (obs, OBS)):
            copies.append(
                pltpu.make_async_copy(
                    ref.at[:, :, pl.ds(c * LANES, LANES)], out.at[pl.ds(HALO, slab), c], sems.at[len(copies)]
                )
            )
    for cp in copies:
        cp.start()
    for cp in copies:
        cp.wait()
    rim = jnp.zeros((SUB, LANES), jnp.float32)

    def clear(zz, _):
        for ref in (U1, E):
            for c in range(ref.shape[1]):
                ref[zz, c, pl.ds(0, SUB), :] = rim
                ref[zz, c, pl.ds(ref.shape[2] - SUB, SUB), :] = rim
        return 0

    lax.fori_loop(HALO, top, clear, 0)
    refs = (K, P0, SRC, OBS, P1, P2, U1, U2, U3, HR, SR, NP0, WL, WR, G, E)
    ranges = [[(HALO + n, top - n)] for n in (1, 1, 2)] + [[(HALO + 3, top - 3, True)]]
    sweeps(refs, ranges, lambda zz: jnp.float32(1.0), lambda zz: mid.at[zz - HALO - SWEEPS])


def fill_kernel(low, *args):
    mine, theirs, rest = args[:3]
    P0, SRC, OBS, sems = args[-4:]
    nx, depth = P0.shape[2], P0.shape[0]
    half, par = nx // 2, lax.axis_index("draw") % 2
    pairs = []
    for which, start, sweeps_from in ((par, mine, mine.at[pl.ds(HALO, 2 * SWEEPS)]), (1 - par, theirs, rest)):
        rows = pl.ds(pl.multiple_of(half * which, half), half)
        planes = pl.ds(0 if low else depth - HALO, HALO)
        pairs.append((start.at[pl.ds(0, HALO)], P0.at[planes, :, rows]))
        planes = pl.ds(HALO - SWEEPS if low else depth - HALO, SWEEPS)
        for n, field in enumerate((SRC, OBS)):
            pairs.append((sweeps_from.at[pl.ds(n * SWEEPS, SWEEPS)], field.at[planes, :, rows]))
    copies = [pltpu.make_async_copy(a, b, sems.at[i]) for i, (a, b) in enumerate(pairs)]
    for cp in copies:
        cp.start()
    for cp in copies:
        cp.wait()


def side_kernel(low, stages, parts, *args):
    halos = args[: len(args) - 2 * FIELDS - (3 in stages) - len(parts) - 1]
    refs = args[len(halos) + FIELDS : len(halos) + 2 * FIELDS]
    ends, sems = args[len(halos) + 2 * FIELDS : -1], args[-1]
    K, depth = refs[0], refs[0].shape[0]
    top = depth - HALO

    pairs = []
    if halos:
        pairs.append((halos[0], K.at[pl.ds(0 if low else top, HALO)]))
    copies = [pltpu.make_async_copy(a, b, sems.at[i]) for i, (a, b) in enumerate(pairs)]
    for cp in copies:
        cp.start()
    for cp in copies:
        cp.wait()

    space, spaces = lax.axis_index("space"), lax.axis_size("space")
    met = jnp.where(space > 0 if low else space + 1 < spaces, 1.0, 0.0).astype(jnp.float32)
    if low:
        near, last, shift = (1, HALO + 1), [(3, HALO, False), (HALO, HALO + 3, True)], HALO
        ranges = [[near], [near], [(2, HALO + 2)], last]
    else:
        near, last, shift = (top - 1, depth - 1), [(top - 3, top, True), (top, depth - 3, False)], top - 3
        ranges = [[near], [near], [(top - 2, depth - 2)], last]

    def inside(zz):
        return jnp.where(zz < HALO if low else zz >= top, met, jnp.float32(1.0))

    ranges = [spans if n in stages else [] for n, spans in enumerate(ranges)]
    sweeps(refs, ranges, inside, lambda zz: ends[0].at[zz - shift])
    gradients(refs, [(out, *part) for out, part in zip(ends[len(ends) - len(parts) :], parts)])


def gradients(fields, parts):
    K, P0, U1, G, E = fields[0], fields[1], fields[6], fields[-2], fields[-1]
    tiles, nx = K.shape[1], K.shape[2]
    draw, draws = lax.axis_index("draw"), lax.axis_size("draw")
    block, groups = nx // draws, draws // 2
    count = block // SUB

    for out, own, first, z0 in parts:
        parity = draw % 2 if own else 1 - draw % 2
        for s in range(out.shape[0]):
            base = (2 * ((draw // 2 + first + s) % groups) + parity) * block
            start = pl.multiple_of(base, SUB)
            for z in range(out.shape[1]):
                zz = z + z0 + HALO
                v = around_padded(U1, zz, start + SUB, count)
                w = around_padded(E, zz, start + SUB, count)
                for q in range(count):
                    at = pl.ds(pl.multiple_of(start + SUB * q, SUB), SUB)
                    for c in range(tiles):
                        g = G[zz, c, at, :] + P0[zz, c, at, :] * six(v[q][c]) + six(w[q][c])
                        out[s, z, pl.ds(SUB * q, SUB), pl.ds(c * LANES, LANES)] = 0.5 * K[zz, c, at, :] * g


def far_kernel(z0, *args):
    gradients(args[:FIELDS], [(args[FIELDS], True, 1, z0)])


def rest_kernel(*args):
    pieces, fields = args[:3], args[3 : 3 + FIELDS]
    press, keep, sems = args[3 + FIELDS :]
    copies, at = [], 0
    for ref in pieces:
        copies.append(pltpu.make_async_copy(ref, press.at[pl.ds(at, ref.shape[0])], sems.at[len(copies)]))
        at += ref.shape[0]
    for cp in copies:
        cp.start()
    gradients(fields, [(keep, True, 0, 0)])
    for cp in copies:
        cp.wait()


def local(log_perm, noise, source, start_pressure, observe):
    draws, spaces = lax.axis_size("draw"), lax.axis_size("space")
    slab, nx, ny = log_perm.shape
    tiles, depth, half = ny // LANES, slab + 2 * HALO, nx // 2
    up = [(i, i + 1) for i in range(spaces - 1)]
    down = [(j, i) for i, j in up]
    pair = [(i, i ^ 1) for i in range(draws)]
    f32 = jnp.float32
    field = pltpu.VMEM((depth, tiles, nx, LANES), f32)
    padded = pltpu.VMEM((depth, tiles, nx + 2 * SUB, LANES), f32)
    kinds = [field] * 6 + [padded] + [field] * 8 + [padded]
    edge = jax.ShapeDtypeStruct((EDGE, tiles, half, LANES), f32)
    rim = jax.ShapeDtypeStruct((HALO, tiles, nx, LANES), f32)
    whole = jax.ShapeDtypeStruct((slab, nx, ny), f32)
    mid = jax.ShapeDtypeStruct((slab - 2 * SWEEPS, nx, ny), f32)
    groups = draws // 2
    cut = slab // 2
    near = jax.ShapeDtypeStruct((1, slab, nx // draws, ny), f32)
    params = pltpu.CompilerParams(vmem_limit_bytes=8 * 2**20)
    cells = slab * nx * ny

    inputs = (log_perm, noise[0], start_pressure, source, observe)
    K, to_up, to_down, top, bottom = pl.pallas_call(
        first_kernel,
        out_shape=(field, edge, edge, rim, rim),
        in_specs=[OFFCHIP] * 5,
        out_specs=(ONCHIP,) * 5,
        scratch_shapes=[pltpu.VMEM((slab, nx, ny), f32)] * 2 + [pltpu.SemaphoreType.DMA((2 + 6 * tiles,))],
        compiler_params=params,
        cost_estimate=pl.CostEstimate(flops=cells, bytes_accessed=20 * cells, transcendentals=cells),
    )(*[pltpu.with_memory_space_constraint(a, pltpu.HBM) for a in inputs])
    alo = lax.ppermute(to_up, "space", up)
    ahi = lax.ppermute(to_down, "space", down)
    klo = lax.ppermute(top, "space", up)
    khi = lax.ppermute(bottom, "space", down)
    state = pl.pallas_call(
        inner_kernel,
        out_shape=(*kinds[1:], mid),
        in_specs=[ONCHIP] + [ANYWHERE] * 3,
        out_specs=(ONCHIP,) * 16,
        scratch_shapes=[pltpu.SemaphoreType.DMA((3 * tiles,))],
        compiler_params=params,
        cost_estimate=pl.CostEstimate(flops=200 * cells, bytes_accessed=60 * cells, transcendentals=0),
    )(K, start_pressure, source, observe)
    fields, centre = (K, *state[:-1]), state[-1]

    def blocks(count, planes):
        return jax.ShapeDtypeStruct((count, planes, nx // draws, ny), f32)

    def side(low, stages, halos, fields, parts=()):
        ends = (jax.ShapeDtypeStruct((SWEEPS, nx, ny), f32),) if 3 in stages else ()
        ends += tuple(blocks(groups - 1 if first else 1, planes) for _, first, _, planes in parts)
        n = len(halos)
        work = 1 if low else 30 * len(stages) * cells
        out = pl.pallas_call(
            functools.partial(side_kernel, low, stages, [part[:-1] for part in parts]),
            out_shape=(*kinds, *ends),
            in_specs=[ONCHIP] * (n + FIELDS),
            out_specs=(ONCHIP,) * (FIELDS + len(ends)),
            scratch_shapes=[pltpu.SemaphoreType.DMA((1,))],
            input_output_aliases={n + i: i for i in range(FIELDS)},
            compiler_params=params,
            cost_estimate=pl.CostEstimate(flops=work, bytes_accessed=work, transcendentals=0),
        )(*halos, *fields)
        return out[:FIELDS], *out[FIELDS:]

    alo, ahi, last = lax.optimization_barrier((alo, ahi, fields[-1]))
    fields = (*fields[:-1], last)
    lower, upper = [
        (mine, *[lax.ppermute(mine[a:b], "draw", pair) for a, b in ((0, HALO), (HALO, EDGE))]) for mine in (alo, ahi)
    ]

    def fill(low, pieces, fields):
        out = pl.pallas_call(
            functools.partial(fill_kernel, low),
            out_shape=kinds[1:4],
            in_specs=[ONCHIP] * 6,
            out_specs=(ONCHIP,) * 3,
            scratch_shapes=[pltpu.SemaphoreType.DMA((6,))],
            input_output_aliases={3 + i: i for i in range(3)},
            compiler_params=params,
            cost_estimate=pl.CostEstimate(flops=1, bytes_accessed=1, transcendentals=0),
        )(*pieces, *fields[1:4])
        return (fields[0], *out, *fields[4:])

    def onward(keep, got):
        return [
            lax.ppermute(keep[s - 1] + got[s - 1], "draw", [(j, (j + 2 * s) % draws) for j in range(draws)])
            for s in range(1, groups)
        ]

    def swap(send):
        return lax.ppermute(send, "draw", pair)

    def keep_far(z0, planes, fields):
        return pl.pallas_call(
            functools.partial(far_kernel, z0),
            out_shape=blocks(groups - 1, planes),
            in_specs=[ONCHIP] * FIELDS,
            out_specs=ONCHIP,
            compiler_params=params,
            cost_estimate=pl.CostEstimate(flops=10 * cells, bytes_accessed=10 * cells, transcendentals=0),
        )(*fields)

    fields = fill(True, lower, fields)
    (fields,) = side(True, (0, 1, 2), (klo,), fields)
    khi, last = lax.optimization_barrier((khi, fields[-1]))
    fields = (*fields[:-1], last)
    parts = [(False, 1, 0, cut), (False, 0, 0, cut), (True, 1, 0, cut)]
    fields, low, send_far, send_near, keep = side(True, (3,), (), fields, parts)
    got_far, near_low = swap(send_far), swap(send_near)
    fields = fill(False, upper, fields)
    (fields,) = side(False, (0, 1), (khi,), fields)
    got_far, near_low, last = lax.optimization_barrier((got_far, near_low, fields[-1]))
    moved_low = onward(keep, got_far)
    parts = [(False, 1, cut, slab - cut), (False, 0, cut, slab - cut)]
    fields, high, send_far, send_near = side(False, (2, 3), (), (*fields[:-1], last), parts)
    got_far, near_high = swap(send_far), swap(send_near)
    moved_low, last = lax.optimization_barrier((moved_low, fields[-1]))
    fields = (*fields[:-1], last)
    keep = keep_far(cut, slab - cut, fields)
    sums = [keep[s - 1] + got_far[s - 1] for s in range(1, groups)]
    sums, last = lax.optimization_barrier((sums, fields[-1]))
    fields = (*fields[:-1], last)
    moved_high = [
        lax.ppermute(a, "draw", [(j, (j + 2 * s) % draws) for j in range(draws)]) for s, a in enumerate(sums, 1)
    ]
    press, keep = pl.pallas_call(
        rest_kernel,
        out_shape=(whole, near),
        in_specs=[ONCHIP] * (3 + FIELDS),
        out_specs=(OFFCHIP, ONCHIP),
        scratch_shapes=[pltpu.SemaphoreType.DMA((3,))],
        compiler_params=params,
        cost_estimate=pl.CostEstimate(flops=30 * cells, bytes_accessed=30 * cells, transcendentals=0),
    )(low, centre, high, *fields)
    total = keep[0] + jnp.concatenate([near_low[0], near_high[0]], axis=0)
    for a, b in zip(moved_low, moved_high):
        total = total + jnp.concatenate([a, b], axis=0)
    return press[None], total


def solution(mesh):
    return jax.shard_map(
        local,
        mesh=mesh,
        in_specs=(
            P(("epi", "space"), None, None),
            P("draw", ("epi", "space"), None, None),
            P(("epi", "space"), None, None),
            P(("epi", "space"), None, None),
            P(("epi", "space"), None, None),
        ),
        out_specs=(P("draw", ("epi", "space"), None, None), P(("epi", "space"), "draw", None)),
        check_vma=False,
    )
```

```python
import functools

import jax
import jax.numpy as jnp
from jax import lax
from jax.experimental import pallas as pl
from jax.experimental.pallas import tpu as pltpu
from jax.sharding import PartitionSpec as P

SWEEPS = 3
HALO = SWEEPS + 1
EDGE = HALO + 2 * SWEEPS
FIELDS = 16
LANES = 128
SUB = 8
ANYWHERE = pl.BlockSpec(memory_space=pl.ANY)
OFFCHIP = pl.BlockSpec(memory_space=pltpu.HBM)
ONCHIP = pl.BlockSpec(memory_space=pltpu.VMEM)


def lane_shifts(own):
    lane = lax.broadcasted_iota(jnp.int32, (SUB, LANES), 1)
    zero = jnp.zeros((SUB, LANES), jnp.float32)
    fwd = [zero] + [pltpu.roll(v, 1, 1) for v in own]
    bwd = [pltpu.roll(v, LANES - 1, 1) for v in own] + [zero]
    return [
        (jnp.where(lane == 0, fwd[c], fwd[c + 1]), jnp.where(lane == LANES - 1, bwd[c + 1], bwd[c]))
        for c in range(len(own))
    ]


def around(ref, zz, r, rows):
    sub = lax.broadcasted_iota(jnp.int32, (SUB, LANES), 0)
    zero = jnp.zeros((SUB, LANES), jnp.float32)
    own = [ref[zz, c, pl.ds(SUB * r, SUB), :] for c in range(ref.shape[1])]
    sides = lane_shifts(own)
    return own, [sides[c] + cross(ref, zz, c, r, rows, own[c], sub, zero) for c in range(len(own))]


def around_padded(ref, zz, start, count):
    sub = lax.broadcasted_iota(jnp.int32, (SUB, LANES), 0)
    groups = [pl.ds(pl.multiple_of(start + SUB * (q - 1), SUB), SUB) for q in range(count + 2)]
    tiles = ref.shape[1]
    own = [[ref[zz, c, g, :] for c in range(tiles)] for g in groups]
    down = [[pltpu.roll(v, 1, 0) for v in line] for line in own[:-1]]
    up = [[pltpu.roll(v, SUB - 1, 0) for v in line] for line in own[1:]]
    out = []
    for q in range(1, count + 1):
        sides = lane_shifts(own[q])
        line = []
        for c in range(tiles):
            north = jnp.where(sub == 0, down[q - 1][c], down[q][c])
            south = jnp.where(sub == SUB - 1, up[q][c], up[q - 1][c])
            line.append(sides[c] + (north, south, ref[zz - 1, c, groups[q], :], ref[zz + 1, c, groups[q], :]))
        out.append(line)
    return out


def cross(ref, zz, c, r, rows, own, sub, zero):
    if r > 0:
        north = ref[zz, c, pl.ds(SUB * r - 1, SUB), :]
    else:
        north = jnp.where(sub == 0, zero, pltpu.roll(own, 1, 0))
    if r + 1 < rows:
        south = ref[zz, c, pl.ds(SUB * r + 1, SUB), :]
    else:
        south = jnp.where(sub == SUB - 1, zero, pltpu.roll(own, SUB - 1, 0))
    here = pl.ds(SUB * r, SUB)
    return north, south, ref[zz - 1, c, here, :], ref[zz + 1, c, here, :]


def faces(K, WL, WR, zz, c, r, rows):
    sub = lax.broadcasted_iota(jnp.int32, (SUB, LANES), 0)
    zero = jnp.zeros((SUB, LANES), jnp.float32)
    here = pl.ds(SUB * r, SUB)
    k = K[zz, c, here, :]
    rest = [k + v for v in cross(K, zz, c, r, rows, k, sub, zero)]
    return (WL[zz, c, here, :], WR[zz, c, here, :], *rest)


def six(parts):
    a, b, c, d, e, f = parts
    return ((a + b) + (c + d)) + (e + f)


def weighted(weights, parts):
    return six([w * v for w, v in zip(weights, parts)])


def sweeps(refs, ranges, inside, press):
    K, P0, SRC, OBS, P1, P2, U1, U2, U3, HR, SR, NP0, WL, WR, G, E = refs
    tiles, rows = K.shape[1], K.shape[2] // SUB

    def at(r):
        return pl.ds(SUB * r, SUB)

    def coefficients(zz):
        valid = 0.5 * inside(zz)
        for r in range(rows):
            k, kn = around(K, zz, r, rows)
            for c in range(tiles):
                w = [k[c] + v for v in kn[c]]
                HR[zz, c, at(r), :] = valid / (0.5 + 0.5 * six(w))
                WL[zz, c, at(r), :] = w[0]
                WR[zz, c, at(r), :] = w[1]

    def first(zz):
        for r in range(rows):
            _, pn = around(P0, zz, r, rows)
            for c in range(tiles):
                w = faces(K, WL, WR, zz, c, r, rows)
                hr = HR[zz, c, at(r), :]
                rinv = hr + hr
                sr = SRC[zz, c, at(r), :] * rinv
                SR[zz, c, at(r), :] = sr
                NP0[zz, c, at(r), :] = six(pn[c])
                P1[zz, c, at(r), :] = sr + weighted(w, pn[c]) * hr
                U3[zz, c, at(r), :] = OBS[zz, c, at(r), :] * rinv

    def combined(zz):
        valid = inside(zz)
        for r in range(rows):
            k, kn = around(K, zz, r, rows)
            _, pn = around(P0, zz, r, rows)
            for c in range(tiles):
                w = [k[c] + v for v in kn[c]]
                rinv = valid / (0.5 + 0.5 * six(w))
                hr = 0.5 * rinv
                sr = SRC[zz, c, at(r), :] * rinv
                HR[zz, c, at(r), :] = hr
                SR[zz, c, at(r), :] = sr
                WL[zz, c, at(r), :] = w[0]
                WR[zz, c, at(r), :] = w[1]
                NP0[zz, c, at(r), :] = six(pn[c])
                P1[zz, c, at(r), :] = sr + weighted(w, pn[c]) * hr
                U3[zz, c, at(r), :] = OBS[zz, c, at(r), :] * rinv

    def second(zz):
        for r in range(rows):
            _, a = around(P1, zz, r, rows)
            _, v = around(U3, zz, r, rows)
            for c in range(tiles):
                w = faces(K, WL, WR, zz, c, r, rows)
                hr = HR[zz, c, at(r), :]
                p2 = SR[zz, c, at(r), :] + weighted(w, a[c]) * hr
                u2 = weighted(w, v[c]) * hr
                P2[zz, c, at(r), :] = p2
                U2[zz, c, at(r), :] = u2
                G[zz, c, at(r), :] = u2 * six(a[c]) + p2 * six(v[c])

    def third(zz, own):
        for r in range(rows):
            p2, a = around(P2, zz, r, rows)
            u2, v = around(U2, zz, r, rows)
            for c in range(tiles):
                w = faces(K, WL, WR, zz, c, r, rows)
                hr = HR[zz, c, at(r), :]
                p1, u3 = P1[zz, c, at(r), :], U3[zz, c, at(r), :]
                p3 = SR[zz, c, at(r), :] + weighted(w, a[c]) * hr
                u1 = weighted(w, v[c]) * hr
                e = -(u1 * p1 + u2[c] * p2[c] + u3 * p3)
                U1[zz, c, at(r + 1), :] = u1
                E[zz, c, at(r + 1), :] = e
                if own:
                    g = u3 * six(a[c]) + p1 * six(v[c]) + u1 * NP0[zz, c, at(r), :]
                    press(zz)[at(r), pl.ds(c * LANES, LANES)] = p3
                    G[zz, c, at(r), :] = (G[zz, c, at(r), :] + 6.0 * e) + g

    stages = [coefficients, first, second, third]
    if ranges[0] and ranges[0] == ranges[1]:
        stages, ranges = [combined, second, third], ranges[1:]
    for body, spans in zip(stages, ranges):
        for span in spans:
            lo, hi, *own = span
            lax.fori_loop(lo, hi, lambda zz, _, body=body, own=own: body(zz, *own) or 0, 0)


def edges_kernel(p0, src, obs, up, down, sems):
    slab, nx, ny = p0.shape
    half = nx // 2
    rows = pl.ds(pl.multiple_of(half * (lax.axis_index("draw") % 2), half), half)
    copies = []
    for c in range(ny // LANES):
        cols = pl.ds(c * LANES, LANES)
        at = 0
        for ref, width in ((p0, HALO), (src, SWEEPS), (obs, SWEEPS)):
            for start, out in ((slab - width, up), (0, down)):
                pair = (ref.at[pl.ds(start, width), rows, cols], out.at[pl.ds(at, width), c])
                copies.append(pltpu.make_async_copy(*pair, sems.at[len(copies)]))
            at += width
    for cp in copies:
        cp.start()
    for cp in copies:
        cp.wait()


def conduct_kernel(log_perm, noise, K, top, bottom, means, draws, sems):
    slab, nx, ny = log_perm.shape
    copies = [
        pltpu.make_async_copy(a, b, sems.at[i]) for i, (a, b) in enumerate(((log_perm, means), (noise, draws)))
    ]
    for cp in copies:
        cp.start()
    for cp in copies:
        cp.wait()

    def plane(z, _, out=None, first=0):
        for r in range(nx // SUB):
            for c in range(ny // LANES):
                here, cols = pl.ds(SUB * r, SUB), pl.ds(c * LANES, LANES)
                k = jnp.exp(means[z, here, cols] + draws[z, here, cols])
                K[z + HALO, c, here, :] = k
                if out is not None:
                    out[z - first, c, here, :] = k
        return 0

    low, high = functools.partial(plane, out=bottom), functools.partial(plane, out=top, first=slab - HALO)
    lax.fori_loop(0, HALO, low, 0)
    lax.fori_loop(HALO, slab - HALO, plane, 0)
    lax.fori_loop(slab - HALO, slab, high, 0)


def inner_kernel(K, p0, src, obs, P0, SRC, OBS, P1, P2, U1, U2, U3, HR, SR, NP0, WL, WR, G, E, mid, sems):
    slab = p0.shape[0]
    top = HALO + slab
    copies = []
    for c in range(K.shape[1]):
        for ref, out in ((p0, P0), (src, SRC), (obs, OBS)):
            copies.append(
                pltpu.make_async_copy(
                    ref.at[:, :, pl.ds(c * LANES, LANES)], out.at[pl.ds(HALO, slab), c], sems.at[len(copies)]
                )
            )
    for cp in copies:
        cp.start()
    for cp in copies:
        cp.wait()
    rim = jnp.zeros((SUB, LANES), jnp.float32)

    def clear(zz, _):
        for ref in (U1, E):
            for c in range(ref.shape[1]):
                ref[zz, c, pl.ds(0, SUB), :] = rim
                ref[zz, c, pl.ds(ref.shape[2] - SUB, SUB), :] = rim
        return 0

    lax.fori_loop(HALO, top, clear, 0)
    refs = (K, P0, SRC, OBS, P1, P2, U1, U2, U3, HR, SR, NP0, WL, WR, G, E)
    ranges = [[(HALO + n, top - n)] for n in (1, 1, 2)] + [[(HALO + 3, top - 3, True)]]
    sweeps(refs, ranges, lambda zz: jnp.float32(1.0), lambda zz: mid.at[zz - HALO - SWEEPS])


def side_kernel(low, stages, parts, *args):
    halos = args[: len(args) - 2 * FIELDS - (3 in stages) - len(parts) - 1]
    refs = args[len(halos) + FIELDS : len(halos) + 2 * FIELDS]
    ends, sems = args[len(halos) + 2 * FIELDS : -1], args[-1]
    K, P0, SRC, OBS = refs[:4]
    nx, depth = K.shape[2], K.shape[0]
    half, top = nx // 2, depth - HALO
    par = lax.axis_index("draw") % 2

    pairs = []
    if halos:
        k, mine, *theirs = halos
        pairs.append((k, K.at[pl.ds(0 if low else top, HALO)]))
        for half_rows, which in ((None, par), (theirs, 1 - par)):
            rows = pl.ds(pl.multiple_of(half * which, half), half)
            first = 0
            for field, width in ((P0, HALO), (SRC, SWEEPS), (OBS, SWEEPS)):
                planes = pl.ds(HALO - width if low else top, width)
                if half_rows is None:
                    ref = mine.at[pl.ds(first, width)]
                else:
                    ref = theirs[0] if first == 0 else theirs[1].at[pl.ds(first - HALO, width)]
                pairs.append((ref, field.at[planes, :, rows]))
                first += width
    copies = [pltpu.make_async_copy(a, b, sems.at[i]) for i, (a, b) in enumerate(pairs)]
    for cp in copies:
        cp.start()
    for cp in copies:
        cp.wait()

    space, spaces = lax.axis_index("space"), lax.axis_size("space")
    met = jnp.where(space > 0 if low else space + 1 < spaces, 1.0, 0.0).astype(jnp.float32)
    if low:
        near, last, shift = (1, HALO + 1), [(3, HALO, False), (HALO, HALO + 3, True)], HALO
        ranges = [[near], [near], [(2, HALO + 2)], last]
    else:
        near, last, shift = (top - 1, depth - 1), [(top - 3, top, True), (top, depth - 3, False)], top - 3
        ranges = [[near], [near], [(top - 2, depth - 2)], last]

    def inside(zz):
        return jnp.where(zz < HALO if low else zz >= top, met, jnp.float32(1.0))

    ranges = [spans if n in stages else [] for n, spans in enumerate(ranges)]
    sweeps(refs, ranges, inside, lambda zz: ends[0].at[zz - shift])
    gradients(refs, [(out, *part) for out, part in zip(ends[len(ends) - len(parts) :], parts)])


def gradients(fields, parts):
    K, P0, U1, G, E = fields[0], fields[1], fields[6], fields[-2], fields[-1]
    tiles, nx = K.shape[1], K.shape[2]
    draw, draws = lax.axis_index("draw"), lax.axis_size("draw")
    block, groups = nx // draws, draws // 2
    count = block // SUB

    for out, own, first, z0 in parts:
        parity = draw % 2 if own else 1 - draw % 2
        for s in range(out.shape[0]):
            base = (2 * ((draw // 2 + first + s) % groups) + parity) * block
            start = pl.multiple_of(base, SUB)
            for z in range(out.shape[1]):
                zz = z + z0 + HALO
                v = around_padded(U1, zz, start + SUB, count)
                w = around_padded(E, zz, start + SUB, count)
                for q in range(count):
                    at = pl.ds(pl.multiple_of(start + SUB * q, SUB), SUB)
                    for c in range(tiles):
                        g = G[zz, c, at, :] + P0[zz, c, at, :] * six(v[q][c]) + six(w[q][c])
                        out[s, z, pl.ds(SUB * q, SUB), pl.ds(c * LANES, LANES)] = 0.5 * K[zz, c, at, :] * g


def far_kernel(z0, *args):
    gradients(args[:FIELDS], [(args[FIELDS], True, 1, z0)])


def rest_kernel(*args):
    pieces, fields = args[:3], args[3 : 3 + FIELDS]
    press, keep, sems = args[3 + FIELDS :]
    copies, at = [], 0
    for ref in pieces:
        copies.append(pltpu.make_async_copy(ref, press.at[pl.ds(at, ref.shape[0])], sems.at[len(copies)]))
        at += ref.shape[0]
    for cp in copies:
        cp.start()
    gradients(fields, [(keep, True, 0, 0)])
    for cp in copies:
        cp.wait()


def local(log_perm, noise, source, start_pressure, observe):
    draws, spaces = lax.axis_size("draw"), lax.axis_size("space")
    slab, nx, ny = log_perm.shape
    tiles, depth, half = ny // LANES, slab + 2 * HALO, nx // 2
    up = [(i, i + 1) for i in range(spaces - 1)]
    down = [(j, i) for i, j in up]
    pair = [(i, i ^ 1) for i in range(draws)]
    f32 = jnp.float32
    field = pltpu.VMEM((depth, tiles, nx, LANES), f32)
    padded = pltpu.VMEM((depth, tiles, nx + 2 * SUB, LANES), f32)
    kinds = [field] * 6 + [padded] + [field] * 8 + [padded]
    edge = jax.ShapeDtypeStruct((EDGE, tiles, half, LANES), f32)
    rim = jax.ShapeDtypeStruct((HALO, tiles, nx, LANES), f32)
    whole = jax.ShapeDtypeStruct((slab, nx, ny), f32)
    mid = jax.ShapeDtypeStruct((slab - 2 * SWEEPS, nx, ny), f32)
    groups = draws // 2
    cut = slab // 2
    near = jax.ShapeDtypeStruct((1, slab, nx // draws, ny), f32)
    params = pltpu.CompilerParams(vmem_limit_bytes=8 * 2**20)
    cells = slab * nx * ny

    def offchip(*arrays):
        return [pltpu.with_memory_space_constraint(a, pltpu.HBM) for a in arrays]

    to_up, to_down = pl.pallas_call(
        edges_kernel,
        out_shape=(edge, edge),
        in_specs=[OFFCHIP] * 3,
        out_specs=(ONCHIP,) * 2,
        scratch_shapes=[pltpu.SemaphoreType.DMA((6 * tiles,))],
        compiler_params=params,
        cost_estimate=pl.CostEstimate(flops=1, bytes_accessed=1, transcendentals=0),
    )(*offchip(start_pressure, source, observe))
    K, top, bottom = pl.pallas_call(
        conduct_kernel,
        out_shape=(field, rim, rim),
        in_specs=[OFFCHIP] * 2,
        out_specs=(ONCHIP,) * 3,
        scratch_shapes=[pltpu.VMEM((slab, nx, ny), f32)] * 2 + [pltpu.SemaphoreType.DMA((2,))],
        compiler_params=params,
        cost_estimate=pl.CostEstimate(flops=1, bytes_accessed=1, transcendentals=0),
    )(*offchip(log_perm, noise[0]))
    alo = lax.ppermute(to_up, "space", up)
    ahi = lax.ppermute(to_down, "space", down)
    klo = lax.ppermute(top, "space", up)
    khi = lax.ppermute(bottom, "space", down)
    state = pl.pallas_call(
        inner_kernel,
        out_shape=(*kinds[1:], mid),
        in_specs=[ONCHIP] + [ANYWHERE] * 3,
        out_specs=(ONCHIP,) * 16,
        scratch_shapes=[pltpu.SemaphoreType.DMA((3 * tiles,))],
        compiler_params=params,
        cost_estimate=pl.CostEstimate(flops=200 * cells, bytes_accessed=60 * cells, transcendentals=0),
    )(K, start_pressure, source, observe)
    fields, centre = (K, *state[:-1]), state[-1]

    def blocks(count, planes):
        return jax.ShapeDtypeStruct((count, planes, nx // draws, ny), f32)

    def side(low, stages, halos, fields, parts=()):
        ends = (jax.ShapeDtypeStruct((SWEEPS, nx, ny), f32),) if 3 in stages else ()
        ends += tuple(blocks(groups - 1 if first else 1, planes) for _, first, _, planes in parts)
        n = len(halos)
        work = 1 if low else 30 * len(stages) * cells
        out = pl.pallas_call(
            functools.partial(side_kernel, low, stages, [part[:-1] for part in parts]),
            out_shape=(*kinds, *ends),
            in_specs=[ONCHIP] * (n + FIELDS),
            out_specs=(ONCHIP,) * (FIELDS + len(ends)),
            scratch_shapes=[pltpu.SemaphoreType.DMA((8,))],
            input_output_aliases={n + i: i for i in range(FIELDS)},
            compiler_params=params,
            cost_estimate=pl.CostEstimate(flops=work, bytes_accessed=work, transcendentals=0),
        )(*halos, *fields)
        return out[:FIELDS], *out[FIELDS:]

    alo, ahi, last = lax.optimization_barrier((alo, ahi, fields[-1]))
    fields = (*fields[:-1], last)
    lower, upper = [
        (k, mine, *[lax.ppermute(mine[a:b], "draw", pair) for a, b in ((0, HALO), (HALO, EDGE))])
        for k, mine in ((klo, alo), (khi, ahi))
    ]

    def onward(keep, got):
        return [
            lax.ppermute(keep[s - 1] + got[s - 1], "draw", [(j, (j + 2 * s) % draws) for j in range(draws)])
            for s in range(1, groups)
        ]

    def swap(send):
        return lax.ppermute(send, "draw", pair)

    def keep_far(z0, planes, fields):
        return pl.pallas_call(
            functools.partial(far_kernel, z0),
            out_shape=blocks(groups - 1, planes),
            in_specs=[ONCHIP] * FIELDS,
            out_specs=ONCHIP,
            compiler_params=params,
            cost_estimate=pl.CostEstimate(flops=10 * cells, bytes_accessed=10 * cells, transcendentals=0),
        )(*fields)

    (fields,) = side(True, (0, 1, 2), lower, fields)
    parts = [(False, 1, 0, cut), (False, 0, 0, cut), (True, 1, 0, cut)]
    fields, low, send_far, send_near, keep = side(True, (3,), (), fields, parts)
    got_far, near_low = swap(send_far), swap(send_near)
    (fields,) = side(False, (0, 1), upper, fields)
    got_far, near_low, last = lax.optimization_barrier((got_far, near_low, fields[-1]))
    moved_low = onward(keep, got_far)
    parts = [(False, 1, cut, slab - cut), (False, 0, cut, slab - cut)]
    fields, high, send_far, send_near = side(False, (2, 3), (), (*fields[:-1], last), parts)
    got_far, near_high = swap(send_far), swap(send_near)
    moved_low, last = lax.optimization_barrier((moved_low, fields[-1]))
    fields = (*fields[:-1], last)
    keep = keep_far(cut, slab - cut, fields)
    sums = [keep[s - 1] + got_far[s - 1] for s in range(1, groups)]
    sums, last = lax.optimization_barrier((sums, fields[-1]))
    fields = (*fields[:-1], last)
    moved_high = [
        lax.ppermute(a, "draw", [(j, (j + 2 * s) % draws) for j in range(draws)]) for s, a in enumerate(sums, 1)
    ]
    press, keep = pl.pallas_call(
        rest_kernel,
        out_shape=(whole, near),
        in_specs=[ONCHIP] * (3 + FIELDS),
        out_specs=(OFFCHIP, ONCHIP),
        scratch_shapes=[pltpu.SemaphoreType.DMA((3,))],
        compiler_params=params,
        cost_estimate=pl.CostEstimate(flops=30 * cells, bytes_accessed=30 * cells, transcendentals=0),
    )(low, centre, high, *fields)
    total = keep[0] + jnp.concatenate([near_low[0], near_high[0]], axis=0)
    for a, b in zip(moved_low, moved_high):
        total = total + jnp.concatenate([a, b], axis=0)
    return press[None], total


def solution(mesh):
    return jax.shard_map(
        local,
        mesh=mesh,
        in_specs=(
            P(("epi", "space"), None, None),
            P("draw", ("epi", "space"), None, None),
            P(("epi", "space"), None, None),
            P(("epi", "space"), None, None),
            P(("epi", "space"), None, None),
        ),
        out_specs=(P("draw", ("epi", "space"), None, None), P(("epi", "space"), "draw", None)),
        check_vma=False,
    )
```

```python
import functools

import jax
import jax.numpy as jnp
from jax import lax
from jax.experimental import pallas as pl
from jax.experimental.pallas import tpu as pltpu
from jax.sharding import PartitionSpec as P

SWEEPS = 3
HALO = SWEEPS + 1
EDGE = HALO + 2 * SWEEPS
FIELDS = 16
LANES = 128
SUB = 8
ANYWHERE = pl.BlockSpec(memory_space=pl.ANY)
OFFCHIP = pl.BlockSpec(memory_space=pltpu.HBM)
ONCHIP = pl.BlockSpec(memory_space=pltpu.VMEM)


def lane_shifts(own):
    lane = lax.broadcasted_iota(jnp.int32, (SUB, LANES), 1)
    zero = jnp.zeros((SUB, LANES), jnp.float32)
    fwd = [zero] + [pltpu.roll(v, 1, 1) for v in own]
    bwd = [pltpu.roll(v, LANES - 1, 1) for v in own] + [zero]
    return [
        (jnp.where(lane == 0, fwd[c], fwd[c + 1]), jnp.where(lane == LANES - 1, bwd[c + 1], bwd[c]))
        for c in range(len(own))
    ]


def around(ref, zz, r, rows):
    sub = lax.broadcasted_iota(jnp.int32, (SUB, LANES), 0)
    zero = jnp.zeros((SUB, LANES), jnp.float32)
    own = [ref[zz, c, pl.ds(SUB * r, SUB), :] for c in range(ref.shape[1])]
    sides = lane_shifts(own)
    return own, [sides[c] + cross(ref, zz, c, r, rows, own[c], sub, zero) for c in range(len(own))]


def around_padded(ref, zz, start, count):
    sub = lax.broadcasted_iota(jnp.int32, (SUB, LANES), 0)
    groups = [pl.ds(pl.multiple_of(start + SUB * (q - 1), SUB), SUB) for q in range(count + 2)]
    tiles = ref.shape[1]
    own = [[ref[zz, c, g, :] for c in range(tiles)] for g in groups]
    down = [[pltpu.roll(v, 1, 0) for v in line] for line in own[:-1]]
    up = [[pltpu.roll(v, SUB - 1, 0) for v in line] for line in own[1:]]
    out = []
    for q in range(1, count + 1):
        sides = lane_shifts(own[q])
        line = []
        for c in range(tiles):
            north = jnp.where(sub == 0, down[q - 1][c], down[q][c])
            south = jnp.where(sub == SUB - 1, up[q][c], up[q - 1][c])
            line.append(sides[c] + (north, south, ref[zz - 1, c, groups[q], :], ref[zz + 1, c, groups[q], :]))
        out.append(line)
    return out


def cross(ref, zz, c, r, rows, own, sub, zero):
    if r > 0:
        north = ref[zz, c, pl.ds(SUB * r - 1, SUB), :]
    else:
        north = jnp.where(sub == 0, zero, pltpu.roll(own, 1, 0))
    if r + 1 < rows:
        south = ref[zz, c, pl.ds(SUB * r + 1, SUB), :]
    else:
        south = jnp.where(sub == SUB - 1, zero, pltpu.roll(own, SUB - 1, 0))
    here = pl.ds(SUB * r, SUB)
    return north, south, ref[zz - 1, c, here, :], ref[zz + 1, c, here, :]


def faces(K, WL, WR, zz, c, r, rows):
    sub = lax.broadcasted_iota(jnp.int32, (SUB, LANES), 0)
    zero = jnp.zeros((SUB, LANES), jnp.float32)
    here = pl.ds(SUB * r, SUB)
    k = K[zz, c, here, :]
    rest = [k + v for v in cross(K, zz, c, r, rows, k, sub, zero)]
    return (WL[zz, c, here, :], WR[zz, c, here, :], *rest)


def six(parts):
    a, b, c, d, e, f = parts
    return ((a + b) + (c + d)) + (e + f)


def weighted(weights, parts):
    return six([w * v for w, v in zip(weights, parts)])


def sweeps(refs, ranges, inside, press):
    K, P0, SRC, OBS, P1, P2, U1, U2, U3, HR, SR, NP0, WL, WR, G, E = refs
    tiles, rows = K.shape[1], K.shape[2] // SUB

    def at(r):
        return pl.ds(SUB * r, SUB)

    def coefficients(zz):
        valid = 0.5 * inside(zz)
        for r in range(rows):
            k, kn = around(K, zz, r, rows)
            for c in range(tiles):
                w = [k[c] + v for v in kn[c]]
                HR[zz, c, at(r), :] = valid / (0.5 + 0.5 * six(w))
                WL[zz, c, at(r), :] = w[0]
                WR[zz, c, at(r), :] = w[1]

    def first(zz):
        for r in range(rows):
            _, pn = around(P0, zz, r, rows)
            for c in range(tiles):
                w = faces(K, WL, WR, zz, c, r, rows)
                hr = HR[zz, c, at(r), :]
                rinv = hr + hr
                sr = SRC[zz, c, at(r), :] * rinv
                SR[zz, c, at(r), :] = sr
                NP0[zz, c, at(r), :] = six(pn[c])
                P1[zz, c, at(r), :] = sr + weighted(w, pn[c]) * hr
                U3[zz, c, at(r), :] = OBS[zz, c, at(r), :] * rinv

    def combined(zz):
        valid = inside(zz)
        for r in range(rows):
            k, kn = around(K, zz, r, rows)
            _, pn = around(P0, zz, r, rows)
            for c in range(tiles):
                w = [k[c] + v for v in kn[c]]
                rinv = valid / (0.5 + 0.5 * six(w))
                hr = 0.5 * rinv
                sr = SRC[zz, c, at(r), :] * rinv
                HR[zz, c, at(r), :] = hr
                SR[zz, c, at(r), :] = sr
                WL[zz, c, at(r), :] = w[0]
                WR[zz, c, at(r), :] = w[1]
                NP0[zz, c, at(r), :] = six(pn[c])
                P1[zz, c, at(r), :] = sr + weighted(w, pn[c]) * hr
                U3[zz, c, at(r), :] = OBS[zz, c, at(r), :] * rinv

    def second(zz):
        for r in range(rows):
            _, a = around(P1, zz, r, rows)
            _, v = around(U3, zz, r, rows)
            for c in range(tiles):
                w = faces(K, WL, WR, zz, c, r, rows)
                hr = HR[zz, c, at(r), :]
                p2 = SR[zz, c, at(r), :] + weighted(w, a[c]) * hr
                u2 = weighted(w, v[c]) * hr
                P2[zz, c, at(r), :] = p2
                U2[zz, c, at(r), :] = u2
                G[zz, c, at(r), :] = u2 * six(a[c]) + p2 * six(v[c])

    def third(zz, own):
        for r in range(rows):
            p2, a = around(P2, zz, r, rows)
            u2, v = around(U2, zz, r, rows)
            for c in range(tiles):
                w = faces(K, WL, WR, zz, c, r, rows)
                hr = HR[zz, c, at(r), :]
                p1, u3 = P1[zz, c, at(r), :], U3[zz, c, at(r), :]
                p3 = SR[zz, c, at(r), :] + weighted(w, a[c]) * hr
                u1 = weighted(w, v[c]) * hr
                e = -(u1 * p1 + u2[c] * p2[c] + u3 * p3)
                U1[zz, c, at(r + 1), :] = u1
                E[zz, c, at(r + 1), :] = e
                if own:
                    g = u3 * six(a[c]) + p1 * six(v[c]) + u1 * NP0[zz, c, at(r), :]
                    press(zz)[at(r), pl.ds(c * LANES, LANES)] = p3
                    G[zz, c, at(r), :] = (G[zz, c, at(r), :] + 6.0 * e) + g

    stages = [coefficients, first, second, third]
    if ranges[0] and ranges[0] == ranges[1]:
        stages, ranges = [combined, second, third], ranges[1:]
    for body, spans in zip(stages, ranges):
        for span in spans:
            lo, hi, *own = span
            lax.fori_loop(lo, hi, lambda zz, _, body=body, own=own: body(zz, *own) or 0, 0, unroll=hi - lo <= HALO)


def edges_kernel(p0, src, obs, up, down, sems):
    slab, nx, ny = p0.shape
    half = nx // 2
    rows = pl.ds(pl.multiple_of(half * (lax.axis_index("draw") % 2), half), half)
    copies = []
    for c in range(ny // LANES):
        cols = pl.ds(c * LANES, LANES)
        at = 0
        for ref, width in ((p0, HALO), (src, SWEEPS), (obs, SWEEPS)):
            for start, out in ((slab - width, up), (0, down)):
                pair = (ref.at[pl.ds(start, width), rows, cols], out.at[pl.ds(at, width), c])
                copies.append(pltpu.make_async_copy(*pair, sems.at[len(copies)]))
            at += width
    for cp in copies:
        cp.start()
    for cp in copies:
        cp.wait()


def conduct_kernel(log_perm, noise, K, top, bottom, means, draws, sems):
    slab, nx, ny = log_perm.shape
    copies = [
        pltpu.make_async_copy(a, b, sems.at[i]) for i, (a, b) in enumerate(((log_perm, means), (noise, draws)))
    ]
    for cp in copies:
        cp.start()
    for cp in copies:
        cp.wait()

    def plane(z, _, out=None, first=0):
        for r in range(nx // SUB):
            for c in range(ny // LANES):
                here, cols = pl.ds(SUB * r, SUB), pl.ds(c * LANES, LANES)
                k = jnp.exp(means[z, here, cols] + draws[z, here, cols])
                K[z + HALO, c, here, :] = k
                if out is not None:
                    out[z - first, c, here, :] = k
        return 0

    low, high = functools.partial(plane, out=bottom), functools.partial(plane, out=top, first=slab - HALO)
    lax.fori_loop(0, HALO, low, 0)
    lax.fori_loop(HALO, slab - HALO, plane, 0)
    lax.fori_loop(slab - HALO, slab, high, 0)


def inner_kernel(K, p0, src, obs, P0, SRC, OBS, P1, P2, U1, U2, U3, HR, SR, NP0, WL, WR, G, E, mid, sems):
    slab = p0.shape[0]
    top = HALO + slab
    copies = []
    for c in range(K.shape[1]):
        for ref, out in ((p0, P0), (src, SRC), (obs, OBS)):
            copies.append(
                pltpu.make_async_copy(
                    ref.at[:, :, pl.ds(c * LANES, LANES)], out.at[pl.ds(HALO, slab), c], sems.at[len(copies)]
                )
            )
    for cp in copies:
        cp.start()
    for cp in copies:
        cp.wait()
    rim = jnp.zeros((SUB, LANES), jnp.float32)

    def clear(zz, _):
        for ref in (U1, E):
            for c in range(ref.shape[1]):
                ref[zz, c, pl.ds(0, SUB), :] = rim
                ref[zz, c, pl.ds(ref.shape[2] - SUB, SUB), :] = rim
        return 0

    lax.fori_loop(HALO, top, clear, 0)
    refs = (K, P0, SRC, OBS, P1, P2, U1, U2, U3, HR, SR, NP0, WL, WR, G, E)
    ranges = [[(HALO + n, top - n)] for n in (1, 1, 2)] + [[(HALO + 3, top - 3, True)]]
    sweeps(refs, ranges, lambda zz: jnp.float32(1.0), lambda zz: mid.at[zz - HALO - SWEEPS])


def side_kernel(low, stages, parts, *args):
    halos = args[: len(args) - 2 * FIELDS - (3 in stages) - len(parts) - 1]
    refs = args[len(halos) + FIELDS : len(halos) + 2 * FIELDS]
    ends, sems = args[len(halos) + 2 * FIELDS : -1], args[-1]
    K, P0, SRC, OBS = refs[:4]
    nx, depth = K.shape[2], K.shape[0]
    half, top = nx // 2, depth - HALO
    par = lax.axis_index("draw") % 2

    pairs = []
    if halos:
        k, mine, *theirs = halos
        pairs.append((k, K.at[pl.ds(0 if low else top, HALO)]))
        for half_rows, which in ((None, par), (theirs, 1 - par)):
            rows = pl.ds(pl.multiple_of(half * which, half), half)
            first = 0
            for field, width in ((P0, HALO), (SRC, SWEEPS), (OBS, SWEEPS)):
                planes = pl.ds(HALO - width if low else top, width)
                if half_rows is None:
                    ref = mine.at[pl.ds(first, width)]
                else:
                    ref = theirs[0] if first == 0 else theirs[1].at[pl.ds(first - HALO, width)]
                pairs.append((ref, field.at[planes, :, rows]))
                first += width
    copies = [pltpu.make_async_copy(a, b, sems.at[i]) for i, (a, b) in enumerate(pairs)]
    for cp in copies:
        cp.start()
    for cp in copies:
        cp.wait()

    space, spaces = lax.axis_index("space"), lax.axis_size("space")
    met = jnp.where(space > 0 if low else space + 1 < spaces, 1.0, 0.0).astype(jnp.float32)
    if low:
        near, last, shift = (1, HALO + 1), [(3, HALO, False), (HALO, HALO + 3, True)], HALO
        ranges = [[near], [near], [(2, HALO + 2)], last]
    else:
        near, last, shift = (top - 1, depth - 1), [(top - 3, top, True), (top, depth - 3, False)], top - 3
        ranges = [[near], [near], [(top - 2, depth - 2)], last]

    def inside(zz):
        return jnp.where(zz < HALO if low else zz >= top, met, jnp.float32(1.0))

    ranges = [spans if n in stages else [] for n, spans in enumerate(ranges)]
    sweeps(refs, ranges, inside, lambda zz: ends[0].at[zz - shift])
    gradients(refs, [(out, *part) for out, part in zip(ends[len(ends) - len(parts) :], parts)])


def gradients(fields, parts):
    K, P0, U1, G, E = fields[0], fields[1], fields[6], fields[-2], fields[-1]
    tiles, nx = K.shape[1], K.shape[2]
    draw, draws = lax.axis_index("draw"), lax.axis_size("draw")
    block, groups = nx // draws, draws // 2
    count = block // SUB

    for out, own, first, z0 in parts:
        parity = draw % 2 if own else 1 - draw % 2
        for s in range(out.shape[0]):
            base = (2 * ((draw // 2 + first + s) % groups) + parity) * block
            start = pl.multiple_of(base, SUB)
            for z in range(out.shape[1]):
                zz = z + z0 + HALO
                v = around_padded(U1, zz, start + SUB, count)
                w = around_padded(E, zz, start + SUB, count)
                for q in range(count):
                    at = pl.ds(pl.multiple_of(start + SUB * q, SUB), SUB)
                    for c in range(tiles):
                        g = G[zz, c, at, :] + P0[zz, c, at, :] * six(v[q][c]) + six(w[q][c])
                        out[s, z, pl.ds(SUB * q, SUB), pl.ds(c * LANES, LANES)] = 0.5 * K[zz, c, at, :] * g


def far_kernel(z0, *args):
    gradients(args[:FIELDS], [(args[FIELDS], True, 1, z0)])


def rest_kernel(*args):
    pieces, fields = args[:3], args[3 : 3 + FIELDS]
    press, keep, sems = args[3 + FIELDS :]
    copies, at = [], 0
    for ref in pieces:
        copies.append(pltpu.make_async_copy(ref, press.at[pl.ds(at, ref.shape[0])], sems.at[len(copies)]))
        at += ref.shape[0]
    for cp in copies:
        cp.start()
    gradients(fields, [(keep, True, 0, 0)])
    for cp in copies:
        cp.wait()


def local(log_perm, noise, source, start_pressure, observe):
    draws, spaces = lax.axis_size("draw"), lax.axis_size("space")
    slab, nx, ny = log_perm.shape
    tiles, depth, half = ny // LANES, slab + 2 * HALO, nx // 2
    up = [(i, i + 1) for i in range(spaces - 1)]
    down = [(j, i) for i, j in up]
    pair = [(i, i ^ 1) for i in range(draws)]
    f32 = jnp.float32
    field = pltpu.VMEM((depth, tiles, nx, LANES), f32)
    padded = pltpu.VMEM((depth, tiles, nx + 2 * SUB, LANES), f32)
    kinds = [field] * 6 + [padded] + [field] * 8 + [padded]
    edge = jax.ShapeDtypeStruct((EDGE, tiles, half, LANES), f32)
    rim = jax.ShapeDtypeStruct((HALO, tiles, nx, LANES), f32)
    whole = jax.ShapeDtypeStruct((slab, nx, ny), f32)
    mid = jax.ShapeDtypeStruct((slab - 2 * SWEEPS, nx, ny), f32)
    groups = draws // 2
    cut = slab // 2
    near = jax.ShapeDtypeStruct((1, slab, nx // draws, ny), f32)
    params = pltpu.CompilerParams(vmem_limit_bytes=8 * 2**20)
    cells = slab * nx * ny

    def offchip(*arrays):
        return [pltpu.with_memory_space_constraint(a, pltpu.HBM) for a in arrays]

    to_up, to_down = pl.pallas_call(
        edges_kernel,
        out_shape=(edge, edge),
        in_specs=[OFFCHIP] * 3,
        out_specs=(ONCHIP,) * 2,
        scratch_shapes=[pltpu.SemaphoreType.DMA((6 * tiles,))],
        compiler_params=params,
        cost_estimate=pl.CostEstimate(flops=1, bytes_accessed=1, transcendentals=0),
    )(*offchip(start_pressure, source, observe))
    K, top, bottom = pl.pallas_call(
        conduct_kernel,
        out_shape=(field, rim, rim),
        in_specs=[OFFCHIP] * 2,
        out_specs=(ONCHIP,) * 3,
        scratch_shapes=[pltpu.VMEM((slab, nx, ny), f32)] * 2 + [pltpu.SemaphoreType.DMA((2,))],
        compiler_params=params,
        cost_estimate=pl.CostEstimate(flops=1, bytes_accessed=1, transcendentals=0),
    )(*offchip(log_perm, noise[0]))
    alo = lax.ppermute(to_up, "space", up)
    ahi = lax.ppermute(to_down, "space", down)
    klo = lax.ppermute(top, "space", up)
    khi = lax.ppermute(bottom, "space", down)
    state = pl.pallas_call(
        inner_kernel,
        out_shape=(*kinds[1:], mid),
        in_specs=[ONCHIP] + [ANYWHERE] * 3,
        out_specs=(ONCHIP,) * 16,
        scratch_shapes=[pltpu.SemaphoreType.DMA((3 * tiles,))],
        compiler_params=params,
        cost_estimate=pl.CostEstimate(flops=200 * cells, bytes_accessed=60 * cells, transcendentals=0),
    )(K, start_pressure, source, observe)
    fields, centre = (K, *state[:-1]), state[-1]

    def blocks(count, planes):
        return jax.ShapeDtypeStruct((count, planes, nx // draws, ny), f32)

    def side(low, stages, halos, fields, parts=()):
        ends = (jax.ShapeDtypeStruct((SWEEPS, nx, ny), f32),) if 3 in stages else ()
        ends += tuple(blocks(groups - 1 if first else 1, planes) for _, first, _, planes in parts)
        n = len(halos)
        work = 1 if low else 30 * len(stages) * cells
        out = pl.pallas_call(
            functools.partial(side_kernel, low, stages, [part[:-1] for part in parts]),
            out_shape=(*kinds, *ends),
            in_specs=[ONCHIP] * (n + FIELDS),
            out_specs=(ONCHIP,) * (FIELDS + len(ends)),
            scratch_shapes=[pltpu.SemaphoreType.DMA((8,))],
            input_output_aliases={n + i: i for i in range(FIELDS)},
            compiler_params=params,
            cost_estimate=pl.CostEstimate(flops=work, bytes_accessed=work, transcendentals=0),
        )(*halos, *fields)
        return out[:FIELDS], *out[FIELDS:]

    alo, ahi, last = lax.optimization_barrier((alo, ahi, fields[-1]))
    fields = (*fields[:-1], last)
    lower, upper = [
        (k, mine, *[lax.ppermute(mine[a:b], "draw", pair) for a, b in ((0, HALO), (HALO, EDGE))])
        for k, mine in ((klo, alo), (khi, ahi))
    ]

    def onward(keep, got):
        return [
            lax.ppermute(keep[s - 1] + got[s - 1], "draw", [(j, (j + 2 * s) % draws) for j in range(draws)])
            for s in range(1, groups)
        ]

    def swap(send):
        return lax.ppermute(send, "draw", pair)

    def keep_far(z0, planes, fields):
        return pl.pallas_call(
            functools.partial(far_kernel, z0),
            out_shape=blocks(groups - 1, planes),
            in_specs=[ONCHIP] * FIELDS,
            out_specs=ONCHIP,
            compiler_params=params,
            cost_estimate=pl.CostEstimate(flops=10 * cells, bytes_accessed=10 * cells, transcendentals=0),
        )(*fields)

    (fields,) = side(True, (0, 1, 2), lower, fields)
    parts = [(False, 1, 0, cut), (False, 0, 0, cut), (True, 1, 0, cut)]
    fields, low, send_far, send_near, keep = side(True, (3,), (), fields, parts)
    got_far, near_low = swap(send_far), swap(send_near)
    (fields,) = side(False, (0, 1), upper, fields)
    got_far, near_low, last = lax.optimization_barrier((got_far, near_low, fields[-1]))
    moved_low = onward(keep, got_far)
    parts = [(False, 1, cut, slab - cut), (False, 0, cut, slab - cut)]
    fields, high, send_far, send_near = side(False, (2, 3), (), (*fields[:-1], last), parts)
    got_far, near_high = swap(send_far), swap(send_near)
    moved_low, last = lax.optimization_barrier((moved_low, fields[-1]))
    fields = (*fields[:-1], last)
    keep = keep_far(cut, slab - cut, fields)
    sums = [keep[s - 1] + got_far[s - 1] for s in range(1, groups)]
    sums, last = lax.optimization_barrier((sums, fields[-1]))
    fields = (*fields[:-1], last)
    moved_high = [
        lax.ppermute(a, "draw", [(j, (j + 2 * s) % draws) for j in range(draws)]) for s, a in enumerate(sums, 1)
    ]
    press, keep = pl.pallas_call(
        rest_kernel,
        out_shape=(whole, near),
        in_specs=[ONCHIP] * (3 + FIELDS),
        out_specs=(OFFCHIP, ONCHIP),
        scratch_shapes=[pltpu.SemaphoreType.DMA((3,))],
        compiler_params=params,
        cost_estimate=pl.CostEstimate(flops=30 * cells, bytes_accessed=30 * cells, transcendentals=0),
    )(low, centre, high, *fields)
    total = keep[0] + jnp.concatenate([near_low[0], near_high[0]], axis=0)
    for a, b in zip(moved_low, moved_high):
        total = total + jnp.concatenate([a, b], axis=0)
    return press[None], total


def solution(mesh):
    return jax.shard_map(
        local,
        mesh=mesh,
        in_specs=(
            P(("epi", "space"), None, None),
            P("draw", ("epi", "space"), None, None),
            P(("epi", "space"), None, None),
            P(("epi", "space"), None, None),
            P(("epi", "space"), None, None),
        ),
        out_specs=(P("draw", ("epi", "space"), None, None), P(("epi", "space"), "draw", None)),
        check_vma=False,
    )
```
